32 devices in a mesh: req: 8 (over z, x), tp: 4 (over y, core).
Axes of the slice: x: 2, y: 2, z: 4, core: 2. Of those that a mesh axis runs over, the one named last changes fastest.
Arguments:
- tokens: bfloat16 [4096, 3584], P('req'), may hold values from -400 to 400, as said below
- norm_gain: float32 [3584], P(('req', 'tp')), may hold values from 0.5 to 1.5
- qkv_weight: float32 [3584, 4608], P(('req', 'tp')), may hold values from -0.09375 to 0.09375
- qkv_bias: float32 [4608], P(('req', 'tp')), may hold values from -48 to 48
- lengths: int32 [8, 4], P('req'), may hold values from 1 to 256, 512 in all within a row
Outputs:
- context: bfloat16 [4096, 3584], P('req', 'tp')
The draws below stay inside these ranges and needn't reach their ends.
Inputs may be any that keep to these rules, and one draw needn't show every extreme that they name: `tokens`: hidden states of order one to some hundreds. Each replica's tenant lengths sum to 512, the largest is exactly 256.
All inputs are finite; a program needn't handle non-finite values.
Results may differ from the reference program's by a relative error of at most 0.009.
The reference program's roundings to bfloat16 on the way count: a program that leaves them out, or rounds other values in their place, can miss the bound.
Values may be sent and summed in bfloat16 or wider, within the bound.
A program may use at most 128 MiB of HBM per device.

```python
import math
import jax
import jax.numpy as jnp
import numpy as np
from jax import lax

D = 3584
HEADS = 28
HEAD_DIM = 128
TOK_DEV = 512
TENANTS = 4
SINKS = 4
GROUP = 7
QKV = 4608
MOST = 256
WINDOW = 160
TOKENS = 4096
N_REQ = 8


def draw_tokens(key, part):
    first, second, third = jax.random.split(key, 3)
    base = jnp.clip(jax.random.normal(first, (TOKENS, D), jnp.float32), -4.0, 4.0)
    rows = jnp.exp(jax.random.uniform(second, (TOKENS, 1), jnp.float32, 0.0, math.log(10.0)))
    cols = jnp.exp(jax.random.uniform(third, (1, D), jnp.float32, 0.0, math.log(10.0)))
    return (base * rows * cols).astype(jnp.bfloat16)


def draw_qkv_bias(key, part):
    first = jax.random.fold_in(key, 0)
    return jnp.clip(0.5 * jax.random.normal(first, (QKV,), jnp.float32), -2.0, 2.0)


def block_levels(stream_key, dims, pieces, low, top_value):
    loudness, own = 1.0, jax.random.fold_in(stream_key, 6)
    for axis_at, shards_of in pieces:
        steps = jnp.exp(jax.random.uniform(jax.random.fold_in(own, axis_at), (shards_of,), jnp.float32, low / len(pieces), top_value / len(pieces)))
        loudness = loudness * jnp.repeat(steps, dims[axis_at] // shards_of).reshape([-1 if axis == axis_at else 1 for axis in range(len(dims))])
    return loudness


def length_profile(number_of, total, limit, skew):
    weights = [(1 << 20) // math.isqrt(grade ** skew) + 1 for grade in range(2, number_of + 1)]
    rest, counts = total - limit - (number_of - 1), [1] * (number_of - 1)
    while rest > 0:
        candidates = [i for i in range(number_of - 1) if counts[i] < limit]
        mass, left = sum([weights[i] for i in candidates]), rest
        for i in candidates:
            more = min(limit - counts[i], max(1, left * weights[i] // mass), rest)
            counts[i] = counts[i] + more
            rest = rest - more
    return np.array([limit] + counts)


def ragged(stream_key, count, total, limit, skew):
    if count == 2:
        one = jax.random.randint(stream_key, (), max(1, total - limit), min(limit, total - 1) + 1)
        return jnp.stack([one, total - one])
    sizes = jnp.asarray(length_profile(count, total, limit, skew), jnp.int32)
    twos = (count - 1) // 2
    giver, taker = sizes[1:1 + 2 * twos:2], sizes[2:2 + 2 * twos:2]
    slack = jnp.minimum(giver - 1, limit - taker)
    passed = jax.random.randint(jax.random.fold_in(stream_key, 1), (twos,), 0, 1 << 20) % (slack + 1)
    sizes = sizes.at[1:1 + 2 * twos:2].set(giver - passed).at[2:2 + 2 * twos:2].set(taker + passed)
    return sizes[jax.random.permutation(jax.random.fold_in(stream_key, 2), count)]


def scatter_about(key, extent, spread, limit, shards=(), kind=jnp.bfloat16):
    drawn = spread * jax.random.normal(key, extent, jnp.float32)
    if shards:
        drawn = drawn * block_levels(key, extent, shards, -0.22, 0.18)
    return jnp.clip(drawn, -limit, limit).astype(kind)


def setup_inputs(seed: int = 0) -> dict:
    key_of = jax.random.split(jax.random.key(seed), 6)
    return {
        "tokens": draw_tokens(jax.random.fold_in(key_of[5], 71), 0),
        "norm_gain": jnp.clip(1.0 + 0.1 * jax.random.normal(key_of[1], (D,), jnp.float32), 0.5, 1.5),
        "qkv_weight": scatter_about(key_of[2], (D, QKV), D ** -0.5, 0.09375, ((0, 32),), jnp.float32),
        "qkv_bias": draw_qkv_bias(jax.random.fold_in(key_of[5], 71), 0),
        "lengths": jax.vmap(lambda own: ragged(own, TENANTS, TOK_DEV, MOST, 2))(jax.random.split(key_of[4], N_REQ)).reshape((N_REQ, TENANTS)).astype(jnp.int32),
    }


def normalize(values, gain):
    wide = values.astype(jnp.float32)
    meansq = lax.optimization_barrier(jnp.mean(wide * wide, axis=-1, keepdims=True))
    return (wide * lax.rsqrt(meansq + 1e-06) * gain.astype(jnp.float32)).astype(jnp.bfloat16)

def positions(lens, count):
    index = jnp.arange(count, dtype=jnp.int32)
    ends = jnp.cumsum(lens).astype(jnp.int32)
    after = index[:, None] >= ends[None, :]
    tenant = lax.optimization_barrier(jnp.sum(after.astype(jnp.int32), axis=1)).astype(jnp.int32)
    start = lax.optimization_barrier(jnp.sum(jnp.where(after, lens[None, :], 0), axis=1)).astype(jnp.int32)
    return (tenant, index - start)

def rotate(values, pos):
    half = HEAD_DIM // 2
    freqs = jnp.exp(-(jnp.arange(half, dtype=jnp.float32) * 2.0 / HEAD_DIM) * math.log(1000000.0))
    angle = pos.astype(jnp.float32)[:, None] * freqs[None, :]
    cosine = jnp.concatenate([jnp.cos(angle), jnp.cos(angle)], axis=-1)
    sine = jnp.concatenate([jnp.sin(angle), jnp.sin(angle)], axis=-1)
    shape = (values.shape[0],) + (1,) * (values.ndim - 2) + (HEAD_DIM,)
    cosine = cosine.reshape(shape)
    sine = sine.reshape(shape)
    turned = jnp.concatenate([-values[..., half:], values[..., :half]], axis=-1)
    return values * cosine + turned * sine

def attend(joined, tenant, pos):
    count = joined.shape[0]
    blocks = joined.reshape(count, -1, GROUP + 2, HEAD_DIM)
    query = rotate(blocks[:, :, :GROUP], pos).astype(jnp.bfloat16)
    key_part = rotate(blocks[:, :, GROUP], pos).astype(jnp.bfloat16)
    value_part = blocks[:, :, GROUP + 1].astype(jnp.bfloat16)
    scores = jnp.einsum('qghd,kgd->ghqk', query.astype(jnp.float32), key_part.astype(jnp.float32)) / math.sqrt(HEAD_DIM)
    same = tenant[:, None] == tenant[None, :]
    causal = pos[None, :] <= pos[:, None]
    near = jnp.logical_or(pos[:, None] - pos[None, :] < WINDOW, pos[None, :] < SINKS)
    allowed = jnp.logical_and(jnp.logical_and(same, causal), near)
    scores = jnp.where(allowed[None, None], scores, -1e+30)
    peak = lax.optimization_barrier(jnp.max(scores, axis=-1, keepdims=True))
    expo = jnp.where(allowed[None, None], jnp.exp(scores - peak), 0.0)
    weights = (expo / lax.optimization_barrier(jnp.sum(expo, axis=-1, keepdims=True))).astype(jnp.bfloat16)
    mixed = jnp.einsum('ghqk,kgd->qghd', weights.astype(jnp.float32), value_part.astype(jnp.float32))
    return mixed.reshape(count, -1).astype(jnp.bfloat16)

def reference(tokens, norm_gain, qkv_weight, qkv_bias, lengths):
    gain_b = norm_gain.astype(jnp.bfloat16)
    weight_b = qkv_weight.astype(jnp.bfloat16)
    bias_f = qkv_bias.astype(jnp.bfloat16).astype(jnp.float32)
    stacked = tokens.reshape(N_REQ, TOK_DEV, D)

    def replica(items):
        rows, lens = items
        normed = normalize(rows, gain_b)
        joined = jnp.dot(normed, weight_b, preferred_element_type=jnp.float32) + bias_f[None, :]
        tenant, pos = positions(lens, TOK_DEV)
        return attend(joined, tenant, pos)
    out = lax.map(replica, (stacked, lengths))
    return out.reshape(TOKENS, HEADS * HEAD_DIM)
```

```python
import functools
import math

import jax
import jax.numpy as jnp
from jax import lax
from jax.experimental import pallas as pl
from jax.experimental.pallas import tpu as pltpu
from jax.sharding import PartitionSpec as P

HEAD_DIM = 128
SINKS = 4
GROUP = 7
WINDOW = 160
MOST = 256
MESH = pl.DeviceIdType.MESH


def normalize(values, gain):
    wide = values.astype(jnp.float32)
    meansq = jnp.mean(wide * wide, axis=-1, keepdims=True)
    return (wide * lax.rsqrt(meansq + 1e-06) * gain.astype(jnp.float32)).astype(jnp.bfloat16)


def starts(lens, count):
    index = jnp.arange(count, dtype=jnp.int32)
    start, end = jnp.zeros((count,), jnp.int32), jnp.int32(0)
    for t in range(lens.shape[0]):
        end = end + lens[t]
        start = jnp.where(index >= end, end, start)
    return start


def rotated(v, cosine, sine):
    return (v * cosine + pltpu.roll(v, HEAD_DIM // 2, 1) * sine).astype(jnp.bfloat16)


def start_of(query_at, lens_ref):
    start, end = jnp.zeros_like(query_at), jnp.int32(0)
    for t in range(lens_ref.shape[1]):
        end = end + lens_ref[0, t]
        start = jnp.where(query_at >= end, end, start)
    return start


def attend_kernel(lens_ref, qkv_ref, out_ref):
    count = qkv_ref.shape[0]
    block = 128
    back = -(-(MOST - 1) // block)
    for at in range(count // block):
        first = max(0, at - back)
        wide = (at + 1 - first) * block
        rows = slice(at * block, (at + 1) * block)
        seen = slice(first * block, (at + 1) * block)
        query_at = at * block + lax.broadcasted_iota(jnp.int32, (block, 1), 0)
        key_at = first * block + lax.broadcasted_iota(jnp.int32, (block, wide), 1)
        start = start_of(query_at, lens_ref)
        low = jnp.maximum(query_at - (WINDOW - 1), start)
        allowed = jnp.logical_and(
            key_at <= query_at,
            jnp.logical_or(
                key_at >= low, jnp.logical_and(key_at >= start, key_at < start + SINKS)
            ),
        )
        query = jnp.concatenate(
            [qkv_ref[rows, h * HEAD_DIM : (h + 1) * HEAD_DIM] for h in range(GROUP)], axis=0
        )
        scores = lax.dot_general(
            query, qkv_ref[seen, GROUP * HEAD_DIM : (GROUP + 1) * HEAD_DIM],
            (((1,), (1,)), ((), ())), preferred_element_type=jnp.float32,
        ) * (1.0 / math.sqrt(HEAD_DIM))
        scores = jnp.where(allowed[None], scores.reshape(GROUP, block, wide), -1e30)
        peak = jnp.max(scores, axis=-1, keepdims=True)
        expo = jnp.exp(scores - peak)
        weights = (expo * (1.0 / jnp.sum(expo, axis=-1, keepdims=True))).astype(jnp.bfloat16)
        mixed = jnp.dot(
            weights.reshape(GROUP * block, wide), qkv_ref[seen, (GROUP + 1) * HEAD_DIM :],
            preferred_element_type=jnp.float32,
        ).astype(jnp.bfloat16)
        for h in range(GROUP):
            out_ref[rows, h * HEAD_DIM : (h + 1) * HEAD_DIM] = mixed[h * block : (h + 1) * block]


def attend_turned(qkv, lens):
    count = qkv.shape[0]
    vmem = pl.BlockSpec(memory_space=pltpu.VMEM)
    return pl.pallas_call(
        attend_kernel,
        out_shape=jax.ShapeDtypeStruct((count, GROUP * HEAD_DIM), jnp.bfloat16),
        in_specs=[pl.BlockSpec(memory_space=pltpu.SMEM), vmem],
        out_specs=vmem,
        compiler_params=pltpu.CompilerParams(vmem_limit_bytes=64 << 20),
        name="attention",
    )(lens, qkv)


CHUNKS = ((896, 1152), (0, 384), (384, 640), (640, 896))
BLOCK = 128
PARTS = 4


def serve_kernel(
    lens_hbm, gain_hbm, bias_hbm, w_hbm, tok_hbm, out_hbm,
    lens_ref, gain_ref, bias_ref, small_sem, wide_w, wb0, wb1, wb2, wb3, full0, full1, full2, full3,
    tok, normed, acc0, acc1, acc2, acc3, qkv, cosine, sine, mask, gains, ctx, side, line, sides,
    tok_sem, w_sem, line_send, line_recv, side_send, side_recv, first_send, first_recv,
    near_send, near_recv, far_send, far_recv, mate_send, mate_recv,
    tx_send, tx_recv, ty_send, ty_recv, out_send, out_recv, out_sem,
):
    f32, bf16 = jnp.float32, jnp.bfloat16
    wbs, fulls, accs = (wb0, wb1, wb2, wb3), (full0, full1, full2, full3), (acc0, acc1, acc2, acc3)
    number = len(CHUNKS)
    req, tp = lax.axis_index("req"), lax.axis_index("tp")
    z, x, y, c = req // 2, req % 2, tp // 2, tp % 2
    group, place, me = 2 * y + x, 2 * x + y, 4 * x + 2 * y + c
    count, depth = tok.shape
    shard = wide_w.shape[1]
    width = wide_w.shape[2]
    swapped = x != c

    def device(at_z, at_x, at_y, at_c):
        return (2 * at_z + at_x, 2 * at_y + at_c)

    def flipped(m):
        fx, fy, fc = m // 4, m // 2 % 2, m % 2
        return (
            1 - x if fx else x,
            1 - y if fy else y,
            1 - c if fc else c,
        )

    def remote(source, to, send_sem, recv_sem, where):
        return pltpu.make_async_remote_copy(
            src_ref=source, dst_ref=to, send_sem=send_sem, recv_sem=recv_sem,
            device_id=where, device_id_type=MESH,
        )

    partner = device(z, 1 - x, y, 1 - c)
    mate = device(z, x, y, 1 - c)

    barrier = pltpu.get_barrier_semaphore()
    for m in range(1, 8):
        pl.semaphore_signal(barrier, inc=1, device_id=device(z, *flipped(m)), device_id_type=MESH)
    for dz in range(1, 4):
        pl.semaphore_signal(
            barrier, inc=1, device_id=device((z + dz) % 4, x, y, c), device_id_type=MESH
        )

    smalls = [
        pltpu.make_async_copy(source, to, small_sem.at[k])
        for k, (source, to) in enumerate(
            ((gain_hbm, gain_ref), (bias_hbm, bias_ref), (lens_hbm, lens_ref))
        )
    ]
    for copy in smalls:
        copy.start()
    flips = ((0, 0), (1, 0), (0, 1), (1, 1))
    loads = []
    for k, (fx, fy) in enumerate(flips):
        g = 2 * (1 - y if fy else y) + (1 - x if fx else x)
        copy = pltpu.make_async_copy(
            w_hbm.at[:, pl.ds(pl.multiple_of(g * width, 128), width)], wide_w.at[k], w_sem.at[k]
        )
        copy.start()
        loads.append(copy)
    tok_copy = pltpu.make_async_copy(tok_hbm, tok, tok_sem)

    @pl.when(jnp.logical_not(swapped))
    def _():
        tok_copy.start()

    def rounded(v):
        return v.astype(bf16).astype(f32)

    for copy in smalls:
        copy.wait()
    side[...] = jnp.zeros_like(side)
    side[0:1, 0:shard] = rounded(gain_ref[...])
    side[1:2, :] = rounded(bias_ref[:, 0:128])
    side[2:3, 0 : width // 8 - 128] = rounded(bias_ref[:, 128:])
    side[3:4, 0 : lens_ref.shape[1]] = lens_ref[...].astype(f32)

    pl.semaphore_wait(barrier, 10)
    lines = []
    for dz in range(1, 4):
        copy = remote(
            side, line.at[z], line_send.at[dz - 1], line_recv.at[dz - 1],
            device((z + dz) % 4, x, y, c),
        )
        copy.start()
        lines.append(copy)
    line[z] = side[...]

    def half(k, p):
        return fulls[k].at[p, :, c]

    def near(way, k, j):
        ref = fulls[k].at[z, j, c]
        return remote(
            ref, ref, near_send.at[way, k, j], near_recv.at[way, k, j],
            device(z - 1 + 2 * way, x, y, c),
        )

    def far(way, k, d):
        ref = half(k, z + (d - 1) * (1 - 2 * way))
        return remote(
            ref, ref, far_send.at[way, k, d - 2], far_recv.at[way, k, d - 2],
            device(z - 1 + 2 * way, x, y, c),
        )

    def sends(way):
        return z >= 1 if way == 0 else z <= 2

    def has(way, d):
        return z + d <= 3 if way == 0 else z - d >= 0

    def start_near(k, j):
        for way in range(2):
            copy = near(way, k, j)

            @pl.when(sends(way))
            def _():
                copy.start()

    firsts = {}
    for i, (fx, fy) in enumerate(flips):
        loads[i].wait()
        for k, (lo, hi) in enumerate(CHUNKS):
            if i == 0:
                fulls[k][z, place, c] = wide_w[i, :, lo:hi].astype(bf16)
            else:
                wbs[k][i - 1] = wide_w[i, :, lo:hi].astype(bf16)
                copy = remote(
                    wbs[k].at[i - 1], fulls[k].at[z, place, c],
                    first_send.at[k, i - 1], first_recv.at[k, i - 1],
                    device(z, 1 - x if fx else x, 1 - y if fy else y, c),
                )
                copy.start()
                firsts[k, i - 1] = copy
        if i == 0:
            start_near(0, place)
    for k in range(1, number):
        start_near(k, place)

    def send_mate(k, p):
        ref = half(k, p)
        return remote(ref, ref, mate_send.at[k, p], mate_recv.at[k, p], mate)

    for copy in lines:
        copy.wait_recv()
    shares = []
    for m in range(1, 8):
        copy = remote(
            line, sides.at[me], side_send.at[m - 1], side_recv.at[m - 1], device(z, *flipped(m))
        )
        copy.start()
        shares.append(copy)
    sides[me] = line[...]

    for k in range(number):
        for i, (fx, fy) in enumerate(flips[1:]):
            firsts[k, i].wait_recv()
            start_near(k, 2 * (1 - x if fx else x) + (1 - y if fy else y))
        send_mate(k, z).start()

    rows = count // 2 // PARTS

    def part_rows(at_y, n):
        return pl.ds(pl.multiple_of(at_y * (count // 2) + n * rows, rows), rows)

    def tok_x(n):
        at = part_rows(y, n)
        return remote(tok_hbm.at[at], tok.at[at], tx_send.at[n], tx_recv.at[n], partner)

    def tok_y(n):
        at = tok.at[part_rows(y, n)]
        return remote(at, at, ty_send.at[n], ty_recv.at[n], device(z, x, 1 - y, c))

    @pl.when(swapped)
    def _():
        for n in range(PARTS):
            tok_x(n).start()

    for copy in shares:
        copy.wait_recv()

    def spread(piece, step, n, size):
        wide = jnp.concatenate(piece + [jnp.zeros((8, size - 128 * len(piece)), f32)], axis=1)
        return pltpu.roll(wide, step * n, 1) if n else wide

    for p in range(4):
        total = jnp.zeros((8, 8 * 128), f32)
        for n in range(8):
            total = total + spread([sides[n, p]], shard, n, 8 * 128)
        gains[p] = total[:, 0 : 8 * shard]

    own_lens = sides[4 * c + 2 * y + c, z][3:4, :]
    ends, end = [], jnp.zeros((1, 1), f32)
    for t in range(lens_ref.shape[1]):
        end = end + own_lens[:, t : t + 1]
        ends.append(end)

    def start_at(query):
        start = jnp.zeros_like(query)
        for e in ends:
            start = jnp.where(query >= e, e, start)
        return start

    def tables():
        query = lax.broadcasted_iota(jnp.int32, (count, 1), 0).astype(f32)
        pos = query - start_at(query)
        lane = lax.broadcasted_iota(jnp.int32, (1, HEAD_DIM), 1)
        mid = HEAD_DIM // 2
        freqs = jnp.exp(-((lane % mid).astype(f32) * 2.0 / HEAD_DIM) * math.log(1000000.0))
        angle = pos * freqs
        cosine[...] = jnp.cos(angle)
        sine[...] = jnp.where(lane < mid, -1.0, 1.0) * jnp.sin(angle)

    back = -(-(MOST - 1) // BLOCK)

    def reach(at):
        first = max(0, at - back)
        return first, (at + 1 - first) * BLOCK

    def masks():
        for at in range(count // BLOCK):
            first, wide = reach(at)
            query = (at * BLOCK + lax.broadcasted_iota(jnp.int32, (BLOCK, 1), 0)).astype(f32)
            key = (first * BLOCK + lax.broadcasted_iota(jnp.int32, (BLOCK, wide), 1)).astype(f32)
            start = start_at(query)
            low = jnp.maximum(query - (WINDOW - 1), start)
            allowed = jnp.logical_and(
                key <= query,
                jnp.logical_or(key >= low, jnp.logical_and(key >= start, key < start + SINKS)),
            )
            mask[at, :, 0:wide] = jnp.where(allowed, 0.0, -1e30)

    def normalise():
        @pl.loop(0, count // 32)
        def _(i):
            at = pl.ds(pl.multiple_of(i * 32, 32), 32)
            square = jnp.zeros((32, 8 * shard), f32)
            for p in range(4):
                wide = tok[at, p * 8 * shard : (p + 1) * 8 * shard].astype(f32)
                square = square + wide * wide
            mean = jnp.sum(square, axis=-1, keepdims=True) * (1.0 / depth)
            scale = lax.rsqrt(mean + 1e-06)
            for p in range(4):
                wide = tok[at, p * 8 * shard : (p + 1) * 8 * shard].astype(f32)
                normed[p, at, :] = (wide * scale * gains[p, 0:1, :]).astype(bf16)

    def product(k, p):
        block = fulls[k][p].reshape(8 * shard, fulls[k].shape[-1])
        return jnp.dot(normed[p], block, preferred_element_type=f32)

    def take_mate(k, p):
        ref = fulls[k].at[p, :, 1 - c]
        remote(ref, ref, mate_send.at[k, p], mate_recv.at[k, p], mate).wait_recv()

    orders = (z, 1 + z % 2, 2 + z // 2 - 2 * (z % 2), 3 * (1 - z // 2))

    def add(k, n):
        p = orders[n]
        take_mate(k, p)
        if n == 0:
            accs[k][...] = product(k, p)
        else:
            accs[k][...] += product(k, p)

    def bias_line():
        total = jnp.zeros((8, width), f32)
        for n in range(8):
            both = sides[n, group]
            total = total + spread(
                [pltpu.roll(both, 7, 0), pltpu.roll(both, 6, 0)], width // 8, n, width
            )
        return total[0:1, :]

    def finish(k, bias):
        lo, hi = CHUNKS[k]
        p = orders[3]
        take_mate(k, p)
        joined = accs[k][...] + product(k, p) + bias[:, lo:hi]
        for h in range(lo // HEAD_DIM, hi // HEAD_DIM):
            v = joined[:, h * HEAD_DIM - lo : (h + 1) * HEAD_DIM - lo]
            qkv[h] = rotated(v, cosine[...], sine[...]) if h <= GROUP else v.astype(bf16)

    def out_at(k, at):
        lo, hi = CHUNKS[k]
        place = (pl.ds(at * BLOCK, BLOCK), pl.ds(lo, hi - lo))
        return ctx.at[place], out_hbm.at[place]

    def out_remote(k, at):
        source, to = out_at(k, at)
        return remote(source, to, out_send.at[k - 1, at], out_recv.at[k - 1, at], partner)

    def out_local(k, at):
        source, to = out_at(k, at)
        return pltpu.make_async_copy(source, to, out_sem.at[k - 1, at])

    def attend(k):
        lo, hi = CHUNKS[k]
        heads = range(lo // HEAD_DIM, hi // HEAD_DIM)
        many = len(heads)
        for at in range(count // BLOCK):
            first, wide = reach(at)
            here = slice(at * BLOCK, (at + 1) * BLOCK)
            seen = slice(first * BLOCK, (at + 1) * BLOCK)
            query = jnp.concatenate([qkv[h, here, :] for h in heads], axis=0)
            scores = lax.dot_general(
                query, qkv[GROUP, seen, :], (((1,), (1,)), ((), ())), preferred_element_type=f32
            ) * (1.0 / math.sqrt(HEAD_DIM))
            scores = scores.reshape(many, BLOCK, wide) + mask[at, :, 0:wide][None]
            peak = jnp.max(scores, axis=-1, keepdims=True)
            expo = jnp.exp(scores - peak)
            weights = (expo * (1.0 / jnp.sum(expo, axis=-1, keepdims=True))).astype(bf16)
            mixed = jnp.dot(
                weights.reshape(many * BLOCK, wide), qkv[GROUP + 1, seen, :],
                preferred_element_type=f32,
            ).astype(bf16)
            for n, h in enumerate(heads):
                ctx[here, h * HEAD_DIM : (h + 1) * HEAD_DIM] = mixed[n * BLOCK : (n + 1) * BLOCK]

            @pl.when(swapped)
            def _():
                out_remote(k, at).start()

            @pl.when(jnp.logical_not(swapped))
            def _():
                out_local(k, at).start()

    def receive(d, k):
        for way in range(2):
            p = z + d * (1 - 2 * way)

            @pl.when(has(way, d))
            def _():
                if d == 1:
                    for j in range(4):
                        ref = fulls[k].at[p, j, c]
                        remote(
                            ref, ref, near_send.at[way, k, j], near_recv.at[way, k, j], mate
                        ).wait_recv()
                else:
                    ref = half(k, p)
                    remote(
                        ref, ref, far_send.at[way, k, d - 2], far_recv.at[way, k, d - 2], mate
                    ).wait_recv()
                if d < 3:
                    copy = far(way, k, d + 1)

                    @pl.when(sends(way))
                    def _():
                        copy.start()
                send_mate(k, p).start()

    def pass_tokens(n):
        @pl.when(swapped)
        def _():
            tok_x(n).wait_recv()
            tok_y(n).start()

    tables()
    masks()
    for k in range(number):
        receive(1, k)
        pass_tokens(k)

    @pl.when(swapped)
    def _():
        for n in range(PARTS):
            at = tok.at[part_rows(1 - y, n)]
            remote(at, at, ty_send.at[n], ty_recv.at[n], mate).wait_recv()

    @pl.when(jnp.logical_not(swapped))
    def _():
        tok_copy.wait()

    normalise()
    bias = bias_line()
    for k in range(number):
        receive(2, k)
        add(k, 0)
        add(k, 1)
    for k in range(number):
        receive(3, k)
        add(k, 2)
        finish(k, bias)
        if k:
            attend(k)

    @pl.when(swapped)
    def _():
        for k in range(1, number):
            for at in range(count // BLOCK):
                out_remote(k, at).wait_recv()
        for k in range(1, number):
            for at in range(count // BLOCK):
                out_remote(k, at).wait_send()
        for n in range(PARTS):
            tok_x(n).wait_send()
            tok_y(n).wait_send()

    @pl.when(jnp.logical_not(swapped))
    def _():
        for k in range(1, number):
            for at in range(count // BLOCK):
                out_local(k, at).wait()

    for copy in lines + shares + list(firsts.values()):
        copy.wait_send()
    for k in range(number):
        for p in range(4):
            send_mate(k, p).wait_send()
        for way in range(2):
            @pl.when(sends(way))
            def _():
                for j in range(4):
                    near(way, k, j).wait_send()
            for d in (2, 3):
                @pl.when(jnp.logical_and(sends(way), has(way, d - 1)))
                def _():
                    far(way, k, d).wait_send()


def serve(tokens, norm_gain, qkv_weight, qkv_bias, lens):
    count, depth = tokens.shape
    shard, columns = qkv_weight.shape
    width = columns // 4
    sizes = [hi - lo for lo, hi in CHUNKS]
    number, blocks = len(sizes), count // BLOCK
    hbm = pl.BlockSpec(memory_space=pltpu.HBM)
    dma, vmem = pltpu.SemaphoreType.DMA, pltpu.VMEM
    f32, bf16 = jnp.float32, jnp.bfloat16
    pair = lambda *shape: [dma(shape), dma(shape)]
    return pl.pallas_call(
        serve_kernel,
        out_shape=jax.ShapeDtypeStruct((count, GROUP * HEAD_DIM), bf16),
        in_specs=[hbm] * 5,
        out_specs=hbm,
        scratch_shapes=[
            vmem(lens.shape, jnp.int32),
            vmem((1, shard), f32),
            vmem((1, columns // 32), f32),
            dma((3,)),
            vmem((4, shard, width), f32),
            *[vmem((3, shard, size), bf16) for size in sizes],
            *[vmem((4, 4, 2, shard, size), bf16) for size in sizes],
            vmem((count, depth), bf16),
            vmem((4, count, 8 * shard), bf16),
            *[vmem((count, size), f32) for size in sizes],
            vmem((GROUP + 2, count, HEAD_DIM), bf16),
            vmem((count, HEAD_DIM), f32),
            vmem((count, HEAD_DIM), f32),
            vmem((blocks, BLOCK, 3 * BLOCK), f32),
            vmem((4, 8, 8 * shard), f32),
            vmem((count, GROUP * HEAD_DIM), bf16),
            vmem((8, 128), f32),
            vmem((4, 8, 128), f32),
            vmem((8, 4, 8, 128), f32),
            dma, dma((4,)),
            *pair(3), *pair(7), *pair(number, 3),
            *pair(2, number, 4), *pair(2, number, 2), *pair(number, 4),
            *pair(PARTS), *pair(PARTS), *pair(number - 1, blocks), dma((number - 1, blocks)),
        ],
        compiler_params=pltpu.CompilerParams(
            collective_id=0, has_side_effects=True, vmem_limit_bytes=60 << 20
        ),
        name="serve",
    )(lens, norm_gain.reshape(1, shard), qkv_bias.reshape(1, -1), qkv_weight, tokens)


def turn_plain(joined, lens):
    count = joined.shape[0]
    half = HEAD_DIM // 2
    pos = jnp.arange(count, dtype=jnp.int32) - starts(lens, count)
    freqs = jnp.exp(-(jnp.arange(half, dtype=jnp.float32) * 2.0 / HEAD_DIM) * math.log(1000000.0))
    angle = pos.astype(jnp.float32)[:, None] * freqs[None, :]
    cosine = jnp.tile(jnp.cos(angle), (1, 2))[:, None, :]
    sine = jnp.tile(jnp.sin(angle), (1, 2))[:, None, :]
    heads = joined.reshape(count, GROUP + 2, HEAD_DIM)
    spun = jnp.concatenate([-heads[..., half:], heads[..., :half]], axis=-1)
    turned = (heads * cosine + spun * sine)[:, : GROUP + 1]
    both = jnp.concatenate([turned, heads[:, GROUP + 1 :]], axis=1)
    return both.reshape(count, -1).astype(jnp.bfloat16)


def project_plain(tokens, norm_gain, qkv_weight, qkv_bias):
    tp_count = lax.axis_size("tp")
    req_count = lax.axis_size("req")
    tp_place = lax.axis_index("tp")
    gain_full, bias_full = (
        lax.all_gather(norm_gain.astype(jnp.bfloat16), ("req", "tp"), axis=0, tiled=True),
        lax.all_gather(qkv_bias.astype(jnp.bfloat16), ("req", "tp"), axis=0, tiled=True),
    )
    width = bias_full.shape[0] // tp_count
    bias_block = lax.dynamic_slice_in_dim(bias_full, tp_place * width, width).astype(jnp.float32)
    normed = normalize(tokens, gain_full)
    weight_b = qkv_weight.astype(jnp.bfloat16)
    count = tokens.shape[0]
    gathered = lax.all_gather(weight_b, "req", axis=0, tiled=True)
    regrouped = lax.all_to_all(gathered, "tp", split_axis=1, concat_axis=0, tiled=True)
    shard_rows = weight_b.shape[0]
    reordered = (
        normed.reshape(count, req_count, tp_count, shard_rows)
        .transpose(0, 2, 1, 3)
        .reshape(count, -1)
    )
    joined = jnp.dot(reordered, regrouped, preferred_element_type=jnp.float32)
    return joined + bias_block[None, :]


def shards(small, tokens, norm_gain, qkv_weight, qkv_bias, lengths):
    if small:
        return serve(tokens, norm_gain, qkv_weight, qkv_bias, lengths)
    qkv = turn_plain(project_plain(tokens, norm_gain, qkv_weight, qkv_bias), lengths[0])
    return attend_turned(qkv, lengths)


def solution(mesh):
    placed = (
        P("req", None),
        P(("req", "tp")),
        P(("req", "tp"), None),
        P(("req", "tp")),
        P("req", None),
    )
    small = mesh.shape["req"] == 8 and mesh.shape["tp"] == 4
    return jax.shard_map(
        functools.partial(shards, small),
        mesh=mesh, in_specs=placed, out_specs=P("req", "tp"), check_vma=False,
    )
```

```python
import functools
import math

import jax
import jax.numpy as jnp
from jax import lax
from jax.experimental import pallas as pl
from jax.experimental.pallas import tpu as pltpu
from jax.sharding import PartitionSpec as P

HEAD_DIM = 128
SINKS = 4
GROUP = 7
WINDOW = 160
MOST = 256
MESH = pl.DeviceIdType.MESH


def normalize(values, gain):
    wide = values.astype(jnp.float32)
    meansq = jnp.mean(wide * wide, axis=-1, keepdims=True)
    return (wide * lax.rsqrt(meansq + 1e-06) * gain.astype(jnp.float32)).astype(jnp.bfloat16)


def starts(lens, count):
    index = jnp.arange(count, dtype=jnp.int32)
    start, end = jnp.zeros((count,), jnp.int32), jnp.int32(0)
    for t in range(lens.shape[0]):
        end = end + lens[t]
        start = jnp.where(index >= end, end, start)
    return start


def rotated(v, cosine, sine):
    return (v * cosine + pltpu.roll(v, HEAD_DIM // 2, 1) * sine).astype(jnp.bfloat16)


def start_of(query_at, lens_ref):
    start, end = jnp.zeros_like(query_at), jnp.int32(0)
    for t in range(lens_ref.shape[1]):
        end = end + lens_ref[0, t]
        start = jnp.where(query_at >= end, end, start)
    return start


def attend_kernel(lens_ref, qkv_ref, out_ref):
    count = qkv_ref.shape[0]
    block = 128
    back = -(-(MOST - 1) // block)
    for at in range(count // block):
        first = max(0, at - back)
        wide = (at + 1 - first) * block
        rows = slice(at * block, (at + 1) * block)
        seen = slice(first * block, (at + 1) * block)
        query_at = at * block + lax.broadcasted_iota(jnp.int32, (block, 1), 0)
        key_at = first * block + lax.broadcasted_iota(jnp.int32, (block, wide), 1)
        start = start_of(query_at, lens_ref)
        low = jnp.maximum(query_at - (WINDOW - 1), start)
        allowed = jnp.logical_and(
            key_at <= query_at,
            jnp.logical_or(
                key_at >= low, jnp.logical_and(key_at >= start, key_at < start + SINKS)
            ),
        )
        query = jnp.concatenate(
            [qkv_ref[rows, h * HEAD_DIM : (h + 1) * HEAD_DIM] for h in range(GROUP)], axis=0
        )
        scores = lax.dot_general(
            query, qkv_ref[seen, GROUP * HEAD_DIM : (GROUP + 1) * HEAD_DIM],
            (((1,), (1,)), ((), ())), preferred_element_type=jnp.float32,
        ) * (1.0 / math.sqrt(HEAD_DIM))
        scores = jnp.where(allowed[None], scores.reshape(GROUP, block, wide), -1e30)
        peak = jnp.max(scores, axis=-1, keepdims=True)
        expo = jnp.exp(scores - peak)
        weights = (expo * (1.0 / jnp.sum(expo, axis=-1, keepdims=True))).astype(jnp.bfloat16)
        mixed = jnp.dot(
            weights.reshape(GROUP * block, wide), qkv_ref[seen, (GROUP + 1) * HEAD_DIM :],
            preferred_element_type=jnp.float32,
        ).astype(jnp.bfloat16)
        for h in range(GROUP):
            out_ref[rows, h * HEAD_DIM : (h + 1) * HEAD_DIM] = mixed[h * block : (h + 1) * block]


def attend_turned(qkv, lens):
    count = qkv.shape[0]
    vmem = pl.BlockSpec(memory_space=pltpu.VMEM)
    return pl.pallas_call(
        attend_kernel,
        out_shape=jax.ShapeDtypeStruct((count, GROUP * HEAD_DIM), jnp.bfloat16),
        in_specs=[pl.BlockSpec(memory_space=pltpu.SMEM), vmem],
        out_specs=vmem,
        compiler_params=pltpu.CompilerParams(vmem_limit_bytes=64 << 20),
        name="attention",
    )(lens, qkv)


CHUNKS = ((896, 1152), (0, 384), (384, 640), (640, 896))
OFF = 3
BLOCK = 128
PARTS = 4
UNITS, DIRECT = 8, 5


def serve_kernel(
    lens_hbm, gain_hbm, bias_hbm, w_hbm, tok_hbm, out_hbm,
    lens_ref, gain_ref, bias_ref, small_sem, wide_w, wb0, wb1, wb2, wb3, full0, full1, full2, full3,
    fullo, tok, tok2, normed, normed2, acco, acc0, acc1, acc2, acc3, qkv, kv2, cosine, sine, cosine2, sine2, mask, gains, ctx, side, line, sides,
    tok_sem, w_sem, line_send, line_recv, side_send, side_recv, first_send, first_recv,
    near_send, near_recv, far_send, far_recv, mate_send, mate_recv,
    tx_send, tx_recv, ty_send, ty_recv, tz_send, tz_recv, tv_send, tv_recv, tm_send, tm_recv,
    kx_send, kx_recv, kz_send, kz_recv, kv_send, kv_recv, out_send, out_recv, out_sem,
):
    f32, bf16 = jnp.float32, jnp.bfloat16
    wbs, fulls, accs = (wb0, wb1, wb2, wb3), (full0, full1, full2, full3), (acc0, acc1, acc2, acc3)
    number = len(CHUNKS)
    req, tp = lax.axis_index("req"), lax.axis_index("tp")
    z, x, y, c = req // 2, req % 2, tp // 2, tp % 2
    group, place, me = 2 * y + x, 2 * x + y, 4 * x + 2 * y + c
    count, depth = tok.shape
    shard = wide_w.shape[1]
    width = wide_w.shape[2]
    swapped = x != c
    middle = jnp.logical_or(z == 1, z == 2)
    end = jnp.logical_not(middle)
    pair = jnp.where(middle, 3 * (z // 2), 1 + z // 2)
    orders = (z, 1 + z % 2, 2 + z // 2 - 2 * (z % 2), 3 * (1 - z // 2))

    def device(at_z, at_x, at_y, at_c):
        return (2 * at_z + at_x, 2 * at_y + at_c)

    def flipped(m):
        fx, fy, fc = m // 4, m // 2 % 2, m % 2
        return (
            1 - x if fx else x,
            1 - y if fy else y,
            1 - c if fc else c,
        )

    def remote(source, to, send_sem, recv_sem, where):
        return pltpu.make_async_remote_copy(
            src_ref=source, dst_ref=to, send_sem=send_sem, recv_sem=recv_sem,
            device_id=where, device_id_type=MESH,
        )

    partner = device(z, 1 - x, y, 1 - c)
    mate = device(z, x, y, 1 - c)

    barrier = pltpu.get_barrier_semaphore()
    for m in range(1, 8):
        pl.semaphore_signal(barrier, inc=1, device_id=device(z, *flipped(m)), device_id_type=MESH)
    for dz in range(1, 4):
        pl.semaphore_signal(
            barrier, inc=1, device_id=device((z + dz) % 4, x, y, c), device_id_type=MESH
        )

    pl.semaphore_signal(
        barrier, inc=1, device_id=device(pair, 1 - x, y, 1 - c), device_id_type=MESH
    )

    smalls = [
        pltpu.make_async_copy(source, to, small_sem.at[k])
        for k, (source, to) in enumerate(
            ((gain_hbm, gain_ref), (bias_hbm, bias_ref), (lens_hbm, lens_ref))
        )
    ]
    for copy in smalls:
        copy.start()
    flips = ((0, 0), (1, 0), (0, 1), (1, 1))
    loads = []
    for k, (fx, fy) in enumerate(flips):
        g = 2 * (1 - y if fy else y) + (1 - x if fx else x)
        copy = pltpu.make_async_copy(
            w_hbm.at[:, pl.ds(pl.multiple_of(g * width, 128), width)], wide_w.at[k], w_sem.at[k]
        )
        copy.start()
        loads.append(copy)
    tok_copy = pltpu.make_async_copy(tok_hbm, tok, tok_sem)

    @pl.when(jnp.logical_not(swapped))
    def _():
        tok_copy.start()

    def rounded(v):
        return v.astype(bf16).astype(f32)

    for copy in smalls:
        copy.wait()
    side[...] = jnp.zeros_like(side)
    side[0:1, 0:shard] = rounded(gain_ref[...])
    side[1:2, :] = rounded(bias_ref[:, 0:128])
    side[2:3, 0 : width // 8 - 128] = rounded(bias_ref[:, 128:])
    side[3:4, 0 : lens_ref.shape[1]] = lens_ref[...].astype(f32)

    pl.semaphore_wait(barrier, 11)
    lines = []
    for dz in range(1, 4):
        copy = remote(
            side, line.at[z], line_send.at[dz - 1], line_recv.at[dz - 1],
            device((z + dz) % 4, x, y, c),
        )
        copy.start()
        lines.append(copy)
    line[z] = side[...]

    def half(k, p):
        return fulls[k].at[p, :, c]

    def near(way, k, j):
        ref = fulls[k].at[z, j, c]
        return remote(
            ref, ref, near_send.at[way, k, j], near_recv.at[way, k, j],
            device(z - 1 + 2 * way, x, y, c),
        )

    def far(way, k, d):
        ref = half(k, z + (d - 1) * (1 - 2 * way))
        return remote(
            ref, ref, far_send.at[way, k, d - 2], far_recv.at[way, k, d - 2],
            device(z - 1 + 2 * way, x, y, c),
        )

    def sends(way, k):
        return z >= (2 if k == OFF else 1) if way == 0 else z <= (1 if k == OFF else 2)

    def start_near(k, j):
        for way in range(2):
            copy = near(way, k, j)

            @pl.when(sends(way, k))
            def _():
                copy.start()

    def row_unit(n):
        at = c + (1 - y) * 2 * n + y * 2 * (UNITS - 1 - n)
        size = count // 2 // UNITS
        return pl.ds(pl.multiple_of(at * size, size), size)

    def unit_z(n):
        at = row_unit(n)
        return remote(
            tok_hbm.at[at], tok2.at[at], tz_send.at[n], tz_recv.at[n], device(pair, x, y, c)
        )

    def unit_y(n):
        at = tok2.at[row_unit(n)]
        return remote(at, at, tv_send.at[n], tv_recv.at[n], device(z, x, 1 - y, c))

    def unit_mate(n):
        at = tok2.at[row_unit(n)]
        return remote(at, at, tm_send.at[n], tm_recv.at[n], mate)

    def start_units(*which):
        @pl.when(end)
        def _():
            for n in which:
                unit_z(n).start()

    firsts = {}
    for i, (fx, fy) in enumerate(flips):
        loads[i].wait()
        for k, (lo, hi) in enumerate(CHUNKS):
            if i == 0:
                fulls[k][z, place, c] = wide_w[i, :, lo:hi].astype(bf16)
            else:
                wbs[k][i - 1] = wide_w[i, :, lo:hi].astype(bf16)
                copy = remote(
                    wbs[k].at[i - 1], fulls[k].at[z, place, c],
                    first_send.at[k, i - 1], first_recv.at[k, i - 1],
                    device(z, 1 - x if fx else x, 1 - y if fy else y, c),
                )
                copy.start()
                firsts[k, i - 1] = copy
        if i == 0:
            start_near(OFF, place)
            start_near(0, place)
            start_units(0, 1)

            @pl.when(middle)
            def _():
                for way in range(2):
                    near(way, 1, place).start()

    def send_mate(k, p):
        ref = half(k, p)
        return remote(ref, ref, mate_send.at[k, p], mate_recv.at[k, p], mate)

    for copy in lines:
        copy.wait_recv()
    shares = []
    for m in range(1, 8):
        copy = remote(
            line, sides.at[me], side_send.at[m - 1], side_recv.at[m - 1], device(z, *flipped(m))
        )
        copy.start()
        shares.append(copy)
    sides[me] = line[...]

    rows = count // 2 // PARTS

    def part_rows(at_y, n):
        return pl.ds(pl.multiple_of(at_y * (count // 2) + n * rows, rows), rows)

    def tok_x(n):
        at = part_rows(y, n)
        return remote(tok_hbm.at[at], tok.at[at], tx_send.at[n], tx_recv.at[n], partner)

    def tok_y(n):
        at = tok.at[part_rows(y, n)]
        return remote(at, at, ty_send.at[n], ty_recv.at[n], device(z, x, 1 - y, c))

    def start_tokens(n):
        @pl.when(swapped)
        def _():
            tok_x(n).start()

    def forward(k, *which):
        for i in which:
            fx, fy = flips[i + 1]
            firsts[k, i].wait_recv()
            start_near(k, 2 * (1 - x if fx else x) + (1 - y if fy else y))

    def own_mate(k):
        if k != OFF:
            send_mate(k, z).start()
        else:

            @pl.when(middle)
            def _():
                send_mate(k, z).start()

    def start_end_near(k):
        @pl.when(end)
        def _():
            start_near(k, place)

    forward(OFF, 0, 1)
    forward(0, 0, 1)
    start_tokens(0)
    start_end_near(1)
    forward(1, 0, 1)
    for n in range(1, PARTS):
        start_tokens(n)

    @pl.when(middle)
    def _():
        for way in range(2):
            near(way, 2, place).start()

    for k in (OFF, 0, 1):
        forward(k, 2)
        own_mate(k)
    start_units(2, 3)
    start_end_near(2)
    forward(2, 0, 1, 2)
    own_mate(2)
    start_units(*range(4, DIRECT))

    for copy in shares:
        copy.wait_recv()

    def spread(piece, step, n, size):
        wide = jnp.concatenate(piece + [jnp.zeros((8, size - 128 * len(piece)), f32)], axis=1)
        return pltpu.roll(wide, step * n, 1) if n else wide

    for p in range(4):
        total = jnp.zeros((8, 8 * 128), f32)
        for n in range(8):
            total = total + spread([sides[n, p]], shard, n, 8 * 128)
        gains[p] = total[:, 0 : 8 * shard]

    def ends_of(lens):
        ends, last = [], jnp.zeros((1, 1), f32)
        for t in range(lens_ref.shape[1]):
            last = last + lens[3:4, t : t + 1]
            ends.append(last)
        return ends

    own_ends = ends_of(sides[4 * c + 2 * y + c, z])

    def start_at(query, ends):
        start = jnp.zeros_like(query)
        for e in ends:
            start = jnp.where(query >= e, e, start)
        return start

    def tables(cosine, sine, ends):
        query = lax.broadcasted_iota(jnp.int32, (count, 1), 0).astype(f32)
        pos = query - start_at(query, ends)
        lane = lax.broadcasted_iota(jnp.int32, (1, HEAD_DIM), 1)
        mid = HEAD_DIM // 2
        freqs = jnp.exp(-((lane % mid).astype(f32) * 2.0 / HEAD_DIM) * math.log(1000000.0))
        angle = pos * freqs
        cosine[...] = jnp.cos(angle)
        sine[...] = jnp.where(lane < mid, -1.0, 1.0) * jnp.sin(angle)

    back = -(-(MOST - 1) // BLOCK)

    def reach(at):
        first = max(0, at - back)
        return first, (at + 1 - first) * BLOCK

    def masks():
        for at in range(count // BLOCK):
            first, wide = reach(at)
            query = (at * BLOCK + lax.broadcasted_iota(jnp.int32, (BLOCK, 1), 0)).astype(f32)
            key = (first * BLOCK + lax.broadcasted_iota(jnp.int32, (BLOCK, wide), 1)).astype(f32)
            start = start_at(query, own_ends)
            low = jnp.maximum(query - (WINDOW - 1), start)
            allowed = jnp.logical_and(
                key <= query,
                jnp.logical_or(key >= low, jnp.logical_and(key >= start, key < start + SINKS)),
            )
            mask[at, :, 0:wide] = jnp.where(allowed, 0.0, -1e30)

    def normalise(tok, normed, first=0, many=count):
        @pl.loop(0, many // 32)
        def _(i):
            at = pl.ds(pl.multiple_of(first + i * 32, 32), 32)
            square = jnp.zeros((32, 8 * shard), f32)
            for p in range(4):
                wide = tok[at, p * 8 * shard : (p + 1) * 8 * shard].astype(f32)
                square = square + wide * wide
            mean = jnp.sum(square, axis=-1, keepdims=True) * (1.0 / depth)
            scale = lax.rsqrt(mean + 1e-06)
            for p in range(4):
                part = slice(p * 8 * shard, (p + 1) * 8 * shard)
                wide = tok[at, part].astype(f32)
                normed[at, part] = (wide * scale * gains[p, 0:1, :]).astype(bf16)

    def product(k, p):
        block = fulls[k][p].reshape(8 * shard, fulls[k].shape[-1])
        part = pl.ds(pl.multiple_of(p * 8 * shard, 128), 8 * shard)
        return jnp.dot(normed[:, part], block, preferred_element_type=f32)

    def whole(normed, full):
        block = full[...].reshape(depth, full.shape[-1])
        return jnp.dot(normed[...], block, preferred_element_type=f32)

    def take_mate(k, p):
        ref = fulls[k].at[p, :, 1 - c]
        remote(ref, ref, mate_send.at[k, p], mate_recv.at[k, p], mate).wait_recv()

    def add(k, n):
        p = orders[n]
        take_mate(k, p)
        if n == 0:
            accs[k][...] = product(k, p)
        else:
            accs[k][...] += product(k, p)

    def bias_line(group):
        total = jnp.zeros((8, width), f32)
        for n in range(8):
            both = sides[n, group]
            total = total + spread(
                [pltpu.roll(both, 7, 0), pltpu.roll(both, 6, 0)], width // 8, n, width
            )
        return total[0:1, :]

    def finish(k, bias, sums):
        lo, hi = CHUNKS[k]
        joined = sums + bias[:, lo:hi]
        for h in range(lo // HEAD_DIM, hi // HEAD_DIM):
            v = joined[:, h * HEAD_DIM - lo : (h + 1) * HEAD_DIM - lo]
            qkv[h] = rotated(v, cosine[...], sine[...]) if h <= GROUP else v.astype(bf16)

    def chunk_end(k):
        if k == OFF:

            @pl.when(end)
            def _():
                kv_send_copy().wait_recv()

            return

        @pl.when(end)
        def _():
            add(k, 0)

        ends_get(1, k)
        ends_get(2, k)

        @pl.when(end)
        def _():
            add(k, 1)
            add(k, 2)

        ends_get(3, k)

        @pl.when(end)
        def _():
            p = orders[3]
            take_mate(k, p)
            finish(k, bias, accs[k][...] + product(k, p))

    def chunk_middle(k):
        @pl.when(middle)
        def _():
            if k != OFF:
                for n in range(4):
                    take_mate(k, orders[n])
            finish(k, bias, whole(normed, fulls[k]))

    def out_at(k):
        lo, hi = CHUNKS[k]
        return ctx.at[:, pl.ds(lo, hi - lo)], out_hbm.at[:, pl.ds(lo, hi - lo)]

    def out_remote(k):
        source, to = out_at(k)
        return remote(source, to, out_send.at[k - 1], out_recv.at[k - 1], partner)

    def out_local(k):
        source, to = out_at(k)
        return pltpu.make_async_copy(source, to, out_sem.at[k - 1])

    def attend(k):
        lo, hi = CHUNKS[k]
        heads = range(lo // HEAD_DIM, hi // HEAD_DIM)
        many = len(heads)
        for at in range(count // BLOCK):
            first, wide = reach(at)
            here = slice(at * BLOCK, (at + 1) * BLOCK)
            seen = slice(first * BLOCK, (at + 1) * BLOCK)
            query = jnp.concatenate([qkv[h, here, :] for h in heads], axis=0)
            scores = lax.dot_general(
                query, qkv[GROUP, seen, :], (((1,), (1,)), ((), ())), preferred_element_type=f32
            ) * (1.0 / math.sqrt(HEAD_DIM))
            scores = scores.reshape(many, BLOCK, wide) + mask[at, :, 0:wide][None]
            peak = jnp.max(scores, axis=-1, keepdims=True)
            expo = jnp.exp(scores - peak)
            weights = (expo * (1.0 / jnp.sum(expo, axis=-1, keepdims=True))).astype(bf16)
            mixed = jnp.dot(
                weights.reshape(many * BLOCK, wide), qkv[GROUP + 1, seen, :],
                preferred_element_type=f32,
            ).astype(bf16)
            for n, h in enumerate(heads):
                ctx[here, h * HEAD_DIM : (h + 1) * HEAD_DIM] = mixed[n * BLOCK : (n + 1) * BLOCK]

        @pl.when(swapped)
        def _():
            out_remote(k).start()

        @pl.when(jnp.logical_not(swapped))
        def _():
            out_local(k).start()

    def receive(who, d, k):
        for way in range(2):
            p = z + d * (1 - 2 * way)

            @pl.when(z == ((1, 2, 0), (2, 1, 3))[way][who])
            def _():
                if d == 1:
                    for j in range(4):
                        ref = fulls[k].at[p, j, c]
                        remote(
                            ref, ref, near_send.at[way, k, j], near_recv.at[way, k, j], mate
                        ).wait_recv()
                else:
                    ref = half(k, p)
                    remote(
                        ref, ref, far_send.at[way, k, d - 2], far_recv.at[way, k, d - 2], mate
                    ).wait_recv()
                if who == 1 or (who == 0 and k != OFF):
                    far(way, k, d + 1).start()
                send_mate(k, p).start()

    def inner(d, k):
        receive(0, d, k)

    def outer(d, k):
        receive(1, d, k)

    def ends_get(d, k):
        receive(2, d, k)

    def take_unit(n):
        @pl.when(middle)
        def _():
            unit_z(n).wait_recv()
            if n < UNITS - DIRECT:
                unit_y(n).start()
            unit_mate(n).start()

    def take_sides():
        @pl.when(middle)
        def _():
            for n in range(UNITS - DIRECT):
                at = tok2.at[row_unit(UNITS - 1 - n)]
                remote(at, at, tv_send.at[n], tv_recv.at[n], mate).wait_recv()
                unit_mate(UNITS - 1 - n).start()

    def take_mates():
        for n in range(UNITS):
            at = c + (1 - y) * 2 * n + y * 2 * (UNITS - 1 - n) + 1 - 2 * c
            size = count // 2 // UNITS
            ref = tok2.at[pl.ds(pl.multiple_of(at * size, size), size)]
            remote(ref, ref, tm_send.at[n], tm_recv.at[n], mate).wait_recv()

    both_mid = jnp.logical_and(middle, swapped)
    kx_planes = (0, 2, 3)

    def other_x(i):
        p = orders[kx_planes[i]]
        return remote(fulls[OFF].at[p], fullo.at[p], kx_send.at[i], kx_recv.at[i], partner)

    def other_z(n):
        ref = fullo.at[orders[n]]
        return remote(ref, ref, kz_send.at[0], kz_recv.at[0], device(3 - z, x, y, c))

    def give_other(n):
        @pl.when(middle)
        def _():
            take_mate(OFF, orders[n])
        if n in kx_planes:
            @pl.when(both_mid)
            def _():
                other_x(kx_planes.index(n)).start()

    def take_other(i):
        @pl.when(both_mid)
        def _():
            other_x(i).wait_recv()
            if i == 0:
                other_z(0).start()

    def last_others():
        @pl.when(both_mid)
        def _():
            other_z(1).wait_recv()

    def kv_send_copy():
        return remote(
            kv2, qkv.at[pl.ds(CHUNKS[OFF][0] // HEAD_DIM, 2)], kv_send.at[0], kv_recv.at[0], device(pair, c, y, x)
        )

    def serve_end():
        def sums(full):
            acco[...] = whole(normed2, full)

        @pl.when(swapped)
        def _():
            sums(fullo)

        @pl.when(jnp.logical_not(swapped))
        def _():
            sums(fulls[OFF])

        lo, hi = CHUNKS[OFF]
        joined = acco[...] + bias_line(2 * y + c)[:, lo:hi]
        for h in range(2):
            v = joined[:, h * HEAD_DIM : (h + 1) * HEAD_DIM]
            kv2[h] = rotated(v, cosine2[...], sine2[...])
        kv_send_copy().start()

    def pass_tokens(n):
        @pl.when(swapped)
        def _():
            tok_x(n).wait_recv()
            tok_y(n).start()

    take_unit(0)
    take_unit(1)
    inner(1, OFF)
    give_other(0)
    pass_tokens(0)
    inner(1, 0)
    outer(1, OFF)
    inner(1, 1)
    outer(1, 0)
    pass_tokens(1)
    inner(1, 2)
    give_other(2)

    @pl.when(jnp.logical_not(swapped))
    def _():
        tok_copy.wait()
        normalise(tok, normed)

    pass_tokens(2)
    outer(1, 1)
    inner(2, OFF)
    tables(cosine, sine, own_ends)
    masks()
    take_unit(2)
    pass_tokens(3)
    give_other(1)
    give_other(3)
    inner(2, 0)

    @pl.when(middle)
    def _():
        tables(cosine2, sine2, ends_of(sides[me, pair]))

    take_unit(3)

    @pl.when(swapped)
    def _():
        normalise(tok, normed, y * (count // 2), count // 2)

    take_other(0)
    inner(2, 1)
    outer(1, 2)
    take_other(1)

    @pl.when(swapped)
    def _():
        for n in range(PARTS):
            at = tok.at[part_rows(1 - y, n)]
            remote(at, at, ty_send.at[n], ty_recv.at[n], mate).wait_recv()
        normalise(tok, normed, (1 - y) * (count // 2), count // 2)

    bias = bias_line(group)
    chunk_middle(0)
    for n in range(4, DIRECT):
        take_unit(n)
    take_sides()
    chunk_middle(1)
    inner(2, 2)

    @pl.when(middle)
    def _():
        take_mates()
        normalise(tok2, normed2)

    take_other(2)
    last_others()
    pl.when(middle)(serve_end)
    chunk_end(0)
    for k in range(1, number):
        chunk_end(k)
        if k > 1:
            chunk_middle(k)
        attend(k)

    @pl.when(swapped)
    def _():
        for k in range(1, number):
            out_remote(k).wait_recv()
        for k in range(1, number):
            out_remote(k).wait_send()
        for n in range(PARTS):
            tok_x(n).wait_send()
            tok_y(n).wait_send()

    @pl.when(jnp.logical_not(swapped))
    def _():
        for k in range(1, number):
            out_local(k).wait()

    for copy in lines + shares + list(firsts.values()):
        copy.wait_send()
    for k in range(number):
        def mates():
            for p in range(4):
                send_mate(k, p).wait_send()

        if k != OFF:
            mates()
        else:
            pl.when(middle)(mates)
        for way in range(2):
            @pl.when(sends(way, k))
            def _():
                for j in range(4):
                    near(way, k, j).wait_send()

            @pl.when(z == 2 - way if k == OFF else middle)
            def _():
                far(way, k, 2).wait_send()

            if k != OFF:
                @pl.when(z == 1 + way)
                def _():
                    far(way, k, 3).wait_send()

    @pl.when(end)
    def _():
        for n in range(DIRECT):
            unit_z(n).wait_send()

    @pl.when(middle)
    def _():
        for n in range(UNITS - DIRECT):
            unit_y(n).wait_send()
        for n in range(UNITS):
            unit_mate(n).wait_send()
        kv_send_copy().wait_send()

    @pl.when(both_mid)
    def _():
        for i in range(len(kx_planes)):
            other_x(i).wait_send()
        other_z(0).wait_send()


def serve(tokens, norm_gain, qkv_weight, qkv_bias, lens):
    count, depth = tokens.shape
    shard, columns = qkv_weight.shape
    width = columns // 4
    sizes = [hi - lo for lo, hi in CHUNKS]
    number, blocks = len(sizes), count // BLOCK
    hbm = pl.BlockSpec(memory_space=pltpu.HBM)
    dma, vmem = pltpu.SemaphoreType.DMA, pltpu.VMEM
    f32, bf16 = jnp.float32, jnp.bfloat16
    two = lambda *shape: [dma(shape), dma(shape)]
    return pl.pallas_call(
        serve_kernel,
        out_shape=jax.ShapeDtypeStruct((count, GROUP * HEAD_DIM), bf16),
        in_specs=[hbm] * 5,
        out_specs=hbm,
        scratch_shapes=[
            vmem(lens.shape, jnp.int32),
            vmem((1, shard), f32),
            vmem((1, columns // 32), f32),
            dma((3,)),
            vmem((4, shard, width), f32),
            *[vmem((3, shard, size), bf16) for size in sizes],
            *[vmem((4, 4, 2, shard, size), bf16) for size in sizes],
            vmem((4, 4, 2, shard, sizes[OFF]), bf16),
            vmem((count, depth), bf16),
            vmem((count, depth), bf16),
            vmem((count, depth), bf16),
            vmem((count, depth), bf16),
            vmem((count, sizes[OFF]), f32),
            *[vmem((count, size), f32) for size in sizes],
            vmem((GROUP + 2, count, HEAD_DIM), bf16),
            vmem((2, count, HEAD_DIM), bf16),
            *[vmem((count, HEAD_DIM), f32)] * 4,
            vmem((blocks, BLOCK, 3 * BLOCK), f32),
            vmem((4, 8, 8 * shard), f32),
            vmem((count, GROUP * HEAD_DIM), bf16),
            vmem((8, 128), f32),
            vmem((4, 8, 128), f32),
            vmem((8, 4, 8, 128), f32),
            dma, dma((4,)),
            *two(3), *two(7), *two(number, 3),
            *two(2, number, 4), *two(2, number, 2), *two(number, 4),
            *two(PARTS), *two(PARTS), *two(DIRECT), *two(UNITS - DIRECT), *two(UNITS),
            *two(3), *two(1), *two(1), *two(number - 1), dma((number - 1,)),
        ],
        compiler_params=pltpu.CompilerParams(
            collective_id=0, has_side_effects=True, vmem_limit_bytes=60 << 20
        ),
        name="serve",
    )(lens, norm_gain.reshape(1, shard), qkv_bias.reshape(1, -1), qkv_weight, tokens)


def turn_plain(joined, lens):
    count = joined.shape[0]
    half = HEAD_DIM // 2
    pos = jnp.arange(count, dtype=jnp.int32) - starts(lens, count)
    freqs = jnp.exp(-(jnp.arange(half, dtype=jnp.float32) * 2.0 / HEAD_DIM) * math.log(1000000.0))
    angle = pos.astype(jnp.float32)[:, None] * freqs[None, :]
    cosine = jnp.tile(jnp.cos(angle), (1, 2))[:, None, :]
    sine = jnp.tile(jnp.sin(angle), (1, 2))[:, None, :]
    heads = joined.reshape(count, GROUP + 2, HEAD_DIM)
    spun = jnp.concatenate([-heads[..., half:], heads[..., :half]], axis=-1)
    turned = (heads * cosine + spun * sine)[:, : GROUP + 1]
    both = jnp.concatenate([turned, heads[:, GROUP + 1 :]], axis=1)
    return both.reshape(count, -1).astype(jnp.bfloat16)


def project_plain(tokens, norm_gain, qkv_weight, qkv_bias):
    tp_count = lax.axis_size("tp")
    req_count = lax.axis_size("req")
    tp_place = lax.axis_index("tp")
    gain_full, bias_full = (
        lax.all_gather(norm_gain.astype(jnp.bfloat16), ("req", "tp"), axis=0, tiled=True),
        lax.all_gather(qkv_bias.astype(jnp.bfloat16), ("req", "tp"), axis=0, tiled=True),
    )
    width = bias_full.shape[0] // tp_count
    bias_block = lax.dynamic_slice_in_dim(bias_full, tp_place * width, width).astype(jnp.float32)
    normed = normalize(tokens, gain_full)
    weight_b = qkv_weight.astype(jnp.bfloat16)
    count = tokens.shape[0]
    gathered = lax.all_gather(weight_b, "req", axis=0, tiled=True)
    regrouped = lax.all_to_all(gathered, "tp", split_axis=1, concat_axis=0, tiled=True)
    shard_rows = weight_b.shape[0]
    reordered = (
        normed.reshape(count, req_count, tp_count, shard_rows)
        .transpose(0, 2, 1, 3)
        .reshape(count, -1)
    )
    joined = jnp.dot(reordered, regrouped, preferred_element_type=jnp.float32)
    return joined + bias_block[None, :]


def shards(small, tokens, norm_gain, qkv_weight, qkv_bias, lengths):
    if small:
        return serve(tokens, norm_gain, qkv_weight, qkv_bias, lengths)
    qkv = turn_plain(project_plain(tokens, norm_gain, qkv_weight, qkv_bias), lengths[0])
    return attend_turned(qkv, lengths)


def solution(mesh):
    placed = (
        P("req", None),
        P(("req", "tp")),
        P(("req", "tp"), None),
        P(("req", "tp")),
        P("req", None),
    )
    small = mesh.shape["req"] == 8 and mesh.shape["tp"] == 4
    return jax.shard_map(
        functools.partial(shards, small),
        mesh=mesh, in_specs=placed, out_specs=P("req", "tp"), check_vma=False,
    )
```

```python
import functools
import math

import jax
import jax.numpy as jnp
from jax import lax
from jax.experimental import pallas as pl
from jax.experimental.pallas import tpu as pltpu
from jax.sharding import PartitionSpec as P

HEAD_DIM = 128
SINKS = 4
GROUP = 7
WINDOW = 160
MOST = 256
MESH = pl.DeviceIdType.MESH


def normalize(values, gain):
    wide = values.astype(jnp.float32)
    meansq = jnp.mean(wide * wide, axis=-1, keepdims=True)
    return (wide * lax.rsqrt(meansq + 1e-06) * gain.astype(jnp.float32)).astype(jnp.bfloat16)


def starts(lens, count):
    index = jnp.arange(count, dtype=jnp.int32)
    start, end = jnp.zeros((count,), jnp.int32), jnp.int32(0)
    for t in range(lens.shape[0]):
        end = end + lens[t]
        start = jnp.where(index >= end, end, start)
    return start


def rotated(v, cosine, sine):
    return (v * cosine + pltpu.roll(v, HEAD_DIM // 2, 1) * sine).astype(jnp.bfloat16)


def start_of(query_at, lens_ref):
    start, end = jnp.zeros_like(query_at), jnp.int32(0)
    for t in range(lens_ref.shape[1]):
        end = end + lens_ref[0, t]
        start = jnp.where(query_at >= end, end, start)
    return start


def attend_kernel(lens_ref, qkv_ref, out_ref):
    count = qkv_ref.shape[0]
    block = 128
    back = -(-(MOST - 1) // block)
    for at in range(count // block):
        first = max(0, at - back)
        wide = (at + 1 - first) * block
        rows = slice(at * block, (at + 1) * block)
        seen = slice(first * block, (at + 1) * block)
        query_at = at * block + lax.broadcasted_iota(jnp.int32, (block, 1), 0)
        key_at = first * block + lax.broadcasted_iota(jnp.int32, (block, wide), 1)
        start = start_of(query_at, lens_ref)
        low = jnp.maximum(query_at - (WINDOW - 1), start)
        allowed = jnp.logical_and(
            key_at <= query_at,
            jnp.logical_or(
                key_at >= low, jnp.logical_and(key_at >= start, key_at < start + SINKS)
            ),
        )
        query = jnp.concatenate(
            [qkv_ref[rows, h * HEAD_DIM : (h + 1) * HEAD_DIM] for h in range(GROUP)], axis=0
        )
        scores = lax.dot_general(
            query, qkv_ref[seen, GROUP * HEAD_DIM : (GROUP + 1) * HEAD_DIM],
            (((1,), (1,)), ((), ())), preferred_element_type=jnp.float32,
        ) * (1.0 / math.sqrt(HEAD_DIM))
        scores = jnp.where(allowed[None], scores.reshape(GROUP, block, wide), -1e30)
        peak = jnp.max(scores, axis=-1, keepdims=True)
        expo = jnp.exp(scores - peak)
        weights = (expo * (1.0 / jnp.sum(expo, axis=-1, keepdims=True))).astype(jnp.bfloat16)
        mixed = jnp.dot(
            weights.reshape(GROUP * block, wide), qkv_ref[seen, (GROUP + 1) * HEAD_DIM :],
            preferred_element_type=jnp.float32,
        ).astype(jnp.bfloat16)
        for h in range(GROUP):
            out_ref[rows, h * HEAD_DIM : (h + 1) * HEAD_DIM] = mixed[h * block : (h + 1) * block]


def attend_turned(qkv, lens):
    count = qkv.shape[0]
    vmem = pl.BlockSpec(memory_space=pltpu.VMEM)
    return pl.pallas_call(
        attend_kernel,
        out_shape=jax.ShapeDtypeStruct((count, GROUP * HEAD_DIM), jnp.bfloat16),
        in_specs=[pl.BlockSpec(memory_space=pltpu.SMEM), vmem],
        out_specs=vmem,
        compiler_params=pltpu.CompilerParams(vmem_limit_bytes=64 << 20),
        name="attention",
    )(lens, qkv)


CHUNKS = ((896, 1152), (0, 384), (384, 640), (640, 896))
OFF = 3
BLOCK = 128
PARTS = 4
UNITS, DIRECT = 8, 5


def serve_kernel(
    lens_hbm, gain_hbm, bias_hbm, w_hbm, tok_hbm, out_hbm,
    lens_ref, gain_ref, bias_ref, small_sem, wide_w, wb0, wb1, wb2, wb3, full0, full1, full2, full3,
    fullo, tok, tok2, normed, normed2, acco, acc0, acc1, acc2, acc3, qkv, kv2, cosine, sine, cosine2, sine2, mask, gains, ctx, side, line, sides,
    tok_sem, w_sem, line_send, line_recv, side_send, side_recv, first_send, first_recv,
    near_send, near_recv, far_send, far_recv, mate_send, mate_recv,
    tx_send, tx_recv, ty_send, ty_recv, tz_send, tz_recv, tv_send, tv_recv, tm_send, tm_recv,
    kx_send, kx_recv, kz_send, kz_recv, kv_send, kv_recv, out_send, out_recv, out_sem,
):
    f32, bf16 = jnp.float32, jnp.bfloat16
    wbs, fulls, accs = (wb0, wb1, wb2, wb3), (full0, full1, full2, full3), (acc0, acc1, acc2, acc3)
    number = len(CHUNKS)
    req, tp = lax.axis_index("req"), lax.axis_index("tp")
    z, x, y, c = req // 2, req % 2, tp // 2, tp % 2
    group, place, me = 2 * y + x, 2 * x + y, 4 * x + 2 * y + c
    count, depth = tok.shape
    shard = wide_w.shape[1]
    width = wide_w.shape[2]
    swapped = x != c
    middle = jnp.logical_or(z == 1, z == 2)
    end = jnp.logical_not(middle)
    pair = jnp.where(middle, 3 * (z // 2), 1 + z // 2)
    orders = (z, 1 + z % 2, 2 + z // 2 - 2 * (z % 2), 3 * (1 - z // 2))

    def device(at_z, at_x, at_y, at_c):
        return (2 * at_z + at_x, 2 * at_y + at_c)

    def flipped(m):
        fx, fy, fc = m // 4, m // 2 % 2, m % 2
        return (
            1 - x if fx else x,
            1 - y if fy else y,
            1 - c if fc else c,
        )

    def remote(source, to, send_sem, recv_sem, where):
        return pltpu.make_async_remote_copy(
            src_ref=source, dst_ref=to, send_sem=send_sem, recv_sem=recv_sem,
            device_id=where, device_id_type=MESH,
        )

    partner = device(z, 1 - x, y, 1 - c)
    mate = device(z, x, y, 1 - c)

    barrier = pltpu.get_barrier_semaphore()
    for m in range(1, 8):
        pl.semaphore_signal(barrier, inc=1, device_id=device(z, *flipped(m)), device_id_type=MESH)
    for dz in range(1, 4):
        pl.semaphore_signal(
            barrier, inc=1, device_id=device((z + dz) % 4, x, y, c), device_id_type=MESH
        )

    pl.semaphore_signal(
        barrier, inc=1, device_id=device(pair, 1 - x, y, 1 - c), device_id_type=MESH
    )

    smalls = [
        pltpu.make_async_copy(source, to, small_sem.at[k])
        for k, (source, to) in enumerate(
            ((gain_hbm, gain_ref), (bias_hbm, bias_ref), (lens_hbm, lens_ref))
        )
    ]
    for copy in smalls:
        copy.start()
    flips = ((0, 0), (1, 0), (0, 1), (1, 1))
    loads = []
    for k, (fx, fy) in enumerate(flips):
        g = 2 * (1 - y if fy else y) + (1 - x if fx else x)
        copy = pltpu.make_async_copy(
            w_hbm.at[:, pl.ds(pl.multiple_of(g * width, 128), width)], wide_w.at[k], w_sem.at[k]
        )
        copy.start()
        loads.append(copy)
    tok_copy = pltpu.make_async_copy(tok_hbm, tok, tok_sem)

    @pl.when(jnp.logical_not(swapped))
    def _():
        tok_copy.start()

    def rounded(v):
        return v.astype(bf16).astype(f32)

    for copy in smalls:
        copy.wait()
    side[...] = jnp.zeros_like(side)
    side[0:1, 0:shard] = rounded(gain_ref[...])
    side[1:2, :] = rounded(bias_ref[:, 0:128])
    side[2:3, 0 : width // 8 - 128] = rounded(bias_ref[:, 128:])
    side[3:4, 0 : lens_ref.shape[1]] = lens_ref[...].astype(f32)

    for i in range(4):
        loads[i].wait()
        if i:
            for k, (lo, hi) in enumerate(CHUNKS):
                wbs[k][i - 1] = wide_w[i, :, lo:hi].astype(bf16)
    pl.semaphore_wait(barrier, 11)
    lines = []
    for dz in range(1, 4):
        copy = remote(
            side, line.at[z], line_send.at[dz - 1], line_recv.at[dz - 1],
            device((z + dz) % 4, x, y, c),
        )
        copy.start()
        lines.append(copy)
    line[z] = side[...]

    def half(k, p):
        return fulls[k].at[p, :, c]

    def near(way, k, j):
        ref = fulls[k].at[z, j, c]
        return remote(
            ref, ref, near_send.at[way, k, j], near_recv.at[way, k, j],
            device(z - 1 + 2 * way, x, y, c),
        )

    def far(way, k, d):
        ref = half(k, z + (d - 1) * (1 - 2 * way))
        return remote(
            ref, ref, far_send.at[way, k, d - 2], far_recv.at[way, k, d - 2],
            device(z - 1 + 2 * way, x, y, c),
        )

    def sends(way, k):
        return z >= (2 if k == OFF else 1) if way == 0 else z <= (1 if k == OFF else 2)

    def start_near(k, j):
        for way in range(2):
            copy = near(way, k, j)

            @pl.when(sends(way, k))
            def _():
                copy.start()

    def row_unit(n):
        at = c + (1 - y) * 2 * n + y * 2 * (UNITS - 1 - n)
        size = count // 2 // UNITS
        return pl.ds(pl.multiple_of(at * size, size), size)

    def unit_z(n):
        at = row_unit(n)
        return remote(
            tok_hbm.at[at], tok2.at[at], tz_send.at[n], tz_recv.at[n], device(pair, x, y, c)
        )

    def unit_y(n):
        at = tok2.at[row_unit(n)]
        return remote(at, at, tv_send.at[n], tv_recv.at[n], device(z, x, 1 - y, c))

    def unit_mate(n):
        at = tok2.at[row_unit(n)]
        return remote(at, at, tm_send.at[n], tm_recv.at[n], mate)

    def start_units(*which):
        @pl.when(end)
        def _():
            for n in which:
                unit_z(n).start()

    for k, (lo, hi) in enumerate(CHUNKS):
        fulls[k][z, place, c] = wide_w[0, :, lo:hi].astype(bf16)
    start_near(OFF, place)
    start_near(0, place)
    start_units(0)

    @pl.when(middle)
    def _():
        for way in range(2):
            near(way, 1, place).start()

    firsts = {}
    for k in (OFF, 0, 1, 2):
        for i, (fx, fy) in enumerate(flips[1:]):
            copy = remote(
                wbs[k].at[i], fulls[k].at[z, place, c], first_send.at[k, i], first_recv.at[k, i],
                device(z, 1 - x if fx else x, 1 - y if fy else y, c),
            )
            copy.start()
            firsts[k, i] = copy

    def send_mate(k, p):
        ref = half(k, p)
        return remote(ref, ref, mate_send.at[k, p], mate_recv.at[k, p], mate)

    for copy in lines:
        copy.wait_recv()
    shares = []
    for m in range(1, 8):
        copy = remote(
            line, sides.at[me], side_send.at[m - 1], side_recv.at[m - 1], device(z, *flipped(m))
        )
        copy.start()
        shares.append(copy)
    sides[me] = line[...]

    rows = count // 2 // PARTS

    def part_rows(at_y, n):
        return pl.ds(pl.multiple_of(at_y * (count // 2) + n * rows, rows), rows)

    def tok_x(n):
        at = part_rows(y, n)
        return remote(tok_hbm.at[at], tok.at[at], tx_send.at[n], tx_recv.at[n], partner)

    def tok_y(n):
        at = tok.at[part_rows(y, n)]
        return remote(at, at, ty_send.at[n], ty_recv.at[n], device(z, x, 1 - y, c))

    def start_tokens(n):
        @pl.when(swapped)
        def _():
            tok_x(n).start()

    def forward(k, *which):
        for i in which:
            fx, fy = flips[i + 1]
            firsts[k, i].wait_recv()
            start_near(k, 2 * (1 - x if fx else x) + (1 - y if fy else y))

    def own_mate(k):
        if k != OFF:
            send_mate(k, z).start()
        else:

            @pl.when(middle)
            def _():
                send_mate(k, z).start()

    def start_end_near(k):
        @pl.when(end)
        def _():
            start_near(k, place)

    for k in (OFF, 0):
        forward(k, 0, 1, 2)
        own_mate(k)
    start_units(1)
    start_tokens(0)
    start_end_near(1)
    forward(1, 0, 1, 2)
    own_mate(1)
    start_units(2)
    start_near(2, place)
    forward(2, 0, 1, 2)
    own_mate(2)
    start_units(*range(3, DIRECT))
    start_tokens(1)

    for copy in shares:
        copy.wait_recv()

    def spread(piece, step, n, size):
        wide = jnp.concatenate(piece + [jnp.zeros((8, size - 128 * len(piece)), f32)], axis=1)
        return pltpu.roll(wide, step * n, 1) if n else wide

    for p in range(4):
        total = jnp.zeros((8, 8 * 128), f32)
        for n in range(8):
            total = total + spread([sides[n, p]], shard, n, 8 * 128)
        gains[p] = total[:, 0 : 8 * shard]

    def ends_of(lens):
        ends, last = [], jnp.zeros((1, 1), f32)
        for t in range(lens_ref.shape[1]):
            last = last + lens[3:4, t : t + 1]
            ends.append(last)
        return ends

    own_ends = ends_of(sides[4 * c + 2 * y + c, z])

    def start_at(query, ends):
        start = jnp.zeros_like(query)
        for e in ends:
            start = jnp.where(query >= e, e, start)
        return start

    def tables(cosine, sine, ends):
        query = lax.broadcasted_iota(jnp.int32, (count, 1), 0).astype(f32)
        pos = query - start_at(query, ends)
        lane = lax.broadcasted_iota(jnp.int32, (1, HEAD_DIM), 1)
        mid = HEAD_DIM // 2
        freqs = jnp.exp(-((lane % mid).astype(f32) * 2.0 / HEAD_DIM) * math.log(1000000.0))
        angle = pos * freqs
        cosine[...] = jnp.cos(angle)
        sine[...] = jnp.where(lane < mid, -1.0, 1.0) * jnp.sin(angle)

    back = -(-(MOST - 1) // BLOCK)

    def reach(at):
        first = max(0, at - back)
        return first, (at + 1 - first) * BLOCK

    def masks():
        for at in range(count // BLOCK):
            first, wide = reach(at)
            query = (at * BLOCK + lax.broadcasted_iota(jnp.int32, (BLOCK, 1), 0)).astype(f32)
            key = (first * BLOCK + lax.broadcasted_iota(jnp.int32, (BLOCK, wide), 1)).astype(f32)
            start = start_at(query, own_ends)
            low = jnp.maximum(query - (WINDOW - 1), start)
            allowed = jnp.logical_and(
                key <= query,
                jnp.logical_or(key >= low, jnp.logical_and(key >= start, key < start + SINKS)),
            )
            mask[at, :, 0:wide] = jnp.where(allowed, 0.0, -1e30)

    def normalise(tok, normed, first, many):
        @pl.loop(0, many // 32)
        def _(i):
            at = pl.ds(pl.multiple_of(first + i * 32, 32), 32)
            square = jnp.zeros((32, 8 * shard), f32)
            for p in range(4):
                wide = tok[at, p * 8 * shard : (p + 1) * 8 * shard].astype(f32)
                square = square + wide * wide
            mean = jnp.sum(square, axis=-1, keepdims=True) * (1.0 / depth)
            scale = lax.rsqrt(mean + 1e-06)
            for p in range(4):
                part = slice(p * 8 * shard, (p + 1) * 8 * shard)
                wide = tok[at, part].astype(f32)
                normed[at, part] = (wide * scale * gains[p, 0:1, :]).astype(bf16)

    def product(k, p):
        block = fulls[k][p].reshape(8 * shard, fulls[k].shape[-1])
        part = pl.ds(pl.multiple_of(p * 8 * shard, 128), 8 * shard)
        return jnp.dot(normed[:, part], block, preferred_element_type=f32)

    def whole(lhs, full):
        block = full[...].reshape(depth, full.shape[-1])
        return jnp.dot(lhs, block, preferred_element_type=f32)

    def some_rows(at_y):
        return pl.ds(pl.multiple_of(at_y * (count // 2), count // 2), count // 2)

    def take_mate(k, p):
        ref = fulls[k].at[p, :, 1 - c]
        remote(ref, ref, mate_send.at[k, p], mate_recv.at[k, p], mate).wait_recv()

    def add(k, n):
        p = orders[n]
        take_mate(k, p)
        if n == 0:
            accs[k][...] = product(k, p)
        else:
            accs[k][...] += product(k, p)

    def bias_line(group):
        total = jnp.zeros((8, width), f32)
        for n in range(8):
            both = sides[n, group]
            total = total + spread(
                [pltpu.roll(both, 7, 0), pltpu.roll(both, 6, 0)], width // 8, n, width
            )
        return total[0:1, :]

    def finish(k, sums, rows=slice(None)):
        lo, hi = CHUNKS[k]
        joined = sums + bias[:, lo:hi]
        for h in range(lo // HEAD_DIM, hi // HEAD_DIM):
            v = joined[:, h * HEAD_DIM - lo : (h + 1) * HEAD_DIM - lo]
            qkv[h, rows, :] = (
                rotated(v, cosine[rows, :], sine[rows, :]) if h <= GROUP else v.astype(bf16)
            )

    def chunk_end(k):
        if k == OFF:

            @pl.when(end)
            def _():
                kv_send_copy().wait_recv()

            return

        @pl.when(end)
        def _():
            add(k, 0)

        ends_get(1, k)
        ends_get(2, k)

        @pl.when(end)
        def _():
            add(k, 1)
            add(k, 2)

        ends_get(3, k)

        @pl.when(end)
        def _():
            p = orders[3]
            take_mate(k, p)
            finish(k, accs[k][...] + product(k, p))

    def chunk_middle(k, late):
        @pl.when(middle)
        def _():
            if k != OFF and not late:
                for n in range(4):
                    take_mate(k, orders[n])
            rows = some_rows(1 - y if late else y)
            finish(k, whole(normed[rows, :], fulls[k]), rows)

    def out_at(k):
        lo, hi = CHUNKS[k]
        return ctx.at[:, pl.ds(lo, hi - lo)], out_hbm.at[:, pl.ds(lo, hi - lo)]

    def out_remote(k):
        source, to = out_at(k)
        return remote(source, to, out_send.at[k - 1], out_recv.at[k - 1], partner)

    def out_local(k):
        source, to = out_at(k)
        return pltpu.make_async_copy(source, to, out_sem.at[k - 1])

    def attend(k):
        lo, hi = CHUNKS[k]
        heads = range(lo // HEAD_DIM, hi // HEAD_DIM)
        many = len(heads)
        for at in range(count // BLOCK):
            first, wide = reach(at)
            here = slice(at * BLOCK, (at + 1) * BLOCK)
            seen = slice(first * BLOCK, (at + 1) * BLOCK)
            query = jnp.concatenate([qkv[h, here, :] for h in heads], axis=0)
            scores = lax.dot_general(
                query, qkv[GROUP, seen, :], (((1,), (1,)), ((), ())), preferred_element_type=f32
            ) * (1.0 / math.sqrt(HEAD_DIM))
            scores = scores.reshape(many, BLOCK, wide) + mask[at, :, 0:wide][None]
            peak = jnp.max(scores, axis=-1, keepdims=True)
            expo = jnp.exp(scores - peak)
            weights = (expo * (1.0 / jnp.sum(expo, axis=-1, keepdims=True))).astype(bf16)
            mixed = jnp.dot(
                weights.reshape(many * BLOCK, wide), qkv[GROUP + 1, seen, :],
                preferred_element_type=f32,
            ).astype(bf16)
            for n, h in enumerate(heads):
                ctx[here, h * HEAD_DIM : (h + 1) * HEAD_DIM] = mixed[n * BLOCK : (n + 1) * BLOCK]

        @pl.when(swapped)
        def _():
            out_remote(k).start()

        @pl.when(jnp.logical_not(swapped))
        def _():
            out_local(k).start()

    def receive(who, d, k):
        for way in range(2):
            p = z + d * (1 - 2 * way)

            @pl.when(z == ((1, 2, 0), (2, 1, 3))[way][who])
            def _():
                if d == 1:
                    for j in range(4):
                        ref = fulls[k].at[p, j, c]
                        remote(
                            ref, ref, near_send.at[way, k, j], near_recv.at[way, k, j], mate
                        ).wait_recv()
                else:
                    ref = half(k, p)
                    remote(
                        ref, ref, far_send.at[way, k, d - 2], far_recv.at[way, k, d - 2], mate
                    ).wait_recv()
                if who == 1 or (who == 0 and k != OFF):
                    far(way, k, d + 1).start()
                send_mate(k, p).start()

    def inner(d, k):
        receive(0, d, k)

    def outer(d, k):
        receive(1, d, k)

    def ends_get(d, k):
        receive(2, d, k)

    def take_unit(n):
        @pl.when(middle)
        def _():
            unit_z(n).wait_recv()
            if n < UNITS - DIRECT:
                unit_y(n).start()
            unit_mate(n).start()

    def take_side(n):
        @pl.when(middle)
        def _():
            at = tok2.at[row_unit(UNITS - 1 - n)]
            remote(at, at, tv_send.at[n], tv_recv.at[n], mate).wait_recv()
            unit_mate(UNITS - 1 - n).start()

    def unit_norm(n):
        @pl.when(middle)
        def _():
            at = c + (1 - y) * 2 * n + y * 2 * (UNITS - 1 - n) + 1 - 2 * c
            size = count // 2 // UNITS
            ref = tok2.at[pl.ds(pl.multiple_of(at * size, size), size)]
            remote(ref, ref, tm_send.at[n], tm_recv.at[n], mate).wait_recv()
            first = ((1 - y) * n + y * (UNITS - 1 - n)) * 2 * size
            normalise(tok2, normed2, first, 2 * size)

    both_mid = jnp.logical_and(middle, swapped)
    kx_planes = (0, 2, 3)

    def other_x(i):
        p = orders[kx_planes[i]]
        return remote(fulls[OFF].at[p], fullo.at[p], kx_send.at[i], kx_recv.at[i], partner)

    def other_z(n):
        ref = fullo.at[orders[n]]
        return remote(ref, ref, kz_send.at[0], kz_recv.at[0], device(3 - z, x, y, c))

    def give_other(n):
        @pl.when(middle)
        def _():
            take_mate(OFF, orders[n])
        if n in kx_planes:
            @pl.when(both_mid)
            def _():
                other_x(kx_planes.index(n)).start()

    def take_other(i):
        @pl.when(both_mid)
        def _():
            other_x(i).wait_recv()
            if i == 0:
                other_z(0).start()

    def last_others():
        @pl.when(both_mid)
        def _():
            other_z(1).wait_recv()

    def kv_send_copy():
        return remote(
            kv2, qkv.at[pl.ds(CHUNKS[OFF][0] // HEAD_DIM, 2)], kv_send.at[0], kv_recv.at[0], device(pair, c, y, x)
        )

    def serve_end():
        def sums(full):
            acco[...] = whole(normed2[...], full)

        @pl.when(swapped)
        def _():
            sums(fullo)

        @pl.when(jnp.logical_not(swapped))
        def _():
            sums(fulls[OFF])

        lo, hi = CHUNKS[OFF]
        joined = acco[...] + bias_line(2 * y + c)[:, lo:hi]
        for h in range(2):
            v = joined[:, h * HEAD_DIM : (h + 1) * HEAD_DIM]
            kv2[h] = rotated(v, cosine2[...], sine2[...])
        kv_send_copy().start()

    def pass_tokens(n):
        @pl.when(swapped)
        def _():
            tok_x(n).wait_recv()
            tok_y(n).start()
            normalise(tok, normed, y * (count // 2) + n * rows, rows)

    def tokens_y(n):
        @pl.when(swapped)
        def _():
            at = tok.at[part_rows(1 - y, n)]
            remote(at, at, ty_send.at[n], ty_recv.at[n], mate).wait_recv()
            normalise(tok, normed, (1 - y) * (count // 2) + n * rows, rows)

    bias = bias_line(group)
    take_unit(0)
    inner(1, OFF)
    give_other(0)
    start_tokens(2)
    start_tokens(3)
    pass_tokens(0)
    inner(1, 0)
    outer(1, OFF)
    outer(1, 0)
    take_unit(1)
    unit_norm(0)
    inner(1, 1)
    pass_tokens(1)
    inner(1, 2)
    give_other(2)

    @pl.when(jnp.logical_not(swapped))
    def _():
        tok_copy.wait()
        normalise(tok, normed, 0, count)

    inner(2, OFF)
    outer(1, 1)
    give_other(1)
    give_other(3)
    take_side(0)
    take_unit(2)
    take_other(0)
    unit_norm(1)
    tables(cosine, sine, own_ends)
    masks()
    pass_tokens(2)
    inner(2, 0)
    unit_norm(UNITS - 1)
    tokens_y(0)

    @pl.when(middle)
    def _():
        tables(cosine2, sine2, ends_of(sides[me, pair]))

    outer(1, 2)
    pass_tokens(3)
    unit_norm(2)
    take_side(1)
    inner(2, 1)
    unit_norm(UNITS - 2)
    tokens_y(1)
    take_unit(3)
    chunk_middle(0, False)
    chunk_middle(OFF, False)
    unit_norm(3)
    chunk_middle(1, False)
    for n in range(4, DIRECT):
        take_unit(n)
    take_other(1)
    take_side(2)
    tokens_y(2)
    unit_norm(UNITS - 3)
    inner(2, 2)
    tokens_y(3)
    chunk_end(0)
    chunk_middle(0, True)
    chunk_middle(1, True)
    unit_norm(4)
    take_other(2)
    last_others()
    pl.when(middle)(serve_end)
    for k in range(1, number):
        chunk_end(k)
        if k == 2:
            chunk_middle(k, False)
        if k > 1:
            chunk_middle(k, True)
        attend(k)

    @pl.when(swapped)
    def _():
        for k in range(1, number):
            out_remote(k).wait_recv()
        for k in range(1, number):
            out_remote(k).wait_send()
        for n in range(PARTS):
            tok_x(n).wait_send()
            tok_y(n).wait_send()

    @pl.when(jnp.logical_not(swapped))
    def _():
        for k in range(1, number):
            out_local(k).wait()

    for copy in lines + shares + list(firsts.values()):
        copy.wait_send()
    for k in range(number):
        def mates():
            for p in range(4):
                send_mate(k, p).wait_send()

        if k != OFF:
            mates()
        else:
            pl.when(middle)(mates)
        for way in range(2):
            @pl.when(sends(way, k))
            def _():
                for j in range(4):
                    near(way, k, j).wait_send()

            @pl.when(z == 2 - way if k == OFF else middle)
            def _():
                far(way, k, 2).wait_send()

            if k != OFF:
                @pl.when(z == 1 + way)
                def _():
                    far(way, k, 3).wait_send()

    @pl.when(end)
    def _():
        for n in range(DIRECT):
            unit_z(n).wait_send()

    @pl.when(middle)
    def _():
        for n in range(UNITS - DIRECT):
            unit_y(n).wait_send()
        for n in range(UNITS):
            unit_mate(n).wait_send()
        kv_send_copy().wait_send()

    @pl.when(both_mid)
    def _():
        for i in range(len(kx_planes)):
            other_x(i).wait_send()
        other_z(0).wait_send()


def serve(tokens, norm_gain, qkv_weight, qkv_bias, lens):
    count, depth = tokens.shape
    shard, columns = qkv_weight.shape
    width = columns // 4
    sizes = [hi - lo for lo, hi in CHUNKS]
    number, blocks = len(sizes), count // BLOCK
    hbm = pl.BlockSpec(memory_space=pltpu.HBM)
    dma, vmem = pltpu.SemaphoreType.DMA, pltpu.VMEM
    f32, bf16 = jnp.float32, jnp.bfloat16
    two = lambda *shape: [dma(shape), dma(shape)]
    return pl.pallas_call(
        serve_kernel,
        out_shape=jax.ShapeDtypeStruct((count, GROUP * HEAD_DIM), bf16),
        in_specs=[hbm] * 5,
        out_specs=hbm,
        scratch_shapes=[
            vmem(lens.shape, jnp.int32),
            vmem((1, shard), f32),
            vmem((1, columns // 32), f32),
            dma((3,)),
            vmem((4, shard, width), f32),
            *[vmem((3, shard, size), bf16) for size in sizes],
            *[vmem((4, 4, 2, shard, size), bf16) for size in sizes],
            vmem((4, 4, 2, shard, sizes[OFF]), bf16),
            vmem((count, depth), bf16),
            vmem((count, depth), bf16),
            vmem((count, depth), bf16),
            vmem((count, depth), bf16),
            vmem((count, sizes[OFF]), f32),
            *[vmem((count, size), f32) for size in sizes],
            vmem((GROUP + 2, count, HEAD_DIM), bf16),
            vmem((2, count, HEAD_DIM), bf16),
            *[vmem((count, HEAD_DIM), f32)] * 4,
            vmem((blocks, BLOCK, 3 * BLOCK), f32),
            vmem((4, 8, 8 * shard), f32),
            vmem((count, GROUP * HEAD_DIM), bf16),
            vmem((8, 128), f32),
            vmem((4, 8, 128), f32),
            vmem((8, 4, 8, 128), f32),
            dma, dma((4,)),
            *two(3), *two(7), *two(number, 3),
            *two(2, number, 4), *two(2, number, 2), *two(number, 4),
            *two(PARTS), *two(PARTS), *two(DIRECT), *two(UNITS - DIRECT), *two(UNITS),
            *two(3), *two(1), *two(1), *two(number - 1), dma((number - 1,)),
        ],
        compiler_params=pltpu.CompilerParams(
            collective_id=0, has_side_effects=True, vmem_limit_bytes=60 << 20
        ),
        name="serve",
    )(lens, norm_gain.reshape(1, shard), qkv_bias.reshape(1, -1), qkv_weight, tokens)


def turn_plain(joined, lens):
    count = joined.shape[0]
    half = HEAD_DIM // 2
    pos = jnp.arange(count, dtype=jnp.int32) - starts(lens, count)
    freqs = jnp.exp(-(jnp.arange(half, dtype=jnp.float32) * 2.0 / HEAD_DIM) * math.log(1000000.0))
    angle = pos.astype(jnp.float32)[:, None] * freqs[None, :]
    cosine = jnp.tile(jnp.cos(angle), (1, 2))[:, None, :]
    sine = jnp.tile(jnp.sin(angle), (1, 2))[:, None, :]
    heads = joined.reshape(count, GROUP + 2, HEAD_DIM)
    spun = jnp.concatenate([-heads[..., half:], heads[..., :half]], axis=-1)
    turned = (heads * cosine + spun * sine)[:, : GROUP + 1]
    both = jnp.concatenate([turned, heads[:, GROUP + 1 :]], axis=1)
    return both.reshape(count, -1).astype(jnp.bfloat16)


def project_plain(tokens, norm_gain, qkv_weight, qkv_bias):
    tp_count = lax.axis_size("tp")
    req_count = lax.axis_size("req")
    tp_place = lax.axis_index("tp")
    gain_full, bias_full = (
        lax.all_gather(norm_gain.astype(jnp.bfloat16), ("req", "tp"), axis=0, tiled=True),
        lax.all_gather(qkv_bias.astype(jnp.bfloat16), ("req", "tp"), axis=0, tiled=True),
    )
    width = bias_full.shape[0] // tp_count
    bias_block = lax.dynamic_slice_in_dim(bias_full, tp_place * width, width).astype(jnp.float32)
    normed = normalize(tokens, gain_full)
    weight_b = qkv_weight.astype(jnp.bfloat16)
    count = tokens.shape[0]
    gathered = lax.all_gather(weight_b, "req", axis=0, tiled=True)
    regrouped = lax.all_to_all(gathered, "tp", split_axis=1, concat_axis=0, tiled=True)
    shard_rows = weight_b.shape[0]
    reordered = (
        normed.reshape(count, req_count, tp_count, shard_rows)
        .transpose(0, 2, 1, 3)
        .reshape(count, -1)
    )
    joined = jnp.dot(reordered, regrouped, preferred_element_type=jnp.float32)
    return joined + bias_block[None, :]


def shards(small, tokens, norm_gain, qkv_weight, qkv_bias, lengths):
    if small:
        return serve(tokens, norm_gain, qkv_weight, qkv_bias, lengths)
    qkv = turn_plain(project_plain(tokens, norm_gain, qkv_weight, qkv_bias), lengths[0])
    return attend_turned(qkv, lengths)


def solution(mesh):
    placed = (
        P("req", None),
        P(("req", "tp")),
        P(("req", "tp"), None),
        P(("req", "tp")),
        P("req", None),
    )
    small = mesh.shape["req"] == 8 and mesh.shape["tp"] == 4
    return jax.shard_map(
        functools.partial(shards, small),
        mesh=mesh, in_specs=placed, out_specs=P("req", "tp"), check_vma=False,
    )
```

```python
import functools
import math

import jax
import jax.numpy as jnp
from jax import lax
from jax.experimental import pallas as pl
from jax.experimental.pallas import tpu as pltpu
from jax.sharding import PartitionSpec as P

HEAD_DIM = 128
SINKS = 4
GROUP = 7
WINDOW = 160
MOST = 256
MESH = pl.DeviceIdType.MESH


def normalize(values, gain):
    wide = values.astype(jnp.float32)
    meansq = jnp.mean(wide * wide, axis=-1, keepdims=True)
    return (wide * lax.rsqrt(meansq + 1e-06) * gain.astype(jnp.float32)).astype(jnp.bfloat16)


def starts(lens, count):
    index = jnp.arange(count, dtype=jnp.int32)
    start, end = jnp.zeros((count,), jnp.int32), jnp.int32(0)
    for t in range(lens.shape[0]):
        end = end + lens[t]
        start = jnp.where(index >= end, end, start)
    return start


def rotated(v, cosine, sine):
    return (v * cosine + pltpu.roll(v, HEAD_DIM // 2, 1) * sine).astype(jnp.bfloat16)


def start_of(query_at, lens_ref):
    start, end = jnp.zeros_like(query_at), jnp.int32(0)
    for t in range(lens_ref.shape[1]):
        end = end + lens_ref[0, t]
        start = jnp.where(query_at >= end, end, start)
    return start


def attend_kernel(lens_ref, qkv_ref, out_ref):
    count = qkv_ref.shape[0]
    block = 128
    back = -(-(MOST - 1) // block)
    for at in range(count // block):
        first = max(0, at - back)
        wide = (at + 1 - first) * block
        rows = slice(at * block, (at + 1) * block)
        seen = slice(first * block, (at + 1) * block)
        query_at = at * block + lax.broadcasted_iota(jnp.int32, (block, 1), 0)
        key_at = first * block + lax.broadcasted_iota(jnp.int32, (block, wide), 1)
        start = start_of(query_at, lens_ref)
        low = jnp.maximum(query_at - (WINDOW - 1), start)
        allowed = jnp.logical_and(
            key_at <= query_at,
            jnp.logical_or(
                key_at >= low, jnp.logical_and(key_at >= start, key_at < start + SINKS)
            ),
        )
        query = jnp.concatenate(
            [qkv_ref[rows, h * HEAD_DIM : (h + 1) * HEAD_DIM] for h in range(GROUP)], axis=0
        )
        scores = lax.dot_general(
            query, qkv_ref[seen, GROUP * HEAD_DIM : (GROUP + 1) * HEAD_DIM],
            (((1,), (1,)), ((), ())), preferred_element_type=jnp.float32,
        ) * (1.0 / math.sqrt(HEAD_DIM))
        scores = jnp.where(allowed[None], scores.reshape(GROUP, block, wide), -1e30)
        peak = jnp.max(scores, axis=-1, keepdims=True)
        expo = jnp.exp(scores - peak)
        weights = (expo * (1.0 / jnp.sum(expo, axis=-1, keepdims=True))).astype(jnp.bfloat16)
        mixed = jnp.dot(
            weights.reshape(GROUP * block, wide), qkv_ref[seen, (GROUP + 1) * HEAD_DIM :],
            preferred_element_type=jnp.float32,
        ).astype(jnp.bfloat16)
        for h in range(GROUP):
            out_ref[rows, h * HEAD_DIM : (h + 1) * HEAD_DIM] = mixed[h * block : (h + 1) * block]


def attend_turned(qkv, lens):
    count = qkv.shape[0]
    vmem = pl.BlockSpec(memory_space=pltpu.VMEM)
    return pl.pallas_call(
        attend_kernel,
        out_shape=jax.ShapeDtypeStruct((count, GROUP * HEAD_DIM), jnp.bfloat16),
        in_specs=[pl.BlockSpec(memory_space=pltpu.SMEM), vmem],
        out_specs=vmem,
        compiler_params=pltpu.CompilerParams(vmem_limit_bytes=64 << 20),
        name="attention",
    )(lens, qkv)


CHUNKS = ((896, 1152), (0, 384), (384, 640), (640, 896))
OFF = 3
BLOCK = 128
PARTS = 4
UNITS, DIRECT = 8, 5


def serve_kernel(
    lens_hbm, gain_hbm, bias_hbm, w_hbm, tok_hbm, out_hbm,
    lens_ref, gain_ref, bias_ref, small_sem, wide_w, wb0, wb1, wb2, wb3, full0, full1, full2, full3,
    fullo, tok, tok2, normed, normed2, acco, acc0, acc1, acc2, acc3, qkv, kv2, kv3, cosine, sine, cosine2, sine2, mask, gains, ctx, side, line, sides,
    tok_sem, w_sem, line_send, line_recv, side_send, side_recv, first_send, first_recv,
    near_send, near_recv, far_send, far_recv, mate_send, mate_recv,
    tx_send, tx_recv, ty_send, ty_recv, tz_send, tz_recv, tv_send, tv_recv, tm_send, tm_recv,
    kx_send, kx_recv, kz_send, kz_recv, kv_send, kv_recv, kp_send, kp_recv, out_send, out_recv, out_sem,
):
    f32, bf16 = jnp.float32, jnp.bfloat16
    wbs, fulls, accs = (wb0, wb1, wb2, wb3), (full0, full1, full2, full3), (acc0, acc1, acc2, acc3)
    number = len(CHUNKS)
    req, tp = lax.axis_index("req"), lax.axis_index("tp")
    z, x, y, c = req // 2, req % 2, tp // 2, tp % 2
    group, place, me = 2 * y + x, 2 * x + y, 4 * x + 2 * y + c
    count, depth = tok.shape
    shard = wide_w.shape[1]
    width = wide_w.shape[2]
    swapped = x != c
    middle = jnp.logical_or(z == 1, z == 2)
    end = jnp.logical_not(middle)
    pair = jnp.where(middle, 3 * (z // 2), 1 + z // 2)
    orders = (z, 1 + z % 2, 2 + z // 2 - 2 * (z % 2), 3 * (1 - z // 2))

    def device(at_z, at_x, at_y, at_c):
        return (2 * at_z + at_x, 2 * at_y + at_c)

    def flipped(m):
        fx, fy, fc = m // 4, m // 2 % 2, m % 2
        return (
            1 - x if fx else x,
            1 - y if fy else y,
            1 - c if fc else c,
        )

    def remote(source, to, send_sem, recv_sem, where):
        return pltpu.make_async_remote_copy(
            src_ref=source, dst_ref=to, send_sem=send_sem, recv_sem=recv_sem,
            device_id=where, device_id_type=MESH,
        )

    partner = device(z, 1 - x, y, 1 - c)
    mate = device(z, x, y, 1 - c)

    barrier = pltpu.get_barrier_semaphore()
    for m in range(1, 8):
        pl.semaphore_signal(barrier, inc=1, device_id=device(z, *flipped(m)), device_id_type=MESH)
    for dz in range(1, 4):
        pl.semaphore_signal(
            barrier, inc=1, device_id=device((z + dz) % 4, x, y, c), device_id_type=MESH
        )

    smalls = [
        pltpu.make_async_copy(source, to, small_sem.at[k])
        for k, (source, to) in enumerate(
            ((gain_hbm, gain_ref), (bias_hbm, bias_ref), (lens_hbm, lens_ref))
        )
    ]
    for copy in smalls:
        copy.start()
    flips = ((0, 0), (1, 0), (0, 1), (1, 1))
    loads = []
    for k, (fx, fy) in enumerate(flips):
        g = 2 * (1 - y if fy else y) + (1 - x if fx else x)
        copy = pltpu.make_async_copy(
            w_hbm.at[:, pl.ds(pl.multiple_of(g * width, 128), width)], wide_w.at[k], w_sem.at[k]
        )
        copy.start()
        loads.append(copy)
    tok_copy = pltpu.make_async_copy(tok_hbm, tok, tok_sem)

    @pl.when(jnp.logical_not(swapped))
    def _():
        tok_copy.start()

    def rounded(v):
        return v.astype(bf16).astype(f32)

    for copy in smalls:
        copy.wait()
    side[...] = jnp.zeros_like(side)
    side[0:1, 0:shard] = rounded(gain_ref[...])
    side[1:2, :] = rounded(bias_ref[:, 0:128])
    side[2:3, 0 : width // 8 - 128] = rounded(bias_ref[:, 128:])
    side[3:4, 0 : lens_ref.shape[1]] = lens_ref[...].astype(f32)

    for i in range(4):
        loads[i].wait()
        if i:
            for k, (lo, hi) in enumerate(CHUNKS):
                wbs[k][i - 1] = wide_w[i, :, lo:hi].astype(bf16)
    pl.semaphore_wait(barrier, 10)
    for dz in range(1, 4):
        copy = remote(
            side, line.at[z], line_send.at[0], line_recv.at[0], device((z + dz) % 4, x, y, c)
        )
        copy.start()
    ref = line.at[pl.ds(0, 3)]
    whole_line = remote(ref, ref, line_send.at[0], line_recv.at[0], mate)
    line[z] = side[...]

    def half(k, p):
        return fulls[k].at[p, :, c]

    def near(way, k, j):
        ref = fulls[k].at[z, j, c]
        return remote(
            ref, ref, near_send.at[way, k], near_recv.at[way, k],
            device(z - 1 + 2 * way, x, y, c),
        )

    def far(way, k, d):
        ref = half(k, z + (d - 1) * (1 - 2 * way))
        return remote(
            ref, ref, far_send.at[way, k, d - 2], far_recv.at[way, k, d - 2],
            device(z - 1 + 2 * way, x, y, c),
        )

    def sends(way, k):
        return z >= (2 if k == OFF else 1) if way == 0 else z <= (1 if k == OFF else 2)

    def start_near(k, j):
        for way in range(2):
            copy = near(way, k, j)

            @pl.when(sends(way, k))
            def _():
                copy.start()

    def row_unit(n):
        at = c + (1 - y) * 2 * n + y * 2 * (UNITS - 1 - n)
        size = count // 2 // UNITS
        return pl.ds(pl.multiple_of(at * size, size), size)

    def unit_z(n):
        at = row_unit(n)
        return remote(
            tok_hbm.at[at], tok2.at[at], tz_send.at[0], tz_recv.at[n], device(pair, x, y, c)
        )

    def unit_y(n):
        at = tok2.at[row_unit(n)]
        return remote(at, at, tv_send.at[0], tv_recv.at[n], device(z, x, 1 - y, c))

    def unit_mate(n):
        at = tok2.at[row_unit(n)]
        return remote(at, at, tm_send.at[0], tm_recv.at[n], mate)

    unit_rows = count // 2 // UNITS

    def sent(many, send_sem, recv_sem):
        ref = tok.at[pl.ds(0, many)]
        remote(ref, ref, send_sem.at[0], recv_sem.at[0], mate).wait_send()

    def start_units(*which):
        @pl.when(end)
        def _():
            for n in which:
                unit_z(n).start()

    for k, (lo, hi) in enumerate(CHUNKS):
        fulls[k][z, place, c] = wide_w[0, :, lo:hi].astype(bf16)
    start_near(OFF, place)
    start_near(0, place)
    start_units(0)

    @pl.when(middle)
    def _():
        for way in range(2):
            near(way, 1, place).start()

    firsts = {}
    for k in (OFF, 0, 1, 2):
        for i, (fx, fy) in enumerate(flips[1:]):
            copy = remote(
                wbs[k].at[i], fulls[k].at[z, place, c], first_send.at[k], first_recv.at[k, i],
                device(z, 1 - x if fx else x, 1 - y if fy else y, c),
            )
            copy.start()
            firsts[k, i] = copy

    def send_mate(k, p):
        ref = half(k, p)
        return remote(ref, ref, mate_send.at[k], mate_recv.at[k, p], mate)

    whole_line.wait_recv()
    for m in range(1, 8):
        copy = remote(
            line, sides.at[me], side_send.at[0], side_recv.at[0], device(z, *flipped(m))
        )
        copy.start()
    ref = sides.at[pl.ds(0, 7)]
    whole_sides = remote(ref, ref, side_send.at[0], side_recv.at[0], mate)
    sides[me] = line[...]

    rows = count // 2 // PARTS

    def part_rows(at_y, n):
        return pl.ds(pl.multiple_of(at_y * (count // 2) + n * rows, rows), rows)

    def tok_x(n):
        at = part_rows(y, n)
        return remote(tok_hbm.at[at], tok.at[at], tx_send.at[0], tx_recv.at[n], partner)

    def tok_y(n):
        at = tok.at[part_rows(y, n)]
        return remote(at, at, ty_send.at[0], ty_recv.at[n], device(z, x, 1 - y, c))

    def start_tokens(n):
        @pl.when(swapped)
        def _():
            tok_x(n).start()

    def forward(k, *which):
        for i in which:
            fx, fy = flips[i + 1]
            firsts[k, i].wait_recv()
            start_near(k, 2 * (1 - x if fx else x) + (1 - y if fy else y))

    def own_mate(k):
        if k != OFF:
            send_mate(k, z).start()
        else:

            @pl.when(middle)
            def _():
                send_mate(k, z).start()

    def start_end_near(k):
        @pl.when(end)
        def _():
            start_near(k, place)

    for k in (OFF, 0):
        forward(k, 0, 1, 2)
        own_mate(k)
    start_units(1)
    start_tokens(0)
    start_end_near(1)
    forward(1, 0, 1, 2)
    own_mate(1)
    start_units(2)
    start_near(2, place)
    forward(2, 0, 1, 2)
    own_mate(2)
    start_units(*range(3, DIRECT))
    start_tokens(1)

    whole_sides.wait_recv()

    def spread(piece, step, n, size):
        wide = jnp.concatenate(piece + [jnp.zeros((8, size - 128 * len(piece)), f32)], axis=1)
        return pltpu.roll(wide, step * n, 1) if n else wide

    for p in range(4):
        total = jnp.zeros((8, 8 * 128), f32)
        for n in range(8):
            total = total + spread([sides[n, p]], shard, n, 8 * 128)
        gains[p] = total[:, 0 : 8 * shard]

    def ends_of(lens):
        ends, last = [], jnp.zeros((1, 1), f32)
        for t in range(lens_ref.shape[1]):
            last = last + lens[3:4, t : t + 1]
            ends.append(last)
        return ends

    own_ends = ends_of(sides[4 * c + 2 * y + c, z])

    def start_at(query, ends):
        start = jnp.zeros_like(query)
        for e in ends:
            start = jnp.where(query >= e, e, start)
        return start

    def tables(cosine, sine, ends):
        query = lax.broadcasted_iota(jnp.int32, (count, 1), 0).astype(f32)
        pos = query - start_at(query, ends)
        lane = lax.broadcasted_iota(jnp.int32, (1, HEAD_DIM), 1)
        mid = HEAD_DIM // 2
        freqs = jnp.exp(-((lane % mid).astype(f32) * 2.0 / HEAD_DIM) * math.log(1000000.0))
        angle = pos * freqs
        cosine[...] = jnp.cos(angle)
        sine[...] = jnp.where(lane < mid, -1.0, 1.0) * jnp.sin(angle)

    back = -(-(MOST - 1) // BLOCK)

    def reach(at):
        first = max(0, at - back)
        return first, (at + 1 - first) * BLOCK

    def masks():
        for at in range(count // BLOCK):
            first, wide = reach(at)
            query = (at * BLOCK + lax.broadcasted_iota(jnp.int32, (BLOCK, 1), 0)).astype(f32)
            key = (first * BLOCK + lax.broadcasted_iota(jnp.int32, (BLOCK, wide), 1)).astype(f32)
            start = start_at(query, own_ends)
            low = jnp.maximum(query - (WINDOW - 1), start)
            allowed = jnp.logical_and(
                key <= query,
                jnp.logical_or(key >= low, jnp.logical_and(key >= start, key < start + SINKS)),
            )
            mask[at, :, 0:wide] = jnp.where(allowed, 0.0, -1e30)

    def normalise(tok, normed, first, many):
        @pl.loop(0, many // 32)
        def _(i):
            at = pl.ds(pl.multiple_of(first + i * 32, 32), 32)
            square = jnp.zeros((32, 8 * shard), f32)
            for p in range(4):
                wide = tok[at, p * 8 * shard : (p + 1) * 8 * shard].astype(f32)
                square = square + wide * wide
            mean = jnp.sum(square, axis=-1, keepdims=True) * (1.0 / depth)
            scale = lax.rsqrt(mean + 1e-06)
            for p in range(4):
                part = slice(p * 8 * shard, (p + 1) * 8 * shard)
                wide = tok[at, part].astype(f32)
                normed[at, part] = (wide * scale * gains[p, 0:1, :]).astype(bf16)

    def product(k, p):
        block = fulls[k][p].reshape(8 * shard, fulls[k].shape[-1])
        part = pl.ds(pl.multiple_of(p * 8 * shard, 128), 8 * shard)
        return jnp.dot(normed[:, part], block, preferred_element_type=f32)

    def whole(lhs, full):
        block = full[...].reshape(depth, full.shape[-1])
        return jnp.dot(lhs, block, preferred_element_type=f32)

    def some_rows(at_y):
        return pl.ds(pl.multiple_of(at_y * (count // 2), count // 2), count // 2)

    def take_mate(k, p):
        ref = fulls[k].at[p, :, 1 - c]
        remote(ref, ref, mate_send.at[k], mate_recv.at[k, p], mate).wait_recv()

    def add(k, n):
        p = orders[n]
        take_mate(k, p)
        if n == 0:
            accs[k][...] = product(k, p)
        else:
            accs[k][...] += product(k, p)

    def bias_line(group):
        total = jnp.zeros((8, width), f32)
        for n in range(8):
            both = sides[n, group]
            total = total + spread(
                [pltpu.roll(both, 7, 0), pltpu.roll(both, 6, 0)], width // 8, n, width
            )
        return total[0:1, :]

    def finish(k, sums, rows=slice(None)):
        lo, hi = CHUNKS[k]
        joined = sums + bias[:, lo:hi]
        for h in range(lo // HEAD_DIM, hi // HEAD_DIM):
            v = joined[:, h * HEAD_DIM - lo : (h + 1) * HEAD_DIM - lo]
            qkv[h, rows, :] = (
                rotated(v, cosine[rows, :], sine[rows, :]) if h <= GROUP else v.astype(bf16)
            )

    def chunk_end(k):
        if k == OFF:

            @pl.when(end)
            def _():
                give_heads(kv2).wait_recv()

            return

        @pl.when(end)
        def _():
            add(k, 0)

        ends_get(1, k)
        ends_get(2, k)

        @pl.when(end)
        def _():
            add(k, 1)
            add(k, 2)

        ends_get(3, k)

        @pl.when(end)
        def _():
            p = orders[3]
            take_mate(k, p)
            finish(k, accs[k][...] + product(k, p))

    def chunk_middle(k, late):
        @pl.when(middle)
        def _():
            if k != OFF and not late:
                for n in range(4):
                    take_mate(k, orders[n])
            rows = some_rows(1 - y if late else y)
            finish(k, whole(normed[rows, :], fulls[k]), rows)

    def out_at(k, part):
        lo, hi = CHUNKS[k]
        where = (pl.ds(part * (count // 2), count // 2), pl.ds(lo, hi - lo))
        return ctx.at[where], out_hbm.at[where]

    def out_remote(k, part):
        source, to = out_at(k, part)
        return remote(source, to, out_send.at[0], out_recv.at[0], partner)

    def out_local(k, part):
        source, to = out_at(k, part)
        return pltpu.make_async_copy(source, to, out_sem)

    def attend(k):
        lo, hi = CHUNKS[k]
        heads = range(lo // HEAD_DIM, hi // HEAD_DIM)
        many = len(heads)
        for at in range(count // BLOCK):
            first, wide = reach(at)
            here = slice(at * BLOCK, (at + 1) * BLOCK)
            seen = slice(first * BLOCK, (at + 1) * BLOCK)
            query = jnp.concatenate([qkv[h, here, :] for h in heads], axis=0)
            scores = lax.dot_general(
                query, qkv[GROUP, seen, :], (((1,), (1,)), ((), ())), preferred_element_type=f32
            ) * (1.0 / math.sqrt(HEAD_DIM))
            scores = scores.reshape(many, BLOCK, wide) + mask[at, :, 0:wide][None]
            peak = jnp.max(scores, axis=-1, keepdims=True)
            expo = jnp.exp(scores - peak)
            weights = (expo * (1.0 / jnp.sum(expo, axis=-1, keepdims=True))).astype(bf16)
            mixed = jnp.dot(
                weights.reshape(many * BLOCK, wide), qkv[GROUP + 1, seen, :],
                preferred_element_type=f32,
            ).astype(bf16)
            for n, h in enumerate(heads):
                ctx[here, h * HEAD_DIM : (h + 1) * HEAD_DIM] = mixed[n * BLOCK : (n + 1) * BLOCK]
            if at % 2:
                @pl.when(swapped)
                def _():
                    out_remote(k, at // 2).start()

                @pl.when(jnp.logical_not(swapped))
                def _():
                    out_local(k, at // 2).start()

    def receive(who, d, k):
        for way in range(2):
            p = z + d * (1 - 2 * way)

            @pl.when(z == ((1, 2, 0), (2, 1, 3))[way][who])
            def _():
                ref = half(k, p)
                if d == 1:
                    remote(ref, ref, near_send.at[way, k], near_recv.at[way, k], mate).wait_recv()
                else:
                    remote(
                        ref, ref, far_send.at[way, k, d - 2], far_recv.at[way, k, d - 2], mate
                    ).wait_recv()
                if who == 1 or (who == 0 and k != OFF):
                    far(way, k, d + 1).start()
                send_mate(k, p).start()

    def inner(d, k):
        receive(0, d, k)

    def outer(d, k):
        receive(1, d, k)

    def ends_get(d, k):
        receive(2, d, k)

    def take_unit(n):
        @pl.when(middle)
        def _():
            unit_z(n).wait_recv()
            if n < UNITS - DIRECT:
                unit_y(n).start()
            unit_mate(n).start()

    def take_side(n):
        @pl.when(middle)
        def _():
            at = tok2.at[row_unit(UNITS - 1 - n)]
            remote(at, at, tv_send.at[0], tv_recv.at[n], mate).wait_recv()
            unit_mate(UNITS - 1 - n).start()

    def unit_norm(n):
        @pl.when(middle)
        def _():
            at = c + (1 - y) * 2 * n + y * 2 * (UNITS - 1 - n) + 1 - 2 * c
            size = count // 2 // UNITS
            ref = tok2.at[pl.ds(pl.multiple_of(at * size, size), size)]
            remote(ref, ref, tm_send.at[0], tm_recv.at[n], mate).wait_recv()
            first = ((1 - y) * n + y * (UNITS - 1 - n)) * 2 * size
            normalise(tok2, normed2, first, 2 * size)

    both_mid = jnp.logical_and(middle, swapped)
    kx_planes = (0, 2, 3)

    def other_x(i):
        p = orders[kx_planes[i]]
        return remote(fulls[OFF].at[p], fullo.at[p], kx_send.at[0], kx_recv.at[i], partner)

    def other_z(n):
        ref = fullo.at[orders[n]]
        return remote(ref, ref, kz_send.at[0], kz_recv.at[0], device(3 - z, x, y, c))

    def give_other(n):
        @pl.when(middle)
        def _():
            take_mate(OFF, orders[n])
        if n in kx_planes:
            @pl.when(both_mid)
            def _():
                other_x(kx_planes.index(n)).start()

    def take_other(i):
        @pl.when(both_mid)
        def _():
            other_x(i).wait_recv()
            if i == 0:
                other_z(0).start()

    def last_others():
        @pl.when(both_mid)
        def _():
            other_z(1).wait_recv()

    def give_heads(source):
        return remote(
            source, qkv.at[pl.ds(CHUNKS[OFF][0] // HEAD_DIM, 2)], kv_send.at[0], kv_recv.at[0],
            device(pair, x, y, c),
        )

    heads_over = remote(kv2, kv3, kp_send.at[0], kp_recv.at[0], partner)

    def pass_heads():
        @pl.when(both_mid)
        def _():
            heads_over.wait_recv()
            give_heads(kv3).start()


    def serve_end():
        def sums(full):
            acco[...] = whole(normed2[...], full)

        @pl.when(swapped)
        def _():
            sums(fullo)

        @pl.when(jnp.logical_not(swapped))
        def _():
            sums(fulls[OFF])

        lo, hi = CHUNKS[OFF]
        joined = acco[...] + bias_line(2 * y + c)[:, lo:hi]
        for h in range(2):
            v = joined[:, h * HEAD_DIM : (h + 1) * HEAD_DIM]
            kv2[h] = rotated(v, cosine2[...], sine2[...])

        @pl.when(swapped)
        def _():
            heads_over.start()

        @pl.when(jnp.logical_not(swapped))
        def _():
            give_heads(kv2).start()

    def pass_tokens(n):
        @pl.when(swapped)
        def _():
            tok_x(n).wait_recv()
            tok_y(n).start()
            normalise(tok, normed, y * (count // 2) + n * rows, rows)

    def tokens_y(n):
        @pl.when(swapped)
        def _():
            at = tok.at[part_rows(1 - y, n)]
            remote(at, at, ty_send.at[0], ty_recv.at[n], mate).wait_recv()
            normalise(tok, normed, (1 - y) * (count // 2) + n * rows, rows)

    bias = bias_line(group)
    take_unit(0)
    inner(1, OFF)
    give_other(0)
    start_tokens(2)
    start_tokens(3)
    pass_tokens(0)
    inner(1, 0)
    outer(1, OFF)
    outer(1, 0)
    take_unit(1)
    unit_norm(0)
    inner(1, 1)
    pass_tokens(1)
    inner(1, 2)
    give_other(2)

    @pl.when(jnp.logical_not(swapped))
    def _():
        tok_copy.wait()
        normalise(tok, normed, 0, count)

    inner(2, OFF)
    outer(1, 1)
    give_other(1)
    give_other(3)
    take_side(0)
    take_unit(2)
    take_other(0)
    unit_norm(1)
    tables(cosine, sine, own_ends)
    masks()
    pass_tokens(2)
    inner(2, 0)
    unit_norm(UNITS - 1)
    tokens_y(0)

    @pl.when(middle)
    def _():
        tables(cosine2, sine2, ends_of(sides[me, pair]))

    outer(1, 2)
    pass_tokens(3)
    unit_norm(2)
    take_side(1)
    inner(2, 1)
    unit_norm(UNITS - 2)
    tokens_y(1)
    take_unit(3)
    take_side(2)
    chunk_middle(0, False)
    unit_norm(3)
    chunk_middle(OFF, False)
    tokens_y(2)
    for n in range(4, DIRECT):
        take_unit(n)
    chunk_middle(1, False)
    unit_norm(UNITS - 3)
    take_other(1)
    tokens_y(3)
    inner(2, 2)
    unit_norm(4)
    take_other(2)
    last_others()
    pl.when(middle)(serve_end)
    chunk_middle(0, True)
    chunk_end(0)
    chunk_middle(1, True)
    for k in range(1, number):
        if k == 2:
            pass_heads()
            chunk_middle(k, False)
        chunk_end(k)
        if k > 1:
            chunk_middle(k, True)
        attend(k)

    whole_line.wait_send()
    whole_sides.wait_send()
    for k in range(number):
        remote(wbs[k], wbs[k], first_send.at[k], first_recv.at[k, 0], mate).wait_send()
    for k in range(number):
        def mates():
            ref = fulls[k].at[:, :, c]
            remote(ref, ref, mate_send.at[k], mate_recv.at[k, 0], mate).wait_send()

        if k != OFF:
            mates()
        else:
            pl.when(middle)(mates)
        for way in range(2):
            @pl.when(sends(way, k))
            def _():
                ref = half(k, z)
                remote(ref, ref, near_send.at[way, k], near_recv.at[way, k], mate).wait_send()

            @pl.when(z == 2 - way if k == OFF else middle)
            def _():
                far(way, k, 2).wait_send()

            if k != OFF:
                @pl.when(z == 1 + way)
                def _():
                    far(way, k, 3).wait_send()

    @pl.when(end)
    def _():
        sent(DIRECT * unit_rows, tz_send, tz_recv)

    @pl.when(middle)
    def _():
        sent((UNITS - DIRECT) * unit_rows, tv_send, tv_recv)
        sent(UNITS * unit_rows, tm_send, tm_recv)
        give_heads(kv2).wait_send()

    @pl.when(both_mid)
    def _():
        ref = fullo.at[pl.ds(0, len(kx_planes))]
        remote(ref, ref, kx_send.at[0], kx_recv.at[0], mate).wait_send()
        heads_over.wait_send()
        other_z(0).wait_send()

    @pl.when(swapped)
    def _():
        sent(count // 2, tx_send, tx_recv)
        sent(count // 2, ty_send, ty_recv)
        out = remote(ctx, out_hbm, out_send.at[0], out_recv.at[0], partner)
        out.wait_recv()
        out.wait_send()

    @pl.when(jnp.logical_not(swapped))
    def _():
        pltpu.make_async_copy(ctx, out_hbm, out_sem).wait()


def serve(tokens, norm_gain, qkv_weight, qkv_bias, lens):
    count, depth = tokens.shape
    shard, columns = qkv_weight.shape
    width = columns // 4
    sizes = [hi - lo for lo, hi in CHUNKS]
    number, blocks = len(sizes), count // BLOCK
    hbm = pl.BlockSpec(memory_space=pltpu.HBM)
    dma, vmem = pltpu.SemaphoreType.DMA, pltpu.VMEM
    f32, bf16 = jnp.float32, jnp.bfloat16
    two = lambda *shape: [dma(shape), dma(shape)]
    return pl.pallas_call(
        serve_kernel,
        out_shape=jax.ShapeDtypeStruct((count, GROUP * HEAD_DIM), bf16),
        in_specs=[hbm] * 5,
        out_specs=hbm,
        scratch_shapes=[
            vmem(lens.shape, jnp.int32),
            vmem((1, shard), f32),
            vmem((1, columns // 32), f32),
            dma((3,)),
            vmem((4, shard, width), f32),
            *[vmem((3, shard, size), bf16) for size in sizes],
            *[vmem((4, 4, 2, shard, size), bf16) for size in sizes],
            vmem((4, 4, 2, shard, sizes[OFF]), bf16),
            vmem((count, depth), bf16),
            vmem((count, depth), bf16),
            vmem((count, depth), bf16),
            vmem((count, depth), bf16),
            vmem((count, sizes[OFF]), f32),
            *[vmem((count, size), f32) for size in sizes],
            vmem((GROUP + 2, count, HEAD_DIM), bf16),
            vmem((2, count, HEAD_DIM), bf16),
            vmem((2, count, HEAD_DIM), bf16),
            *[vmem((count, HEAD_DIM), f32)] * 4,
            vmem((blocks, BLOCK, 3 * BLOCK), f32),
            vmem((4, 8, 8 * shard), f32),
            vmem((count, GROUP * HEAD_DIM), bf16),
            vmem((8, 128), f32),
            vmem((4, 8, 128), f32),
            vmem((8, 4, 8, 128), f32),
            dma, dma((4,)),
            *two(1), *two(1), dma((number,)), dma((number, 3)),
            *two(2, number), *two(2, number, 2), dma((number,)), dma((number, 4)),
            *[dma((many,)) for n in (PARTS, PARTS, DIRECT, UNITS - DIRECT, UNITS, 3) for many in (1, n)],
            *two(1), *two(1), *two(1), *two(1), dma,
        ],
        compiler_params=pltpu.CompilerParams(
            collective_id=0, has_side_effects=True, vmem_limit_bytes=60 << 20
        ),
        name="serve",
    )(lens, norm_gain.reshape(1, shard), qkv_bias.reshape(1, -1), qkv_weight, tokens)


def turn_plain(joined, lens):
    count = joined.shape[0]
    half = HEAD_DIM // 2
    pos = jnp.arange(count, dtype=jnp.int32) - starts(lens, count)
    freqs = jnp.exp(-(jnp.arange(half, dtype=jnp.float32) * 2.0 / HEAD_DIM) * math.log(1000000.0))
    angle = pos.astype(jnp.float32)[:, None] * freqs[None, :]
    cosine = jnp.tile(jnp.cos(angle), (1, 2))[:, None, :]
    sine = jnp.tile(jnp.sin(angle), (1, 2))[:, None, :]
    heads = joined.reshape(count, GROUP + 2, HEAD_DIM)
    spun = jnp.concatenate([-heads[..., half:], heads[..., :half]], axis=-1)
    turned = (heads * cosine + spun * sine)[:, : GROUP + 1]
    both = jnp.concatenate([turned, heads[:, GROUP + 1 :]], axis=1)
    return both.reshape(count, -1).astype(jnp.bfloat16)


def project_plain(tokens, norm_gain, qkv_weight, qkv_bias):
    tp_count = lax.axis_size("tp")
    req_count = lax.axis_size("req")
    tp_place = lax.axis_index("tp")
    gain_full, bias_full = (
        lax.all_gather(norm_gain.astype(jnp.bfloat16), ("req", "tp"), axis=0, tiled=True),
        lax.all_gather(qkv_bias.astype(jnp.bfloat16), ("req", "tp"), axis=0, tiled=True),
    )
    width = bias_full.shape[0] // tp_count
    bias_block = lax.dynamic_slice_in_dim(bias_full, tp_place * width, width).astype(jnp.float32)
    normed = normalize(tokens, gain_full)
    weight_b = qkv_weight.astype(jnp.bfloat16)
    count = tokens.shape[0]
    gathered = lax.all_gather(weight_b, "req", axis=0, tiled=True)
    regrouped = lax.all_to_all(gathered, "tp", split_axis=1, concat_axis=0, tiled=True)
    shard_rows = weight_b.shape[0]
    reordered = (
        normed.reshape(count, req_count, tp_count, shard_rows)
        .transpose(0, 2, 1, 3)
        .reshape(count, -1)
    )
    joined = jnp.dot(reordered, regrouped, preferred_element_type=jnp.float32)
    return joined + bias_block[None, :]


def shards(small, tokens, norm_gain, qkv_weight, qkv_bias, lengths):
    if small:
        return serve(tokens, norm_gain, qkv_weight, qkv_bias, lengths)
    qkv = turn_plain(project_plain(tokens, norm_gain, qkv_weight, qkv_bias), lengths[0])
    return attend_turned(qkv, lengths)


def solution(mesh):
    placed = (
        P("req", None),
        P(("req", "tp")),
        P(("req", "tp"), None),
        P(("req", "tp")),
        P("req", None),
    )
    small = mesh.shape["req"] == 8 and mesh.shape["tp"] == 4
    return jax.shard_map(
        functools.partial(shards, small),
        mesh=mesh, in_specs=placed, out_specs=P("req", "tp"), check_vma=False,
    )
```

```python
import functools
import math

import jax
import jax.numpy as jnp
from jax import lax
from jax.experimental import pallas as pl
from jax.experimental.pallas import tpu as pltpu
from jax.sharding import PartitionSpec as P

HEAD_DIM = 128
SINKS = 4
GROUP = 7
WINDOW = 160
MOST = 256
MESH = pl.DeviceIdType.MESH


def normalize(values, gain):
    wide = values.astype(jnp.float32)
    meansq = jnp.mean(wide * wide, axis=-1, keepdims=True)
    return (wide * lax.rsqrt(meansq + 1e-06) * gain.astype(jnp.float32)).astype(jnp.bfloat16)


def starts(lens, count):
    index = jnp.arange(count, dtype=jnp.int32)
    start, end = jnp.zeros((count,), jnp.int32), jnp.int32(0)
    for t in range(lens.shape[0]):
        end = end + lens[t]
        start = jnp.where(index >= end, end, start)
    return start


def rotated(v, cosine, sine):
    return (v * cosine + pltpu.roll(v, HEAD_DIM // 2, 1) * sine).astype(jnp.bfloat16)


def start_of(query_at, lens_ref):
    start, end = jnp.zeros_like(query_at), jnp.int32(0)
    for t in range(lens_ref.shape[1]):
        end = end + lens_ref[0, t]
        start = jnp.where(query_at >= end, end, start)
    return start


def attend_kernel(lens_ref, qkv_ref, out_ref):
    count = qkv_ref.shape[0]
    block = 128
    back = -(-(MOST - 1) // block)
    for at in range(count // block):
        first = max(0, at - back)
        wide = (at + 1 - first) * block
        rows = slice(at * block, (at + 1) * block)
        seen = slice(first * block, (at + 1) * block)
        query_at = at * block + lax.broadcasted_iota(jnp.int32, (block, 1), 0)
        key_at = first * block + lax.broadcasted_iota(jnp.int32, (block, wide), 1)
        start = start_of(query_at, lens_ref)
        low = jnp.maximum(query_at - (WINDOW - 1), start)
        allowed = jnp.logical_and(
            key_at <= query_at,
            jnp.logical_or(
                key_at >= low, jnp.logical_and(key_at >= start, key_at < start + SINKS)
            ),
        )
        query = jnp.concatenate(
            [qkv_ref[rows, h * HEAD_DIM : (h + 1) * HEAD_DIM] for h in range(GROUP)], axis=0
        )
        scores = lax.dot_general(
            query, qkv_ref[seen, GROUP * HEAD_DIM : (GROUP + 1) * HEAD_DIM],
            (((1,), (1,)), ((), ())), preferred_element_type=jnp.float32,
        ) * (1.0 / math.sqrt(HEAD_DIM))
        scores = jnp.where(allowed[None], scores.reshape(GROUP, block, wide), -1e30)
        peak = jnp.max(scores, axis=-1, keepdims=True)
        expo = jnp.exp(scores - peak)
        weights = (expo * (1.0 / jnp.sum(expo, axis=-1, keepdims=True))).astype(jnp.bfloat16)
        mixed = jnp.dot(
            weights.reshape(GROUP * block, wide), qkv_ref[seen, (GROUP + 1) * HEAD_DIM :],
            preferred_element_type=jnp.float32,
        ).astype(jnp.bfloat16)
        for h in range(GROUP):
            out_ref[rows, h * HEAD_DIM : (h + 1) * HEAD_DIM] = mixed[h * block : (h + 1) * block]


def attend_turned(qkv, lens):
    count = qkv.shape[0]
    vmem = pl.BlockSpec(memory_space=pltpu.VMEM)
    return pl.pallas_call(
        attend_kernel,
        out_shape=jax.ShapeDtypeStruct((count, GROUP * HEAD_DIM), jnp.bfloat16),
        in_specs=[pl.BlockSpec(memory_space=pltpu.SMEM), vmem],
        out_specs=vmem,
        compiler_params=pltpu.CompilerParams(vmem_limit_bytes=64 << 20),
        name="attention",
    )(lens, qkv)


CHUNKS = ((896, 1152), (0, 384), (384, 640), (640, 896))
OFF = 3
BLOCK = 128
PARTS = 4
UNITS, DIRECT = 8, 5


def serve_kernel(
    lens_hbm, gain_hbm, bias_hbm, w_hbm, tok_hbm, out_hbm,
    lens_ref, gain_ref, bias_ref, small_sem, wide_w, wb0, wb1, wb2, wb3, full0, full1, full2, full3,
    fullo, tok, tok2, normed, normed2, acco, acc0, acc1, acc2, acc3, qkv, kv2, kv3, cosine, sine, cosine2, sine2, mask, gains, ctx, side, line, sides,
    tok_sem, w_sem, line_send, line_recv, side_send, side_recv, first_send, first_recv,
    near_send, near_recv, far_send, far_recv, mate_send, mate_recv,
    tx_send, tx_recv, ty_send, ty_recv, tz_send, tz_recv, tv_send, tv_recv, tm_send, tm_recv,
    kx_send, kx_recv, kz_send, kz_recv, kv_send, kv_recv, kp_send, kp_recv, out_send, out_recv, out_sem,
):
    f32, bf16 = jnp.float32, jnp.bfloat16
    wbs, fulls, accs = (wb0, wb1, wb2, wb3), (full0, full1, full2, full3), (acc0, acc1, acc2, acc3)
    number = len(CHUNKS)
    req, tp = lax.axis_index("req"), lax.axis_index("tp")
    z, x, y, c = req // 2, req % 2, tp // 2, tp % 2
    group, place, me = 2 * y + x, 2 * x + y, 4 * x + 2 * y + c
    count, depth = tok.shape
    shard = wide_w.shape[1]
    width = wide_w.shape[2]
    swapped = x != c
    middle = jnp.logical_or(z == 1, z == 2)
    end = jnp.logical_not(middle)
    pair = jnp.where(middle, 3 * (z // 2), 1 + z // 2)
    orders = (z, 1 + z % 2, 2 + z // 2 - 2 * (z % 2), 3 * (1 - z // 2))

    def device(at_z, at_x, at_y, at_c):
        return (2 * at_z + at_x, 2 * at_y + at_c)

    def flipped(m):
        fx, fy, fc = m // 4, m // 2 % 2, m % 2
        return (
            1 - x if fx else x,
            1 - y if fy else y,
            1 - c if fc else c,
        )

    def remote(source, to, send_sem, recv_sem, where):
        return pltpu.make_async_remote_copy(
            src_ref=source, dst_ref=to, send_sem=send_sem, recv_sem=recv_sem,
            device_id=where, device_id_type=MESH,
        )

    partner = device(z, 1 - x, y, 1 - c)
    mate = device(z, x, y, 1 - c)

    barrier = pltpu.get_barrier_semaphore()
    for m in range(1, 8):
        pl.semaphore_signal(barrier, inc=1, device_id=device(z, *flipped(m)), device_id_type=MESH)
    for dz in range(1, 4):
        pl.semaphore_signal(
            barrier, inc=1, device_id=device((z + dz) % 4, x, y, c), device_id_type=MESH
        )

    smalls = [
        pltpu.make_async_copy(source, to, small_sem.at[k])
        for k, (source, to) in enumerate(
            ((gain_hbm, gain_ref), (bias_hbm, bias_ref), (lens_hbm, lens_ref))
        )
    ]
    for copy in smalls:
        copy.start()
    flips = ((0, 0), (1, 0), (0, 1), (1, 1))
    loads = []
    for k, (fx, fy) in enumerate(flips):
        g = 2 * (1 - y if fy else y) + (1 - x if fx else x)
        copy = pltpu.make_async_copy(
            w_hbm.at[:, pl.ds(pl.multiple_of(g * width, 128), width)], wide_w.at[k], w_sem.at[k]
        )
        copy.start()
        loads.append(copy)
    tok_copy = pltpu.make_async_copy(tok_hbm, tok, tok_sem)

    @pl.when(jnp.logical_not(swapped))
    def _():
        tok_copy.start()

    def rounded(v):
        return v.astype(bf16).astype(f32)

    for copy in smalls:
        copy.wait()
    side[...] = jnp.zeros_like(side)
    side[0:1, 0:shard] = rounded(gain_ref[...])
    side[1:2, :] = rounded(bias_ref[:, 0:128])
    side[2:3, 0 : width // 8 - 128] = rounded(bias_ref[:, 128:])
    side[3:4, 0 : lens_ref.shape[1]] = lens_ref[...].astype(f32)

    for i in range(4):
        loads[i].wait()
        if i:
            for k, (lo, hi) in enumerate(CHUNKS):
                wbs[k][i - 1] = wide_w[i, :, lo:hi].astype(bf16)
    pl.semaphore_wait(barrier, 10)
    for dz in range(1, 4):
        copy = remote(
            side, line.at[z], line_send.at[0], line_recv.at[0], device((z + dz) % 4, x, y, c)
        )
        copy.start()
    ref = line.at[pl.ds(0, 3)]
    whole_line = remote(ref, ref, line_send.at[0], line_recv.at[0], mate)
    line[z] = side[...]

    def half(k, p):
        return fulls[k].at[p, :, c]

    def near(way, k, j):
        ref = fulls[k].at[z, j, c]
        return remote(
            ref, ref, near_send.at[k], near_recv.at[way, k],
            device(z - 1 + 2 * way, x, y, c),
        )

    def far(way, k, d):
        ref = half(k, z + (d - 1) * (1 - 2 * way))
        return remote(
            ref, ref, far_send.at[k], far_recv.at[k, d - 2],
            device(z - 1 + 2 * way, x, y, c),
        )

    def sends(way, k):
        return z >= (2 if k == OFF else 1) if way == 0 else z <= (1 if k == OFF else 2)

    def start_near(k, j):
        for way in range(2):
            copy = near(way, k, j)

            @pl.when(sends(way, k))
            def _():
                copy.start()

    def row_unit(n):
        at = c + (1 - y) * 2 * n + y * 2 * (UNITS - 1 - n)
        size = count // 2 // UNITS
        return pl.ds(pl.multiple_of(at * size, size), size)

    def unit_z(n):
        at = row_unit(n)
        return remote(
            tok_hbm.at[at], tok2.at[at], tz_send.at[0], tz_recv.at[n], device(pair, x, y, c)
        )

    def unit_y(n):
        at = tok2.at[row_unit(n)]
        return remote(at, at, tv_send.at[0], tv_recv.at[n], device(z, x, 1 - y, c))

    def unit_mate(n):
        at = tok2.at[row_unit(n)]
        return remote(at, at, tm_send.at[0], tm_recv.at[n], mate)

    unit_rows = count // 2 // UNITS

    def sent(many, send_sem, recv_sem):
        ref = tok.at[pl.ds(0, many)]
        remote(ref, ref, send_sem.at[0], recv_sem.at[0], mate).wait_send()

    def start_units(*which):
        @pl.when(end)
        def _():
            for n in which:
                unit_z(n).start()

    for k, (lo, hi) in enumerate(CHUNKS):
        fulls[k][z, place, c] = wide_w[0, :, lo:hi].astype(bf16)
    start_near(OFF, place)
    start_near(0, place)
    start_units(0)

    @pl.when(middle)
    def _():
        for k in (1, 2):
            for way in range(2):
                near(way, k, place).start()

    firsts = {}
    for k in (OFF, 0, 1, 2):
        for i, (fx, fy) in enumerate(flips[1:]):
            copy = remote(
                wbs[k].at[i], fulls[k].at[z, place, c], first_send.at[k], first_recv.at[k, i],
                device(z, 1 - x if fx else x, 1 - y if fy else y, c),
            )
            copy.start()
            firsts[k, i] = copy

    def send_mate(k, p):
        ref = half(k, p)
        return remote(ref, ref, mate_send.at[k], mate_recv.at[k, p], mate)

    whole_line.wait_recv()
    for m in range(1, 8):
        copy = remote(
            line, sides.at[me], side_send.at[0], side_recv.at[0], device(z, *flipped(m))
        )
        copy.start()
    ref = sides.at[pl.ds(0, 7)]
    whole_sides = remote(ref, ref, side_send.at[0], side_recv.at[0], mate)
    sides[me] = line[...]

    rows = count // 2 // PARTS

    def part_rows(at_y, n):
        return pl.ds(pl.multiple_of(at_y * (count // 2) + n * rows, rows), rows)

    def tok_x(n):
        at = part_rows(y, n)
        return remote(tok_hbm.at[at], tok.at[at], tx_send.at[0], tx_recv.at[n], partner)

    def tok_y(n):
        at = tok.at[part_rows(y, n)]
        return remote(at, at, ty_send.at[0], ty_recv.at[n], device(z, x, 1 - y, c))

    def start_tokens(n):
        @pl.when(swapped)
        def _():
            tok_x(n).start()

    def forward(k, *which):
        for i in which:
            fx, fy = flips[i + 1]
            firsts[k, i].wait_recv()
            start_near(k, 2 * (1 - x if fx else x) + (1 - y if fy else y))

    def own_mate(k):
        if k != OFF:
            send_mate(k, z).start()
        else:

            @pl.when(middle)
            def _():
                send_mate(k, z).start()

    def start_end_near(k):
        @pl.when(end)
        def _():
            start_near(k, place)

    for k in (OFF, 0):
        forward(k, 0, 1, 2)
        own_mate(k)
    start_units(1)
    start_tokens(0)
    start_end_near(1)
    forward(1, 0, 1, 2)
    own_mate(1)
    start_units(2)
    start_end_near(2)
    forward(2, 0, 1, 2)
    own_mate(2)
    start_units(*range(3, DIRECT))
    start_tokens(1)

    whole_sides.wait_recv()

    def spread(piece, step, n, size):
        wide = jnp.concatenate(piece + [jnp.zeros((8, size - 128 * len(piece)), f32)], axis=1)
        return pltpu.roll(wide, step * n, 1) if n else wide

    for p in range(4):
        total = jnp.zeros((8, 8 * 128), f32)
        for n in range(8):
            total = total + spread([sides[n, p]], shard, n, 8 * 128)
        gains[p] = total[:, 0 : 8 * shard]

    def ends_of(lens):
        ends, last = [], jnp.zeros((1, 1), f32)
        for t in range(lens_ref.shape[1]):
            last = last + lens[3:4, t : t + 1]
            ends.append(last)
        return ends

    own_ends = ends_of(sides[4 * c + 2 * y + c, z])

    def start_at(query, ends):
        start = jnp.zeros_like(query)
        for e in ends:
            start = jnp.where(query >= e, e, start)
        return start

    def tables(cosine, sine, ends):
        query = lax.broadcasted_iota(jnp.int32, (count, 1), 0).astype(f32)
        pos = query - start_at(query, ends)
        lane = lax.broadcasted_iota(jnp.int32, (1, HEAD_DIM), 1)
        mid = HEAD_DIM // 2
        freqs = jnp.exp(-((lane % mid).astype(f32) * 2.0 / HEAD_DIM) * math.log(1000000.0))
        angle = pos * freqs
        cosine[...] = jnp.cos(angle)
        sine[...] = jnp.where(lane < mid, -1.0, 1.0) * jnp.sin(angle)

    back = -(-(MOST - 1) // BLOCK)

    def reach(at):
        first = max(0, at - back)
        return first, (at + 1 - first) * BLOCK

    def masks():
        for at in range(count // BLOCK):
            first, wide = reach(at)
            query = (at * BLOCK + lax.broadcasted_iota(jnp.int32, (BLOCK, 1), 0)).astype(f32)
            key = (first * BLOCK + lax.broadcasted_iota(jnp.int32, (BLOCK, wide), 1)).astype(f32)
            start = start_at(query, own_ends)
            low = jnp.maximum(query - (WINDOW - 1), start)
            allowed = jnp.logical_and(
                key <= query,
                jnp.logical_or(key >= low, jnp.logical_and(key >= start, key < start + SINKS)),
            )
            mask[at, :, 0:wide] = jnp.where(allowed, 0.0, -1e30)

    def normalise(tok, normed, first, many):
        @pl.loop(0, many // 32)
        def _(i):
            at = pl.ds(pl.multiple_of(first + i * 32, 32), 32)
            square = jnp.zeros((32, 8 * shard), f32)
            for p in range(4):
                wide = tok[at, p * 8 * shard : (p + 1) * 8 * shard].astype(f32)
                square = square + wide * wide
            mean = jnp.sum(square, axis=-1, keepdims=True) * (1.0 / depth)
            scale = lax.rsqrt(mean + 1e-06)
            for p in range(4):
                part = slice(p * 8 * shard, (p + 1) * 8 * shard)
                wide = tok[at, part].astype(f32)
                normed[at, part] = (wide * scale * gains[p, 0:1, :]).astype(bf16)

    def product(k, p):
        block = fulls[k][p].reshape(8 * shard, fulls[k].shape[-1])
        part = pl.ds(pl.multiple_of(p * 8 * shard, 128), 8 * shard)
        return jnp.dot(normed[:, part], block, preferred_element_type=f32)

    def whole(lhs, full):
        block = full[...].reshape(depth, full.shape[-1])
        return jnp.dot(lhs, block, preferred_element_type=f32)

    def some_rows(at_y):
        return pl.ds(pl.multiple_of(at_y * (count // 2), count // 2), count // 2)

    def take_mate(k, p):
        ref = fulls[k].at[p, :, 1 - c]
        remote(ref, ref, mate_send.at[k], mate_recv.at[k, p], mate).wait_recv()

    def add(k, n):
        p = orders[n]
        take_mate(k, p)
        if n == 0:
            accs[k][...] = product(k, p)
        else:
            accs[k][...] += product(k, p)

    def bias_line(group):
        total = jnp.zeros((8, width), f32)
        for n in range(8):
            both = sides[n, group]
            total = total + spread(
                [pltpu.roll(both, 7, 0), pltpu.roll(both, 6, 0)], width // 8, n, width
            )
        return total[0:1, :]

    def finish(k, sums, rows=slice(None)):
        lo, hi = CHUNKS[k]
        joined = sums + bias[:, lo:hi]
        for h in range(lo // HEAD_DIM, hi // HEAD_DIM):
            v = joined[:, h * HEAD_DIM - lo : (h + 1) * HEAD_DIM - lo]
            qkv[h, rows, :] = (
                rotated(v, cosine[rows, :], sine[rows, :]) if h <= GROUP else v.astype(bf16)
            )

    def chunk_end(k):
        if k == OFF:

            @pl.when(end)
            def _():
                for h in range(2):
                    give_head(kv2, h).wait_recv()

            return

        @pl.when(end)
        def _():
            add(k, 0)

        @pl.when(end)
        def _():
            add(k, 1)
            add(k, 2)

        ends_get(3, k)

        @pl.when(end)
        def _():
            p = orders[3]
            take_mate(k, p)
            finish(k, accs[k][...] + product(k, p))

    def chunk_middle(k, late):
        @pl.when(middle)
        def _():
            if k != OFF and not late:
                for n in range(4):
                    take_mate(k, orders[n])
            rows = some_rows(1 - y if late else y)
            finish(k, whole(normed[rows, :], fulls[k]), rows)

    def out_at(k, part):
        lo, hi = CHUNKS[k]
        where = (pl.ds(part * (count // 2), count // 2), pl.ds(lo, hi - lo))
        return ctx.at[where], out_hbm.at[where]

    def out_remote(k, part):
        source, to = out_at(k, part)
        return remote(source, to, out_send.at[0], out_recv.at[0], partner)

    def out_local(k, part):
        source, to = out_at(k, part)
        return pltpu.make_async_copy(source, to, out_sem)

    def attend(k):
        lo, hi = CHUNKS[k]
        heads = range(lo // HEAD_DIM, hi // HEAD_DIM)
        many = len(heads)
        for at in range(count // BLOCK):
            first, wide = reach(at)
            here = slice(at * BLOCK, (at + 1) * BLOCK)
            seen = slice(first * BLOCK, (at + 1) * BLOCK)
            query = jnp.concatenate([qkv[h, here, :] for h in heads], axis=0)
            scores = lax.dot_general(
                query, qkv[GROUP, seen, :], (((1,), (1,)), ((), ())), preferred_element_type=f32
            )
            scores = scores.reshape(many, BLOCK, wide) + mask[at, :, 0:wide][None]
            peak = jnp.max(scores, axis=-1, keepdims=True)
            expo = jnp.exp2((scores - peak) * (math.log2(math.e) / math.sqrt(HEAD_DIM)))
            weights = (expo * (1.0 / jnp.sum(expo, axis=-1, keepdims=True))).astype(bf16)
            mixed = jnp.dot(
                weights.reshape(many * BLOCK, wide), qkv[GROUP + 1, seen, :],
                preferred_element_type=f32,
            ).astype(bf16)
            for n, h in enumerate(heads):
                ctx[here, h * HEAD_DIM : (h + 1) * HEAD_DIM] = mixed[n * BLOCK : (n + 1) * BLOCK]
            if at % 2:
                @pl.when(swapped)
                def _():
                    out_remote(k, at // 2).start()

                @pl.when(jnp.logical_not(swapped))
                def _():
                    out_local(k, at // 2).start()

                if k == 1 and at == 1:
                    pass_head(0)
                if k == 2 and at == 1:
                    @pl.when(jnp.logical_and(middle, jnp.logical_not(swapped)))
                    def _():
                        for h in range(2):
                            give_head(kv2, h).start()

    def receive(who, d, k):
        for way in range(2):
            p = z + d * (1 - 2 * way)

            @pl.when(z == ((1, 2, 0), (2, 1, 3))[way][who])
            def _():
                ref = half(k, p)
                if d == 1:
                    remote(ref, ref, near_send.at[k], near_recv.at[way, k], mate).wait_recv()
                else:
                    remote(
                        ref, ref, far_send.at[k], far_recv.at[k, d - 2], mate
                    ).wait_recv()
                if who == 1 or (who == 0 and k != OFF):
                    far(way, k, d + 1).start()
                send_mate(k, p).start()

    def inner(d, k):
        receive(0, d, k)

    def outer(d, k):
        receive(1, d, k)

    def ends_get(d, k):
        receive(2, d, k)

    def take_unit(n):
        @pl.when(middle)
        def _():
            unit_z(n).wait_recv()
            if n < UNITS - DIRECT:
                unit_y(n).start()
            unit_mate(n).start()

    def take_side(n):
        @pl.when(middle)
        def _():
            at = tok2.at[row_unit(UNITS - 1 - n)]
            remote(at, at, tv_send.at[0], tv_recv.at[n], mate).wait_recv()
            unit_mate(UNITS - 1 - n).start()

    def unit_norm(n):
        @pl.when(middle)
        def _():
            at = c + (1 - y) * 2 * n + y * 2 * (UNITS - 1 - n) + 1 - 2 * c
            size = count // 2 // UNITS
            ref = tok2.at[pl.ds(pl.multiple_of(at * size, size), size)]
            remote(ref, ref, tm_send.at[0], tm_recv.at[n], mate).wait_recv()
            first = ((1 - y) * n + y * (UNITS - 1 - n)) * 2 * size
            normalise(tok2, normed2, first, 2 * size)

    both_mid = jnp.logical_and(middle, swapped)
    kx_planes = (0, 2, 3)

    def other_x(i):
        p = orders[kx_planes[i]]
        return remote(fulls[OFF].at[p], fullo.at[p], kx_send.at[0], kx_recv.at[i], partner)

    def other_z(n):
        ref = fullo.at[orders[n]]
        return remote(ref, ref, kz_send.at[0], kz_recv.at[0], device(3 - z, x, y, c))

    def give_other(n):
        @pl.when(middle)
        def _():
            take_mate(OFF, orders[n])
        if n in kx_planes:
            @pl.when(both_mid)
            def _():
                other_x(kx_planes.index(n)).start()

    def take_other(i):
        @pl.when(both_mid)
        def _():
            other_x(i).wait_recv()
            if i == 0:
                other_z(0).start()

    def last_others():
        @pl.when(both_mid)
        def _():
            other_z(1).wait_recv()

    def give_head(source, h):
        return remote(
            source.at[h], qkv.at[CHUNKS[OFF][0] // HEAD_DIM + h], kv_send.at[h], kv_recv.at[h],
            device(pair, x, y, c),
        )

    def head_over(h):
        return remote(kv2.at[h], kv3.at[h], kp_send.at[h], kp_recv.at[h], partner)

    def pass_head(h):
        @pl.when(both_mid)
        def _():
            head_over(h).wait_recv()
            give_head(kv3, h).start()

    def serve_end():
        def sums(full):
            acco[...] = whole(normed2[...], full)

        @pl.when(swapped)
        def _():
            sums(fullo)

        @pl.when(jnp.logical_not(swapped))
        def _():
            sums(fulls[OFF])

        lo, hi = CHUNKS[OFF]
        joined = acco[...] + bias_line(2 * y + c)[:, lo:hi]
        for h in range(2):
            v = joined[:, h * HEAD_DIM : (h + 1) * HEAD_DIM]
            kv2[h] = rotated(v, cosine2[...], sine2[...])

        @pl.when(swapped)
        def _():
            for h in range(2):
                head_over(h).start()


    def pass_tokens(n):
        @pl.when(swapped)
        def _():
            tok_x(n).wait_recv()
            tok_y(n).start()
            normalise(tok, normed, y * (count // 2) + n * rows, rows)

    def tokens_y(n):
        @pl.when(swapped)
        def _():
            at = tok.at[part_rows(1 - y, n)]
            remote(at, at, ty_send.at[0], ty_recv.at[n], mate).wait_recv()
            normalise(tok, normed, (1 - y) * (count // 2) + n * rows, rows)

    bias = bias_line(group)
    take_unit(0)
    inner(1, OFF)
    give_other(0)
    start_tokens(2)
    start_tokens(3)
    inner(1, 0)
    pass_tokens(0)
    outer(1, OFF)
    outer(1, 0)
    take_unit(1)
    unit_norm(0)
    inner(1, 1)
    pass_tokens(1)
    inner(1, 2)
    give_other(2)

    @pl.when(jnp.logical_not(swapped))
    def _():
        tok_copy.wait()
        normalise(tok, normed, 0, count)

    inner(2, OFF)
    outer(1, 1)
    give_other(1)
    give_other(3)
    take_side(0)
    take_unit(2)
    take_other(0)
    unit_norm(1)
    tables(cosine, sine, own_ends)
    masks()
    pass_tokens(2)
    for k in range(OFF):
        ends_get(1, k)
    inner(2, 0)
    unit_norm(UNITS - 1)
    tokens_y(0)

    @pl.when(middle)
    def _():
        tables(cosine2, sine2, ends_of(sides[me, pair]))

    outer(1, 2)
    pass_tokens(3)
    ends_get(2, 0)
    unit_norm(2)
    take_side(1)
    inner(2, 1)
    unit_norm(UNITS - 2)
    tokens_y(1)
    take_unit(3)
    take_side(2)
    chunk_middle(0, False)
    unit_norm(3)
    chunk_middle(OFF, False)
    ends_get(2, 1)
    tokens_y(2)
    for n in range(4, DIRECT):
        take_unit(n)
    chunk_middle(1, False)
    unit_norm(UNITS - 3)
    take_other(1)
    ends_get(2, 2)
    unit_norm(4)
    inner(2, 2)
    take_other(2)
    last_others()
    pl.when(middle)(serve_end)
    tokens_y(3)
    chunk_middle(0, True)
    chunk_end(0)
    chunk_middle(1, True)
    for k in range(1, number):
        if k == 2:
            pass_head(1)
            chunk_middle(k, False)
        chunk_end(k)
        if k > 1:
            chunk_middle(k, True)
        attend(k)

    whole_line.wait_send()
    whole_sides.wait_send()
    for k in range(number):
        remote(wbs[k], wbs[k], first_send.at[k], first_recv.at[k, 0], mate).wait_send()
    for k in range(number):
        def mates():
            ref = fulls[k].at[:, :, c]
            remote(ref, ref, mate_send.at[k], mate_recv.at[k, 0], mate).wait_send()

        if k != OFF:
            mates()
        else:
            pl.when(middle)(mates)

        def gone(nears, fars):
            ref = fulls[k].at[pl.ds(0, nears), :, c]
            remote(ref, ref, near_send.at[k], near_recv.at[0, k], mate).wait_send()
            if fars:
                ref = fulls[k].at[pl.ds(0, fars), :, c]
                remote(ref, ref, far_send.at[k], far_recv.at[k, 0], mate).wait_send()

        @pl.when(middle)
        def _():
            gone(*((1, 1) if k == OFF else (2, 3)))

        @pl.when(end)
        def _():
            gone(1, 0)

    @pl.when(end)
    def _():
        sent(DIRECT * unit_rows, tz_send, tz_recv)

    @pl.when(middle)
    def _():
        sent((UNITS - DIRECT) * unit_rows, tv_send, tv_recv)
        sent(UNITS * unit_rows, tm_send, tm_recv)
        for h in range(2):
            give_head(kv2, h).wait_send()

    @pl.when(both_mid)
    def _():
        ref = fullo.at[pl.ds(0, len(kx_planes))]
        remote(ref, ref, kx_send.at[0], kx_recv.at[0], mate).wait_send()
        for h in range(2):
            head_over(h).wait_send()
        other_z(0).wait_send()

    @pl.when(swapped)
    def _():
        sent(count // 2, tx_send, tx_recv)
        sent(count // 2, ty_send, ty_recv)
        out = remote(ctx, out_hbm, out_send.at[0], out_recv.at[0], partner)
        out.wait_recv()
        out.wait_send()

    @pl.when(jnp.logical_not(swapped))
    def _():
        pltpu.make_async_copy(ctx, out_hbm, out_sem).wait()


def serve(tokens, norm_gain, qkv_weight, qkv_bias, lens):
    count, depth = tokens.shape
    shard, columns = qkv_weight.shape
    width = columns // 4
    sizes = [hi - lo for lo, hi in CHUNKS]
    number, blocks = len(sizes), count // BLOCK
    hbm = pl.BlockSpec(memory_space=pltpu.HBM)
    dma, vmem = pltpu.SemaphoreType.DMA, pltpu.VMEM
    f32, bf16 = jnp.float32, jnp.bfloat16
    two = lambda *shape: [dma(shape), dma(shape)]
    return pl.pallas_call(
        serve_kernel,
        out_shape=jax.ShapeDtypeStruct((count, GROUP * HEAD_DIM), bf16),
        in_specs=[hbm] * 5,
        out_specs=hbm,
        scratch_shapes=[
            vmem(lens.shape, jnp.int32),
            vmem((1, shard), f32),
            vmem((1, columns // 32), f32),
            dma((3,)),
            vmem((4, shard, width), f32),
            *[vmem((3, shard, size), bf16) for size in sizes],
            *[vmem((4, 4, 2, shard, size), bf16) for size in sizes],
            vmem((4, 4, 2, shard, sizes[OFF]), bf16),
            vmem((count, depth), bf16),
            vmem((count, depth), bf16),
            vmem((count, depth), bf16),
            vmem((count, depth), bf16),
            vmem((count, sizes[OFF]), f32),
            *[vmem((count, size), f32) for size in sizes],
            vmem((GROUP + 2, count, HEAD_DIM), bf16),
            vmem((2, count, HEAD_DIM), bf16),
            vmem((2, count, HEAD_DIM), bf16),
            *[vmem((count, HEAD_DIM), f32)] * 4,
            vmem((blocks, BLOCK, 3 * BLOCK), f32),
            vmem((4, 8, 8 * shard), f32),
            vmem((count, GROUP * HEAD_DIM), bf16),
            vmem((8, 128), f32),
            vmem((4, 8, 128), f32),
            vmem((8, 4, 8, 128), f32),
            dma, dma((4,)),
            *two(1), *two(1), dma((number,)), dma((number, 3)),
            dma((number,)), dma((2, number)), dma((number,)), dma((number, 2)),
            dma((number,)), dma((number, 4)),
            *[dma((many,)) for n in (PARTS, PARTS, DIRECT, UNITS - DIRECT, UNITS, 3) for many in (1, n)],
            *two(1), *two(2), *two(2), *two(1), dma,
        ],
        compiler_params=pltpu.CompilerParams(
            collective_id=0, has_side_effects=True, vmem_limit_bytes=60 << 20
        ),
        name="serve",
    )(lens, norm_gain.reshape(1, shard), qkv_bias.reshape(1, -1), qkv_weight, tokens)


def turn_plain(joined, lens):
    count = joined.shape[0]
    half = HEAD_DIM // 2
    pos = jnp.arange(count, dtype=jnp.int32) - starts(lens, count)
    freqs = jnp.exp(-(jnp.arange(half, dtype=jnp.float32) * 2.0 / HEAD_DIM) * math.log(1000000.0))
    angle = pos.astype(jnp.float32)[:, None] * freqs[None, :]
    cosine = jnp.tile(jnp.cos(angle), (1, 2))[:, None, :]
    sine = jnp.tile(jnp.sin(angle), (1, 2))[:, None, :]
    heads = joined.reshape(count, GROUP + 2, HEAD_DIM)
    spun = jnp.concatenate([-heads[..., half:], heads[..., :half]], axis=-1)
    turned = (heads * cosine + spun * sine)[:, : GROUP + 1]
    both = jnp.concatenate([turned, heads[:, GROUP + 1 :]], axis=1)
    return both.reshape(count, -1).astype(jnp.bfloat16)


def project_plain(tokens, norm_gain, qkv_weight, qkv_bias):
    tp_count = lax.axis_size("tp")
    req_count = lax.axis_size("req")
    tp_place = lax.axis_index("tp")
    gain_full, bias_full = (
        lax.all_gather(norm_gain.astype(jnp.bfloat16), ("req", "tp"), axis=0, tiled=True),
        lax.all_gather(qkv_bias.astype(jnp.bfloat16), ("req", "tp"), axis=0, tiled=True),
    )
    width = bias_full.shape[0] // tp_count
    bias_block = lax.dynamic_slice_in_dim(bias_full, tp_place * width, width).astype(jnp.float32)
    normed = normalize(tokens, gain_full)
    weight_b = qkv_weight.astype(jnp.bfloat16)
    count = tokens.shape[0]
    gathered = lax.all_gather(weight_b, "req", axis=0, tiled=True)
    regrouped = lax.all_to_all(gathered, "tp", split_axis=1, concat_axis=0, tiled=True)
    shard_rows = weight_b.shape[0]
    reordered = (
        normed.reshape(count, req_count, tp_count, shard_rows)
        .transpose(0, 2, 1, 3)
        .reshape(count, -1)
    )
    joined = jnp.dot(reordered, regrouped, preferred_element_type=jnp.float32)
    return joined + bias_block[None, :]


def shards(small, tokens, norm_gain, qkv_weight, qkv_bias, lengths):
    if small:
        return serve(tokens, norm_gain, qkv_weight, qkv_bias, lengths)
    qkv = turn_plain(project_plain(tokens, norm_gain, qkv_weight, qkv_bias), lengths[0])
    return attend_turned(qkv, lengths)


def solution(mesh):
    placed = (
        P("req", None),
        P(("req", "tp")),
        P(("req", "tp"), None),
        P(("req", "tp")),
        P("req", None),
    )
    small = mesh.shape["req"] == 8 and mesh.shape["tp"] == 4
    return jax.shard_map(
        functools.partial(shards, small),
        mesh=mesh, in_specs=placed, out_specs=P("req", "tp"), check_vma=False,
    )
```

```python
import functools
import math

import jax
import jax.numpy as jnp
from jax import lax
from jax.experimental import pallas as pl
from jax.experimental.pallas import tpu as pltpu
from jax.sharding import PartitionSpec as P

HEAD_DIM = 128
SINKS = 4
GROUP = 7
WINDOW = 160
MOST = 256
MESH = pl.DeviceIdType.MESH


def normalize(values, gain):
    wide = values.astype(jnp.float32)
    meansq = jnp.mean(wide * wide, axis=-1, keepdims=True)
    return (wide * lax.rsqrt(meansq + 1e-06) * gain.astype(jnp.float32)).astype(jnp.bfloat16)


def starts(lens, count):
    index = jnp.arange(count, dtype=jnp.int32)
    start, end = jnp.zeros((count,), jnp.int32), jnp.int32(0)
    for t in range(lens.shape[0]):
        end = end + lens[t]
        start = jnp.where(index >= end, end, start)
    return start


def rotated(v, cosine, sine):
    return (v * cosine + pltpu.roll(v, HEAD_DIM // 2, 1) * sine).astype(jnp.bfloat16)


def start_of(query_at, lens_ref):
    start, end = jnp.zeros_like(query_at), jnp.int32(0)
    for t in range(lens_ref.shape[1]):
        end = end + lens_ref[0, t]
        start = jnp.where(query_at >= end, end, start)
    return start


def attend_kernel(lens_ref, qkv_ref, out_ref):
    count = qkv_ref.shape[0]
    block = 128
    back = -(-(MOST - 1) // block)
    for at in range(count // block):
        first = max(0, at - back)
        wide = (at + 1 - first) * block
        rows = slice(at * block, (at + 1) * block)
        seen = slice(first * block, (at + 1) * block)
        query_at = at * block + lax.broadcasted_iota(jnp.int32, (block, 1), 0)
        key_at = first * block + lax.broadcasted_iota(jnp.int32, (block, wide), 1)
        start = start_of(query_at, lens_ref)
        low = jnp.maximum(query_at - (WINDOW - 1), start)
        allowed = jnp.logical_and(
            key_at <= query_at,
            jnp.logical_or(
                key_at >= low, jnp.logical_and(key_at >= start, key_at < start + SINKS)
            ),
        )
        query = jnp.concatenate(
            [qkv_ref[rows, h * HEAD_DIM : (h + 1) * HEAD_DIM] for h in range(GROUP)], axis=0
        )
        scores = lax.dot_general(
            query, qkv_ref[seen, GROUP * HEAD_DIM : (GROUP + 1) * HEAD_DIM],
            (((1,), (1,)), ((), ())), preferred_element_type=jnp.float32,
        ) * (1.0 / math.sqrt(HEAD_DIM))
        scores = jnp.where(allowed[None], scores.reshape(GROUP, block, wide), -1e30)
        peak = jnp.max(scores, axis=-1, keepdims=True)
        expo = jnp.exp(scores - peak)
        weights = (expo * (1.0 / jnp.sum(expo, axis=-1, keepdims=True))).astype(jnp.bfloat16)
        mixed = jnp.dot(
            weights.reshape(GROUP * block, wide), qkv_ref[seen, (GROUP + 1) * HEAD_DIM :],
            preferred_element_type=jnp.float32,
        ).astype(jnp.bfloat16)
        for h in range(GROUP):
            out_ref[rows, h * HEAD_DIM : (h + 1) * HEAD_DIM] = mixed[h * block : (h + 1) * block]


def attend_turned(qkv, lens):
    count = qkv.shape[0]
    vmem = pl.BlockSpec(memory_space=pltpu.VMEM)
    return pl.pallas_call(
        attend_kernel,
        out_shape=jax.ShapeDtypeStruct((count, GROUP * HEAD_DIM), jnp.bfloat16),
        in_specs=[pl.BlockSpec(memory_space=pltpu.SMEM), vmem],
        out_specs=vmem,
        compiler_params=pltpu.CompilerParams(vmem_limit_bytes=64 << 20),
        name="attention",
    )(lens, qkv)


CHUNKS = ((896, 1152), (0, 384), (384, 640), (640, 896))
OFF = 3
BLOCK = 128
PARTS = 4
UNITS, DIRECT = 8, 5


def serve_kernel(
    lens_hbm, gain_hbm, bias_hbm, w_hbm, tok_hbm, out_hbm,
    lens_ref, gain_ref, bias_ref, small_sem, wide_w, wb0, wb1, wb2, wb3, full0, full1, full2, full3,
    fullo, tok, tok2, normed, normed2, acco, acc0, acc1, acc2, acc3, qkv, kv2, kv3, cosine, sine, cosine2, sine2, mask, gains, ctx, side, line, sides,
    tok_sem, w_sem, line_send, line_recv, side_send, side_recv, first_send, first_recv,
    near_send, near_recv, far_send, far_recv, mate_send, mate_recv,
    tx_send, tx_recv, ty_send, ty_recv, tz_send, tz_recv, tv_send, tv_recv, tm_send, tm_recv,
    kx_send, kx_recv, kz_send, kz_recv, kv_send, kv_recv, kp_send, kp_recv, out_send, out_recv, out_sem,
):
    f32, bf16 = jnp.float32, jnp.bfloat16
    wbs, fulls, accs = (wb0, wb1, wb2, wb3), (full0, full1, full2, full3), (acc0, acc1, acc2, acc3)
    number = len(CHUNKS)
    req, tp = lax.axis_index("req"), lax.axis_index("tp")
    z, x, y, c = req // 2, req % 2, tp // 2, tp % 2
    group, place, me = 2 * y + x, 2 * x + y, 4 * x + 2 * y + c
    count, depth = tok.shape
    shard = wide_w.shape[1]
    width = wide_w.shape[2]
    swapped = x != c
    middle = jnp.logical_or(z == 1, z == 2)
    end = jnp.logical_not(middle)
    pair = jnp.where(middle, 3 * (z // 2), 1 + z // 2)
    orders = (z, 1 + z % 2, 2 + z // 2 - 2 * (z % 2), 3 * (1 - z // 2))

    def device(at_z, at_x, at_y, at_c):
        return (2 * at_z + at_x, 2 * at_y + at_c)

    def flipped(m):
        fx, fy, fc = m // 4, m // 2 % 2, m % 2
        return (
            1 - x if fx else x,
            1 - y if fy else y,
            1 - c if fc else c,
        )

    def remote(source, to, send_sem, recv_sem, where):
        return pltpu.make_async_remote_copy(
            src_ref=source, dst_ref=to, send_sem=send_sem, recv_sem=recv_sem,
            device_id=where, device_id_type=MESH,
        )

    partner = device(z, 1 - x, y, 1 - c)
    mate = device(z, x, y, 1 - c)

    barrier = pltpu.get_barrier_semaphore()
    for m in range(1, 8):
        pl.semaphore_signal(barrier, inc=1, device_id=device(z, *flipped(m)), device_id_type=MESH)
    for dz in range(1, 4):
        pl.semaphore_signal(
            barrier, inc=1, device_id=device((z + dz) % 4, x, y, c), device_id_type=MESH
        )

    smalls = [
        pltpu.make_async_copy(source, to, small_sem.at[k])
        for k, (source, to) in enumerate(
            ((gain_hbm, gain_ref), (bias_hbm, bias_ref), (lens_hbm, lens_ref))
        )
    ]
    for copy in smalls:
        copy.start()
    flips = ((0, 0), (1, 0), (0, 1), (1, 1))
    loads = []
    for k, (fx, fy) in enumerate(flips):
        g = 2 * (1 - y if fy else y) + (1 - x if fx else x)
        copy = pltpu.make_async_copy(
            w_hbm.at[:, pl.ds(pl.multiple_of(g * width, 128), width)], wide_w.at[k], w_sem.at[k]
        )
        copy.start()
        loads.append(copy)
    tok_copy = pltpu.make_async_copy(tok_hbm, tok, tok_sem)

    @pl.when(jnp.logical_not(swapped))
    def _():
        tok_copy.start()

    def rounded(v):
        return v.astype(bf16).astype(f32)

    for copy in smalls:
        copy.wait()
    side[...] = jnp.zeros_like(side)
    side[0:1, 0:shard] = rounded(gain_ref[...])
    side[1:2, :] = rounded(bias_ref[:, 0:128])
    side[2:3, 0 : width // 8 - 128] = rounded(bias_ref[:, 128:])
    side[3:4, 0 : lens_ref.shape[1]] = lens_ref[...].astype(f32)

    for i in range(4):
        loads[i].wait()
        if i:
            for k, (lo, hi) in enumerate(CHUNKS):
                wbs[k][i - 1] = wide_w[i, :, lo:hi].astype(bf16)
    pl.semaphore_wait(barrier, 10)
    for dz in range(1, 4):
        copy = remote(
            side, line.at[z], line_send.at[0], line_recv.at[0], device((z + dz) % 4, x, y, c)
        )
        copy.start()
    ref = line.at[pl.ds(0, 3)]
    whole_line = remote(ref, ref, line_send.at[0], line_recv.at[0], mate)
    line[z] = side[...]

    def half(k, p):
        return fulls[k].at[p, :, c]

    def near(way, k, j):
        ref = fulls[k].at[z, j, c]
        return remote(
            ref, ref, near_send.at[k], near_recv.at[way, k],
            device(z - 1 + 2 * way, x, y, c),
        )

    def far(way, k, d):
        ref = half(k, z + (d - 1) * (1 - 2 * way))
        return remote(
            ref, ref, far_send.at[k], far_recv.at[k, d - 2],
            device(z - 1 + 2 * way, x, y, c),
        )

    def sends(way, k):
        return z >= (2 if k == OFF else 1) if way == 0 else z <= (1 if k == OFF else 2)

    def start_near(k, j):
        for way in range(2):
            copy = near(way, k, j)

            @pl.when(sends(way, k))
            def _():
                copy.start()

    def row_unit(n):
        at = c + (1 - y) * 2 * n + y * 2 * (UNITS - 1 - n)
        size = count // 2 // UNITS
        return pl.ds(pl.multiple_of(at * size, size), size)

    def unit_z(n):
        at = row_unit(n)
        return remote(
            tok_hbm.at[at], tok2.at[at], tz_send.at[0], tz_recv.at[n], device(pair, x, y, c)
        )

    def unit_y(n):
        at = tok2.at[row_unit(n)]
        return remote(at, at, tv_send.at[0], tv_recv.at[n], device(z, x, 1 - y, c))

    def unit_mate(n):
        at = tok2.at[row_unit(n)]
        return remote(at, at, tm_send.at[0], tm_recv.at[n], mate)

    unit_rows = count // 2 // UNITS

    def sent(many, send_sem, recv_sem):
        ref = tok.at[pl.ds(0, many)]
        remote(ref, ref, send_sem.at[0], recv_sem.at[0], mate).wait_send()

    def start_units(*which):
        @pl.when(end)
        def _():
            for n in which:
                unit_z(n).start()

    for k, (lo, hi) in enumerate(CHUNKS):
        fulls[k][z, place, c] = wide_w[0, :, lo:hi].astype(bf16)
    start_near(OFF, place)
    start_near(0, place)
    start_units(0)

    @pl.when(middle)
    def _():
        for k in (1, 2):
            for way in range(2):
                near(way, k, place).start()

    firsts = {}
    for k in (OFF, 0, 1, 2):
        for i, (fx, fy) in enumerate(flips[1:]):
            copy = remote(
                wbs[k].at[i], fulls[k].at[z, place, c], first_send.at[k], first_recv.at[k, i],
                device(z, 1 - x if fx else x, 1 - y if fy else y, c),
            )
            copy.start()
            firsts[k, i] = copy

    def send_mate(k, p):
        ref = half(k, p)
        return remote(ref, ref, mate_send.at[k], mate_recv.at[k, p], mate)

    whole_line.wait_recv()
    for m in range(1, 8):
        copy = remote(
            line, sides.at[me], side_send.at[0], side_recv.at[0], device(z, *flipped(m))
        )
        copy.start()
    ref = sides.at[pl.ds(0, 7)]
    whole_sides = remote(ref, ref, side_send.at[0], side_recv.at[0], mate)
    sides[me] = line[...]

    rows = count // 2 // PARTS

    def part_rows(at_y, n):
        return pl.ds(pl.multiple_of(at_y * (count // 2) + n * rows, rows), rows)

    def tok_x(n):
        at = part_rows(y, n)
        return remote(tok_hbm.at[at], tok.at[at], tx_send.at[0], tx_recv.at[n], partner)

    def tok_y(n):
        at = tok.at[part_rows(y, n)]
        return remote(at, at, ty_send.at[0], ty_recv.at[n], device(z, x, 1 - y, c))

    def start_tokens(n):
        @pl.when(swapped)
        def _():
            tok_x(n).start()

    def forward(k, *which):
        for i in which:
            fx, fy = flips[i + 1]
            firsts[k, i].wait_recv()
            start_near(k, 2 * (1 - x if fx else x) + (1 - y if fy else y))

    def own_mate(k):
        if k != OFF:
            send_mate(k, z).start()
        else:

            @pl.when(middle)
            def _():
                send_mate(k, z).start()

    def start_end_near(k):
        @pl.when(end)
        def _():
            start_near(k, place)

    for k in (OFF, 0):
        forward(k, 0, 1, 2)
        own_mate(k)
    start_units(1)
    start_tokens(0)
    start_end_near(1)
    forward(1, 0, 1, 2)
    own_mate(1)
    start_units(2)
    start_end_near(2)
    forward(2, 0, 1, 2)
    own_mate(2)
    start_units(*range(3, DIRECT))
    start_tokens(1)

    whole_sides.wait_recv()

    def spread(piece, step, n, size):
        wide = jnp.concatenate(piece + [jnp.zeros((8, size - 128 * len(piece)), f32)], axis=1)
        return pltpu.roll(wide, step * n, 1) if n else wide

    for p in range(4):
        total = jnp.zeros((8, 8 * 128), f32)
        for n in range(8):
            total = total + spread([sides[n, p]], shard, n, 8 * 128)
        gains[p] = total[:, 0 : 8 * shard]

    def ends_of(lens):
        ends, last = [], jnp.zeros((1, 1), f32)
        for t in range(lens_ref.shape[1]):
            last = last + lens[3:4, t : t + 1]
            ends.append(last)
        return ends

    own_ends = ends_of(sides[4 * c + 2 * y + c, z])

    def start_at(query, ends):
        start = jnp.zeros_like(query)
        for e in ends:
            start = jnp.where(query >= e, e, start)
        return start

    def tables(cosine, sine, ends):
        query = lax.broadcasted_iota(jnp.int32, (count, 1), 0).astype(f32)
        pos = query - start_at(query, ends)
        lane = lax.broadcasted_iota(jnp.int32, (1, HEAD_DIM), 1)
        mid = HEAD_DIM // 2
        freqs = jnp.exp(-((lane % mid).astype(f32) * 2.0 / HEAD_DIM) * math.log(1000000.0))
        angle = pos * freqs
        cosine[...] = jnp.cos(angle)
        sine[...] = jnp.where(lane < mid, -1.0, 1.0) * jnp.sin(angle)

    back = -(-(MOST - 1) // BLOCK)

    def reach(at):
        first = max(0, at - back)
        return first, (at + 1 - first) * BLOCK

    def masks():
        for at in range(count // BLOCK):
            first, wide = reach(at)
            query = (at * BLOCK + lax.broadcasted_iota(jnp.int32, (BLOCK, 1), 0)).astype(f32)
            key = (first * BLOCK + lax.broadcasted_iota(jnp.int32, (BLOCK, wide), 1)).astype(f32)
            start = start_at(query, own_ends)
            low = jnp.maximum(query - (WINDOW - 1), start)
            allowed = jnp.logical_and(
                key <= query,
                jnp.logical_or(key >= low, jnp.logical_and(key >= start, key < start + SINKS)),
            )
            mask[at, :, 0:wide] = jnp.where(allowed, 0.0, -1e30)

    def normalise(tok, normed, first, many):
        @pl.loop(0, many // 32)
        def _(i):
            at = pl.ds(pl.multiple_of(first + i * 32, 32), 32)
            square = jnp.zeros((32, 8 * shard), f32)
            for p in range(4):
                wide = tok[at, p * 8 * shard : (p + 1) * 8 * shard].astype(f32)
                square = square + wide * wide
            mean = jnp.sum(square, axis=-1, keepdims=True) * (1.0 / depth)
            scale = lax.rsqrt(mean + 1e-06)
            for p in range(4):
                part = slice(p * 8 * shard, (p + 1) * 8 * shard)
                wide = tok[at, part].astype(f32)
                normed[at, part] = (wide * scale * gains[p, 0:1, :]).astype(bf16)

    def product(k, p):
        block = fulls[k][p].reshape(8 * shard, fulls[k].shape[-1])
        part = pl.ds(pl.multiple_of(p * 8 * shard, 128), 8 * shard)
        return jnp.dot(normed[:, part], block, preferred_element_type=f32)

    def whole(lhs, full):
        block = full[...].reshape(depth, full.shape[-1])
        return jnp.dot(lhs, block, preferred_element_type=f32)

    def some_rows(at_y):
        return pl.ds(pl.multiple_of(at_y * (count // 2), count // 2), count // 2)

    def take_mate(k, p):
        ref = fulls[k].at[p, :, 1 - c]
        remote(ref, ref, mate_send.at[k], mate_recv.at[k, p], mate).wait_recv()

    def add(k, n):
        p = orders[n]
        take_mate(k, p)
        if n == 0:
            accs[k][...] = product(k, p)
        else:
            accs[k][...] += product(k, p)

    def bias_line(group):
        total = jnp.zeros((8, width), f32)
        for n in range(8):
            both = sides[n, group]
            total = total + spread(
                [pltpu.roll(both, 7, 0), pltpu.roll(both, 6, 0)], width // 8, n, width
            )
        return total[0:1, :]

    def finish(k, sums, rows=slice(None)):
        lo, hi = CHUNKS[k]
        joined = sums + bias[:, lo:hi]
        for h in range(lo // HEAD_DIM, hi // HEAD_DIM):
            v = joined[:, h * HEAD_DIM - lo : (h + 1) * HEAD_DIM - lo]
            qkv[h, rows, :] = (
                rotated(v, cosine[rows, :], sine[rows, :]) if h <= GROUP else v.astype(bf16)
            )

    def chunk_end(k):
        if k == OFF:

            @pl.when(end)
            def _():
                for h in range(2):
                    give_head(kv2, h).wait_recv()

            return

        @pl.when(end)
        def _():
            add(k, 0)

        @pl.when(end)
        def _():
            add(k, 1)
            add(k, 2)

        ends_get(3, k)

        @pl.when(end)
        def _():
            p = orders[3]
            take_mate(k, p)
            finish(k, accs[k][...] + product(k, p))

    def chunk_middle(k, late):
        @pl.when(middle)
        def _():
            if k != OFF and not late:
                for n in range(4):
                    take_mate(k, orders[n])
            rows = some_rows(1 - y if late else y)
            finish(k, whole(normed[rows, :], fulls[k]), rows)

    def out_at(k, part):
        lo, hi = CHUNKS[k]
        where = (pl.ds(part * (count // 2), count // 2), pl.ds(lo, hi - lo))
        return ctx.at[where], out_hbm.at[where]

    def out_remote(k, part):
        source, to = out_at(k, part)
        return remote(source, to, out_send.at[0], out_recv.at[0], partner)

    def out_local(k, part):
        source, to = out_at(k, part)
        return pltpu.make_async_copy(source, to, out_sem)

    def attend(k):
        lo, hi = CHUNKS[k]
        heads = range(lo // HEAD_DIM, hi // HEAD_DIM)
        many = len(heads)
        for at in range(count // BLOCK):
            first, wide = reach(at)
            here = slice(at * BLOCK, (at + 1) * BLOCK)
            seen = slice(first * BLOCK, (at + 1) * BLOCK)
            query = jnp.concatenate([qkv[h, here, :] for h in heads], axis=0)
            scores = lax.dot_general(
                query, qkv[GROUP, seen, :], (((1,), (1,)), ((), ())), preferred_element_type=f32
            )
            scores = scores.reshape(many, BLOCK, wide) + mask[at, :, 0:wide][None]
            peak = jnp.max(scores, axis=-1, keepdims=True)
            expo = jnp.exp2((scores - peak) * (math.log2(math.e) / math.sqrt(HEAD_DIM)))
            weights = (expo * (1.0 / jnp.sum(expo, axis=-1, keepdims=True))).astype(bf16)
            mixed = jnp.dot(
                weights.reshape(many * BLOCK, wide), qkv[GROUP + 1, seen, :],
                preferred_element_type=f32,
            ).astype(bf16)
            for n, h in enumerate(heads):
                ctx[here, h * HEAD_DIM : (h + 1) * HEAD_DIM] = mixed[n * BLOCK : (n + 1) * BLOCK]
            if at % 2:
                @pl.when(swapped)
                def _():
                    out_remote(k, at // 2).start()

                @pl.when(jnp.logical_not(swapped))
                def _():
                    out_local(k, at // 2).start()

                if k == 1 and at == 1:
                    pass_head(0)
                if k == 2 and at == 1:
                    @pl.when(jnp.logical_and(middle, jnp.logical_not(swapped)))
                    def _():
                        for h in range(2):
                            give_head(kv2, h).start()

    def receive(who, d, k):
        for way in range(2):
            p = z + d * (1 - 2 * way)

            @pl.when(z == ((1, 2, 0), (2, 1, 3))[way][who])
            def _():
                ref = half(k, p)
                if d == 1:
                    remote(ref, ref, near_send.at[k], near_recv.at[way, k], mate).wait_recv()
                else:
                    remote(
                        ref, ref, far_send.at[k], far_recv.at[k, d - 2], mate
                    ).wait_recv()
                if who == 1 or (who == 0 and k != OFF):
                    far(way, k, d + 1).start()
                send_mate(k, p).start()

    def inner(d, k):
        receive(0, d, k)

    def outer(d, k):
        receive(1, d, k)

    def ends_get(d, k):
        receive(2, d, k)

    def take_unit(n):
        @pl.when(middle)
        def _():
            unit_z(n).wait_recv()
            if n < UNITS - DIRECT:
                unit_y(n).start()
            unit_mate(n).start()

    def take_side(n):
        @pl.when(middle)
        def _():
            at = tok2.at[row_unit(UNITS - 1 - n)]
            remote(at, at, tv_send.at[0], tv_recv.at[n], mate).wait_recv()
            unit_mate(UNITS - 1 - n).start()

    def unit_norm(n):
        @pl.when(middle)
        def _():
            at = c + (1 - y) * 2 * n + y * 2 * (UNITS - 1 - n) + 1 - 2 * c
            size = count // 2 // UNITS
            ref = tok2.at[pl.ds(pl.multiple_of(at * size, size), size)]
            remote(ref, ref, tm_send.at[0], tm_recv.at[n], mate).wait_recv()
            first = ((1 - y) * n + y * (UNITS - 1 - n)) * 2 * size
            normalise(tok2, normed2, first, 2 * size)

    both_mid = jnp.logical_and(middle, swapped)
    kx_planes = (0, 2, 3)

    def other_x(i):
        p = orders[kx_planes[i]]
        return remote(fulls[OFF].at[p], fullo.at[p], kx_send.at[0], kx_recv.at[i], partner)

    def other_z(n):
        ref = fullo.at[orders[n]]
        return remote(ref, ref, kz_send.at[0], kz_recv.at[0], device(3 - z, x, y, c))

    def give_other(n):
        @pl.when(middle)
        def _():
            take_mate(OFF, orders[n])
        if n in kx_planes:
            @pl.when(both_mid)
            def _():
                other_x(kx_planes.index(n)).start()

    def take_other(i):
        @pl.when(both_mid)
        def _():
            other_x(i).wait_recv()
            if i == 0:
                other_z(0).start()

    def last_others():
        @pl.when(both_mid)
        def _():
            other_z(1).wait_recv()

    def give_head(source, h):
        return remote(
            source.at[h], qkv.at[CHUNKS[OFF][0] // HEAD_DIM + h], kv_send.at[h], kv_recv.at[h],
            device(pair, x, y, c),
        )

    def head_over(h):
        return remote(kv2.at[h], kv3.at[h], kp_send.at[h], kp_recv.at[h], partner)

    def pass_head(h):
        @pl.when(both_mid)
        def _():
            head_over(h).wait_recv()
            give_head(kv3, h).start()

    def serve_end():
        def sums(full):
            acco[...] = whole(normed2[...], full)

        @pl.when(swapped)
        def _():
            sums(fullo)

        @pl.when(jnp.logical_not(swapped))
        def _():
            sums(fulls[OFF])

        lo, hi = CHUNKS[OFF]
        joined = acco[...] + bias_line(2 * y + c)[:, lo:hi]
        for h in range(2):
            v = joined[:, h * HEAD_DIM : (h + 1) * HEAD_DIM]
            kv2[h] = rotated(v, cosine2[...], sine2[...])

        @pl.when(swapped)
        def _():
            for h in range(2):
                head_over(h).start()


    def pass_tokens(n):
        @pl.when(swapped)
        def _():
            tok_x(n).wait_recv()
            tok_y(n).start()
            normalise(tok, normed, y * (count // 2) + n * rows, rows)

    def tokens_y(n):
        @pl.when(swapped)
        def _():
            at = tok.at[part_rows(1 - y, n)]
            remote(at, at, ty_send.at[0], ty_recv.at[n], mate).wait_recv()
            normalise(tok, normed, (1 - y) * (count // 2) + n * rows, rows)

    bias = bias_line(group)
    take_unit(0)
    inner(1, OFF)
    give_other(0)
    start_tokens(2)
    start_tokens(3)
    inner(1, 0)
    pass_tokens(0)
    outer(1, OFF)
    outer(1, 0)
    take_unit(1)
    unit_norm(0)
    inner(1, 1)
    pass_tokens(1)
    inner(1, 2)
    give_other(2)

    @pl.when(jnp.logical_not(swapped))
    def _():
        tok_copy.wait()
        normalise(tok, normed, 0, count)

    inner(2, OFF)
    outer(1, 1)
    give_other(1)
    give_other(3)
    take_side(0)
    take_unit(2)
    unit_norm(1)
    tables(cosine, sine, own_ends)
    masks()
    pass_tokens(2)
    for k in range(OFF):
        ends_get(1, k)
    inner(2, 0)
    unit_norm(UNITS - 1)
    tokens_y(0)

    @pl.when(middle)
    def _():
        tables(cosine2, sine2, ends_of(sides[me, pair]))

    outer(1, 2)
    take_other(0)
    pass_tokens(3)
    ends_get(2, 0)
    unit_norm(2)
    take_side(1)
    inner(2, 1)
    unit_norm(UNITS - 2)
    tokens_y(1)
    take_unit(3)
    take_side(2)
    chunk_middle(0, False)
    unit_norm(3)
    chunk_middle(OFF, False)
    ends_get(2, 1)
    tokens_y(2)
    for n in range(4, DIRECT):
        take_unit(n)
    chunk_middle(1, False)
    unit_norm(UNITS - 3)
    take_other(1)
    ends_get(2, 2)
    unit_norm(4)
    inner(2, 2)
    take_other(2)
    last_others()
    pl.when(middle)(serve_end)
    tokens_y(3)
    chunk_middle(0, True)
    chunk_end(0)
    chunk_middle(1, True)
    for k in range(1, number):
        if k == 2:
            pass_head(1)
            chunk_middle(k, False)
        chunk_end(k)
        if k > 1:
            chunk_middle(k, True)
        attend(k)

    whole_line.wait_send()
    whole_sides.wait_send()
    for k in range(number):
        remote(wbs[k], wbs[k], first_send.at[k], first_recv.at[k, 0], mate).wait_send()
    for k in range(number):
        def mates():
            ref = fulls[k].at[:, :, c]
            remote(ref, ref, mate_send.at[k], mate_recv.at[k, 0], mate).wait_send()

        if k != OFF:
            mates()
        else:
            pl.when(middle)(mates)

        def gone(nears, fars):
            ref = fulls[k].at[pl.ds(0, nears), :, c]
            remote(ref, ref, near_send.at[k], near_recv.at[0, k], mate).wait_send()
            if fars:
                ref = fulls[k].at[pl.ds(0, fars), :, c]
                remote(ref, ref, far_send.at[k], far_recv.at[k, 0], mate).wait_send()

        @pl.when(middle)
        def _():
            gone(*((1, 1) if k == OFF else (2, 3)))

        @pl.when(end)
        def _():
            gone(1, 0)

    @pl.when(end)
    def _():
        sent(DIRECT * unit_rows, tz_send, tz_recv)

    @pl.when(middle)
    def _():
        sent((UNITS - DIRECT) * unit_rows, tv_send, tv_recv)
        sent(UNITS * unit_rows, tm_send, tm_recv)
        for h in range(2):
            give_head(kv2, h).wait_send()

    @pl.when(both_mid)
    def _():
        ref = fullo.at[pl.ds(0, len(kx_planes))]
        remote(ref, ref, kx_send.at[0], kx_recv.at[0], mate).wait_send()
        for h in range(2):
            head_over(h).wait_send()
        other_z(0).wait_send()

    @pl.when(swapped)
    def _():
        sent(count // 2, tx_send, tx_recv)
        sent(count // 2, ty_send, ty_recv)
        out = remote(ctx, out_hbm, out_send.at[0], out_recv.at[0], partner)
        out.wait_recv()
        out.wait_send()

    @pl.when(jnp.logical_not(swapped))
    def _():
        pltpu.make_async_copy(ctx, out_hbm, out_sem).wait()


def serve(tokens, norm_gain, qkv_weight, qkv_bias, lens):
    count, depth = tokens.shape
    shard, columns = qkv_weight.shape
    width = columns // 4
    sizes = [hi - lo for lo, hi in CHUNKS]
    number, blocks = len(sizes), count // BLOCK
    hbm = pl.BlockSpec(memory_space=pltpu.HBM)
    dma, vmem = pltpu.SemaphoreType.DMA, pltpu.VMEM
    f32, bf16 = jnp.float32, jnp.bfloat16
    two = lambda *shape: [dma(shape), dma(shape)]
    return pl.pallas_call(
        serve_kernel,
        out_shape=jax.ShapeDtypeStruct((count, GROUP * HEAD_DIM), bf16),
        in_specs=[hbm] * 5,
        out_specs=hbm,
        scratch_shapes=[
            vmem(lens.shape, jnp.int32),
            vmem((1, shard), f32),
            vmem((1, columns // 32), f32),
            dma((3,)),
            vmem((4, shard, width), f32),
            *[vmem((3, shard, size), bf16) for size in sizes],
            *[vmem((4, 4, 2, shard, size), bf16) for size in sizes],
            vmem((4, 4, 2, shard, sizes[OFF]), bf16),
            vmem((count, depth), bf16),
            vmem((count, depth), bf16),
            vmem((count, depth), bf16),
            vmem((count, depth), bf16),
            vmem((count, sizes[OFF]), f32),
            *[vmem((count, size), f32) for size in sizes],
            vmem((GROUP + 2, count, HEAD_DIM), bf16),
            vmem((2, count, HEAD_DIM), bf16),
            vmem((2, count, HEAD_DIM), bf16),
            *[vmem((count, HEAD_DIM), f32)] * 4,
            vmem((blocks, BLOCK, 3 * BLOCK), f32),
            vmem((4, 8, 8 * shard), f32),
            vmem((count, GROUP * HEAD_DIM), bf16),
            vmem((8, 128), f32),
            vmem((4, 8, 128), f32),
            vmem((8, 4, 8, 128), f32),
            dma, dma((4,)),
            *two(1), *two(1), dma((number,)), dma((number, 3)),
            dma((number,)), dma((2, number)), dma((number,)), dma((number, 2)),
            dma((number,)), dma((number, 4)),
            *[dma((many,)) for n in (PARTS, PARTS, DIRECT, UNITS - DIRECT, UNITS, 3) for many in (1, n)],
            *two(1), *two(2), *two(2), *two(1), dma,
        ],
        compiler_params=pltpu.CompilerParams(
            collective_id=0, has_side_effects=True, vmem_limit_bytes=60 << 20
        ),
        name="serve",
    )(lens, norm_gain.reshape(1, shard), qkv_bias.reshape(1, -1), qkv_weight, tokens)


def turn_plain(joined, lens):
    count = joined.shape[0]
    half = HEAD_DIM // 2
    pos = jnp.arange(count, dtype=jnp.int32) - starts(lens, count)
    freqs = jnp.exp(-(jnp.arange(half, dtype=jnp.float32) * 2.0 / HEAD_DIM) * math.log(1000000.0))
    angle = pos.astype(jnp.float32)[:, None] * freqs[None, :]
    cosine = jnp.tile(jnp.cos(angle), (1, 2))[:, None, :]
    sine = jnp.tile(jnp.sin(angle), (1, 2))[:, None, :]
    heads = joined.reshape(count, GROUP + 2, HEAD_DIM)
    spun = jnp.concatenate([-heads[..., half:], heads[..., :half]], axis=-1)
    turned = (heads * cosine + spun * sine)[:, : GROUP + 1]
    both = jnp.concatenate([turned, heads[:, GROUP + 1 :]], axis=1)
    return both.reshape(count, -1).astype(jnp.bfloat16)


def project_plain(tokens, norm_gain, qkv_weight, qkv_bias):
    tp_count = lax.axis_size("tp")
    req_count = lax.axis_size("req")
    tp_place = lax.axis_index("tp")
    gain_full, bias_full = (
        lax.all_gather(norm_gain.astype(jnp.bfloat16), ("req", "tp"), axis=0, tiled=True),
        lax.all_gather(qkv_bias.astype(jnp.bfloat16), ("req", "tp"), axis=0, tiled=True),
    )
    width = bias_full.shape[0] // tp_count
    bias_block = lax.dynamic_slice_in_dim(bias_full, tp_place * width, width).astype(jnp.float32)
    normed = normalize(tokens, gain_full)
    weight_b = qkv_weight.astype(jnp.bfloat16)
    count = tokens.shape[0]
    gathered = lax.all_gather(weight_b, "req", axis=0, tiled=True)
    regrouped = lax.all_to_all(gathered, "tp", split_axis=1, concat_axis=0, tiled=True)
    shard_rows = weight_b.shape[0]
    reordered = (
        normed.reshape(count, req_count, tp_count, shard_rows)
        .transpose(0, 2, 1, 3)
        .reshape(count, -1)
    )
    joined = jnp.dot(reordered, regrouped, preferred_element_type=jnp.float32)
    return joined + bias_block[None, :]


def shards(small, tokens, norm_gain, qkv_weight, qkv_bias, lengths):
    if small:
        return serve(tokens, norm_gain, qkv_weight, qkv_bias, lengths)
    qkv = turn_plain(project_plain(tokens, norm_gain, qkv_weight, qkv_bias), lengths[0])
    return attend_turned(qkv, lengths)


def solution(mesh):
    placed = (
        P("req", None),
        P(("req", "tp")),
        P(("req", "tp"), None),
        P(("req", "tp")),
        P("req", None),
    )
    small = mesh.shape["req"] == 8 and mesh.shape["tp"] == 4
    return jax.shard_map(
        functools.partial(shards, small),
        mesh=mesh, in_specs=placed, out_specs=P("req", "tp"), check_vma=False,
    )
```
